256 devices in a mesh: dp: 32 (over z, y_hi, core), owner: 8 (over y_lo, x).
Axes of the slice: x: 4, y: 4 (y_hi: 2, y_lo: 2; y = y_hi * 2 + y_lo), z: 8, core: 2. Of those that a mesh axis runs over, the one named last changes fastest.
Arguments:
- hidden: bfloat16 [4096, 4096], P('dp'), may hold values from -6 to 6
- norm_gain: float32 [4096], replicated, may hold values from 0.3 to 3
- cotangent: bfloat16 [4096, 6144], P('dp'), may hold values from -30 to 30
Outputs:
- update: bfloat16 [6144, 4096], P('dp', 'owner')
The draws below stay inside these ranges and needn't reach their ends.
All inputs are finite; a program needn't handle non-finite values. Where the reference program divides by a largest or mean magnitude, that divisor is 1e-20 or more.
Results may differ from the reference program's by a relative error of at most 0.014.
Values may be sent and summed in bfloat16 or wider, within the bound.
No kernel may reach another device: no remote copies, remote signals or barrier semaphores. Data moves between devices by JAX's collectives and lax.ppermute only.
A program may use at most 128 MiB of HBM per device.

```python
import math
import jax
import jax.numpy as jnp
from jax import lax

D = 4096
TILE = 1024
TOK_DEV = 128
TOKENS = 4096
DOUT = 6144
NBLK = 10
N_DP = 32


latent_rank = 16


def shared_latent(key):
    return jax.random.normal(jax.random.fold_in(key, 5), (TOKENS, latent_rank), jnp.float32)


def draw_hidden(key, part):
    latent = shared_latent(key)
    keys = jax.random.split(jax.random.fold_in(key, 23), 2)
    basis = jax.random.normal(keys[0], (latent_rank, D), jnp.float32) / math.sqrt(latent_rank)
    noise = jax.random.normal(keys[1], (TOKENS, D), jnp.float32)
    share = 0.5
    mixed = jnp.dot(latent, basis)
    values = math.sqrt(1.0 - share * share) * noise + share * mixed
    return jnp.clip(values, -6.0, 6.0).astype(jnp.bfloat16)


def draw_cotangent(key, part):
    latent = shared_latent(key)
    keys = jax.random.split(jax.random.fold_in(key, 17), 8)
    columns = 3.0 ** (jnp.arange(DOUT, dtype=jnp.float32) / DOUT)
    columns = columns * jax.random.uniform(keys[1], (DOUT,), jnp.float32, 0.5, 1.5)
    heavy = jax.random.randint(keys[4], (), 0, N_DP)
    group_index = jnp.arange(TOKENS, dtype=jnp.int32) // TOK_DEV
    before = (heavy + N_DP - 1) % N_DP
    chosen = jnp.logical_or(group_index == heavy, group_index == before)
    group_scale = jnp.where(chosen, 5.0, 1.0).astype(jnp.float32)[:, None]
    common_basis = jax.random.normal(keys[5], (latent_rank, DOUT), jnp.float32) / math.sqrt(latent_rank)
    own_basis = jax.random.normal(keys[6], (N_DP, latent_rank, DOUT), jnp.float32) / math.sqrt(latent_rank)
    own_latent = jax.random.normal(keys[7], (N_DP, TOK_DEV, latent_rank), jnp.float32)
    own = jnp.einsum('gtr,grc->gtc', own_latent, own_basis).reshape(TOKENS, DOUT)
    common = jnp.dot(latent, common_basis)
    noise = jax.random.normal(keys[0], (TOKENS, DOUT), jnp.float32)
    noise_share = 0.6
    common_share = 0.4
    own_share = math.sqrt(1.0 - noise_share * noise_share - common_share * common_share)
    values = noise_share * noise + common_share * common + own_share * own
    values = values * group_scale
    return jnp.clip(values * columns, -30.0, 30.0).astype(jnp.bfloat16)


def setup_inputs(seed: int = 0) -> dict:
    arg_keys = jax.random.split(jax.random.key(seed), 4)
    hidden = draw_hidden(jax.random.fold_in(arg_keys[3], 71), 0)
    norm_gain = jnp.clip(jnp.exp(jax.random.uniform(arg_keys[1], (D,), jnp.float32, math.log(0.3), math.log(3.0))), 0.3, 3.0)
    cotangent = draw_cotangent(jax.random.fold_in(arg_keys[3], 71), 0)
    return {"hidden": hidden, "norm_gain": norm_gain, "cotangent": cotangent}


DAMPING = 0.1

def rounded(value):
    return lax.optimization_barrier(value.astype(jnp.bfloat16)).astype(jnp.float32)

def reference(hidden, norm_gain, cotangent):
    highest = lax.Precision.HIGHEST
    states = hidden.astype(jnp.float32)
    normed = (states * lax.rsqrt(lax.optimization_barrier(jnp.mean(states * states, axis=1, keepdims=True)) + 1e-05) * norm_gain).astype(jnp.bfloat16)
    source = jnp.concatenate([normed, cotangent], axis=1)
    identity = jnp.eye(TILE, dtype=jnp.float32)
    results = []
    for block in range(NBLK):
        piece = source[:, block * TILE:(block + 1) * TILE].astype(jnp.float32)
        factor = jnp.dot(piece.T, piece, precision=highest)
        matrix = factor / TOKENS + DAMPING * identity
        scale = 1.0 / jnp.max(lax.optimization_barrier(jnp.sum(jnp.abs(matrix), axis=1)))
        first = 2.0 * scale * identity - scale * scale * matrix
        first_low = rounded(first)
        product = rounded(jnp.dot(first_low, rounded(matrix), precision=highest))
        inverse = rounded(2.0 * first - jnp.dot(product, first_low, precision=highest))
        results.append(jnp.dot(piece, inverse, precision=highest).astype(jnp.bfloat16))
    inputs_side = D // TILE
    pre_in = jnp.concatenate(results[:inputs_side], axis=1).astype(jnp.float32).reshape(N_DP, TOK_DEV, D)
    pre_out = jnp.concatenate(results[inputs_side:], axis=1).astype(jnp.float32).reshape(N_DP, TOK_DEV, DOUT)

    def accumulate(total, pair):
        left, right = pair
        return (total + rounded(jnp.dot(right.T, left, precision=highest)), None)
    summed, _ = lax.scan(accumulate, jnp.zeros((DOUT, D), jnp.float32), (pre_in, pre_out))
    squares = jnp.sum(summed * summed)
    return (summed * lax.rsqrt(squares / (D * DOUT) + 1e-06)).astype(jnp.bfloat16)
```

```python
import functools

import jax
import jax.numpy as jnp
from jax import lax
from jax.sharding import Mesh
from jax.sharding import PartitionSpec as P

TILE = 1024
PIECE = 256
Z, YH, CORE, YL, X = "dp_0", "dp_1", "dp_2", "owner_0", "owner_1"
DP = (Z, YH, CORE)
OWNER = (YL, X)
DAMPING = 0.1
bf16, f32 = jnp.bfloat16, jnp.float32

SWAP2 = [(0, 1), (1, 0)]
SWAP_X = [(0, 1), (1, 0), (2, 3), (3, 2)]


def cols(a, start, width):
    return lax.dynamic_slice_in_dim(a, start, width, 1)


def tdot(a, b):
    return lax.dot_general(a, b, (((0,), (0,)), ((), ())), preferred_element_type=f32)


def mdot(a, b):
    return jnp.dot(a, b, preferred_element_type=f32)


def ring_perm(step, delta=0, skip=False):
    pairs = [(i, (i + step) % 8) for i in range(8)]
    if skip:
        pairs = [(i, j) for i, j in pairs if (i + delta) % 4 != 2]
    return pairs


def ring_reduce(chunk, skip):
    far = chunk(4)
    half = far.shape[0] // 2
    low = lax.ppermute(far[:half].astype(bf16), Z, ring_perm(-1, -4, skip))
    high = lax.ppermute(far[half:].astype(bf16), Z, ring_perm(1, 4, skip))
    nothing = jnp.zeros_like(low)
    low = jnp.concatenate([low, nothing], 0)
    high = jnp.concatenate([nothing, high], 0)
    for d in (3, 2, 1):
        send_low = (chunk(-d) + low.astype(f32)).astype(bf16)
        send_high = (chunk(d) + high.astype(f32)).astype(bf16)
        low = lax.ppermute(send_low, Z, ring_perm(-1, -d, skip))
        high = lax.ppermute(send_high, Z, ring_perm(1, d, skip))
    return chunk(0) + low.astype(f32) + high.astype(f32)


def pair_sum(a, axis):
    a = a.astype(bf16)
    return a.astype(f32) + lax.ppermute(a, axis, SWAP2).astype(f32)


def in_order(flag, own, other):
    first = jnp.where(flag == 0, own, other)
    second = jnp.where(flag == 0, other, own)
    return first, second


def by_core(core, own):
    other = lax.ppermute(own, CORE, SWAP2)
    first, second = in_order(core, own, other)
    both = jnp.stack([first, second], 1)
    return both.reshape(-1, own.shape[-1])


def factor(sums, tokens):
    eye = jnp.eye(TILE, dtype=f32)
    matrix = sums.astype(f32) / tokens + DAMPING * eye
    scale = 1.0 / jnp.max(jnp.sum(jnp.abs(matrix), axis=1))
    first = 2.0 * scale * eye - (scale * scale) * matrix
    return matrix.astype(bf16), first


def all_sum(value, axis, n):
    total = value
    for s in range(1, n):
        total = total + lax.ppermute(value, axis, [(i, (i + s) % n) for i in range(n)])
    return total


def shards(hidden, norm_gain, cotangent):
    z, yh, core = lax.axis_index(Z), lax.axis_index(YH), lax.axis_index(CORE)
    yl, x = lax.axis_index(YL), lax.axis_index(X)
    k, h = 2 * yl + x // 2, x % 2
    piece, other_piece = 2 * h + core, 2 * h + 1 - core
    width, out_width = hidden.shape[1], cotangent.shape[1]
    out_blocks = out_width // TILE
    tokens = hidden.shape[0] * lax.axis_size(DP)

    def strided(p):
        return [cols(cotangent, j * TILE + p * PIECE, PIECE) for j in range(out_blocks)]

    left, left_other, right = strided(piece), strided(other_piece), strided(k)
    right = jnp.concatenate(right, 1)
    left = jnp.concatenate(left, 1)
    cot_recv = lax.ppermute(jnp.concatenate(left_other + [right], 1), CORE, SWAP2)
    left = jnp.concatenate([left, cot_recv[:, : left.shape[1]]], 0)
    right = jnp.concatenate([right, cot_recv[:, left.shape[1] :]], 0)

    states = hidden.astype(f32)
    rms = lax.rsqrt(jnp.mean(states * states, axis=1, keepdims=True) + 1e-05)
    gain = lax.dynamic_slice_in_dim(norm_gain, k * TILE, TILE)
    normed = (cols(hidden, k * TILE, TILE).astype(f32) * rms * gain).astype(bf16)
    normed = jnp.concatenate([normed, lax.ppermute(normed, CORE, SWAP2)], 0)

    def block_of(plane):
        m = plane % 4
        return 3 * (plane // 4) + m - m // 2

    def left_of(delta):
        plane = (z + delta + 8) % 8
        return cols(left, block_of(plane) * PIECE, PIECE)

    in_part = tdot(cols(normed, piece * PIECE, PIECE), normed)

    def factor_chunk(delta):
        plane = (z + delta + 8) % 8
        out = tdot(left_of(delta), cols(right, block_of(plane) * PIECE, PIECE))
        return jnp.concatenate([out, cols(in_part, plane * 128, 128)], 1)

    sums = pair_sum(ring_reduce(factor_chunk, False), YH).astype(bf16)
    out_tile, in_tile = sums[:, :PIECE], sums[:, PIECE:]

    other = lax.ppermute(out_tile, YL, SWAP2)
    mine = jnp.stack(in_order(yl, out_tile, other))
    out_half = jnp.zeros((2, PIECE, TILE), bf16)
    for s in range(4):
        got = mine if s == 0 else lax.ppermute(mine, X, [(i, (i + s) % 4) for i in range(4)])
        source = (x - s + 4) % 4
        for b in range(2):
            at = (source % 2, 0, (2 * b + source // 2) * PIECE)
            out_half = lax.dynamic_update_slice(out_half, got[b][None], at)
    out_sums = by_core(core, out_half)

    other = lax.ppermute(in_tile, X, SWAP_X)
    shard = jnp.stack(in_order(h, in_tile, other))
    in_half = jnp.zeros((2, PIECE, TILE), bf16)

    def put(buffer, value, plane, first=0):
        return lax.dynamic_update_slice(buffer, value, (first, 0, (plane + 8) % 8 * 128))

    in_half = put(in_half, shard, z)
    up = down = shard
    for d in (1, 2, 3):
        up = lax.ppermute(up, Z, ring_perm(-1))
        down = lax.ppermute(down, Z, ring_perm(1))
        in_half = put(put(in_half, up, z + d), down, z - d)
    up = lax.ppermute(up[:1], Z, ring_perm(-1))
    down = lax.ppermute(down[1:], Z, ring_perm(1))
    in_half = put(put(in_half, up, z + 4), down, z - 4, 1)
    in_sums = by_core(core, in_half)

    matrix, first = factor(in_sums, tokens)
    first_low = first.astype(bf16)
    product = mdot(first_low, matrix).astype(bf16)
    in_inverse = (2.0 * first - mdot(product, first_low)).astype(bf16)

    m = z % 4
    row = 2 * yh + core
    slice_rows = out_width // lax.axis_size(DP)
    base = TILE * (m - m // 2)
    own_at = jnp.where(m == 2, TILE, slice_rows * (4 * m + row) - base)
    near = jnp.where(m == 3, 2, m + 1)
    near_at = jnp.where(m == 2, TILE, slice_rows * (4 * near + row) - base)
    matrix, first = factor(out_sums, tokens)
    first_low = first.astype(bf16)
    padded = jnp.pad(first, ((slice_rows, slice_rows), (0, 0)))

    def rows_at(at):
        at = jnp.clip(at, -slice_rows, TILE) + slice_rows
        return lax.dynamic_slice_in_dim(padded, at, slice_rows, 0)

    rows = jnp.concatenate([rows_at(own_at), rows_at(near_at)], 0)
    product = mdot(rows.astype(bf16), matrix).astype(bf16)
    out_inverse = (2.0 * rows - mdot(product, first_low)).astype(bf16)

    def cross_chunk(delta):
        return tdot(left_of(delta), normed)

    cross = pair_sum(ring_reduce(cross_chunk, True), YH).astype(bf16)
    half_done = mdot(cross, in_inverse).astype(bf16)
    keep = cols(half_done, h * 512, 512)
    give = cols(half_done, (1 - h) * 512, 512)
    other = lax.ppermute(give, X, SWAP_X)
    half_done = by_core(core, jnp.stack(in_order(h, keep, other)))
    result = mdot(out_inverse, half_done)

    squares = jnp.sum(result * result).reshape(1, 1)
    squares = all_sum(squares, Z, 8)
    squares = all_sum(squares, (YH, CORE, YL), 8)
    squares = all_sum(squares, X, 4)
    near_part = result[slice_rows:].astype(bf16)
    up = lax.ppermute(near_part, Z, [(0, 1), (1, 2), (4, 5), (5, 6)])
    down = lax.ppermute(near_part, Z, [(3, 2), (7, 6)])
    summed = result[:slice_rows] + up.astype(f32) + down.astype(f32)
    return (summed * lax.rsqrt(squares / (width * out_width) + 1e-06)).astype(bf16)


def solution(mesh):
    split = Mesh(mesh.devices.reshape(8, 2, 2, 2, 4), DP + OWNER)
    return jax.shard_map(
        shards,
        mesh=split,
        in_specs=(P(DP, None), P(), P(DP, None)),
        out_specs=P(DP, OWNER),
        check_vma=False,
    )
```

```python
import functools

import jax
import jax.numpy as jnp
from jax import lax
from jax.experimental import pallas as pl
from jax.experimental.pallas import tpu as pltpu
from jax.sharding import Mesh
from jax.sharding import PartitionSpec as P

TILE = 1024
PIECE = 256
HALF = 512
Z, YH, CORE, YL, X = "dp_0", "dp_1", "dp_2", "owner_0", "owner_1"
DP = (Z, YH, CORE)
OWNER = (YL, X)
DAMPING = 0.1
bf16, f32 = jnp.bfloat16, jnp.float32
PARAMS = pltpu.CompilerParams(vmem_limit_bytes=48 * 1024 * 1024)
VMEM = pl.BlockSpec(memory_space=pltpu.VMEM)
SMEM = pl.BlockSpec(memory_space=pltpu.SMEM)

SWAP2 = [(0, 1), (1, 0)]
SWAP_X = [(0, 1), (1, 0), (2, 3), (3, 2)]
SWAP_BOTH = [(4 * a + b, 4 * (1 - a) + (b ^ 1)) for a in range(2) for b in range(4)]


def tdot(a, b):
    return lax.dot_general(a, b, (((0,), (0,)), ((), ())), preferred_element_type=f32)


def mdot(a, b):
    return jnp.dot(a, b, preferred_element_type=f32)


def aligned(start, size):
    return pl.ds(pl.multiple_of(start, size), size)


def pick_kernel(out_blocks, at_ref, cot_ref, left_ref, send_ref):
    piece, other, k = at_ref[0], at_ref[1], at_ref[2]
    width = out_blocks * PIECE
    for j in range(out_blocks):
        here = slice(j * PIECE, (j + 1) * PIECE)
        there = slice(width + j * PIECE, width + (j + 1) * PIECE)
        left_ref[:, here] = cot_ref[:, aligned(j * TILE + piece * PIECE, PIECE)]
        send_ref[:, here] = cot_ref[:, aligned(j * TILE + other * PIECE, PIECE)]
        send_ref[:, there] = cot_ref[:, aligned(j * TILE + k * PIECE, PIECE)]


def factor_kernel(out_blocks, at_ref, left_ref, send_ref, recv_ref, own_ref, got_ref, in_ref, out_ref):
    piece = aligned(at_ref[0] * PIECE, PIECE)
    in_ref[...] = tdot(own_ref[:, piece], own_ref[...]) + tdot(got_ref[:, piece], got_ref[...])
    width = out_blocks * PIECE
    for j in range(out_blocks):
        here = slice(j * PIECE, (j + 1) * PIECE)
        there = slice(width + j * PIECE, width + (j + 1) * PIECE)
        out_ref[j] = tdot(left_ref[:, here], send_ref[:, there]) + tdot(
            recv_ref[:, here], recv_ref[:, there]
        )


def cross_kernel(at_ref, left_ref, recv_ref, own_ref, got_ref, keep_ref, give_ref):
    mine = aligned(at_ref[0] * 128, 128)
    other = aligned((1 - at_ref[0]) * 128, 128)
    own, got = own_ref[...], got_ref[...]
    keep_ref[0] = tdot(left_ref[:, mine], own) + tdot(recv_ref[:, mine], got)
    give_ref[0] = (tdot(left_ref[:, other], own) + tdot(recv_ref[:, other], got)).astype(bf16)


def assemble_in_kernel(at_ref, *refs):
    pieces, out_ref = refs[:-1], refs[-1]
    z = at_ref[0]
    for delta, ref in zip((0, 1, -1, 2, -2, 3, -3), pieces):
        out_ref[:, aligned((z + delta + 8) % 8 * 32, 32), :] = ref[...]
    far = aligned((z + 4) % 8 * 32, 32)
    out_ref[0, far, :] = pieces[7][0]
    out_ref[1, far, :] = pieces[8][0]


def assemble_out_kernel(at_ref, own_ref, other_ref, *refs):
    yl, x = at_ref[0], at_ref[1]
    out_ref = refs[-1]
    for s in range(4):
        source = (x - s + 4) % 4
        for b in range(2):
            column = 2 * jnp.where(b == 0, yl, 1 - yl) + source // 2
            value = (own_ref, other_ref)[b][...] if s == 0 else refs[s - 1][b]
            out_ref[source % 2, :, aligned(column * PIECE, PIECE)] = value


def load_factor(tokens, core, own_ref, other_ref, sums_ref):
    for half in range(2):
        sums_ref[aligned((2 * half + core) * PIECE, PIECE), :] = own_ref[half]
        sums_ref[aligned((2 * half + 1 - core) * PIECE, PIECE), :] = other_ref[half]
    largest = jnp.zeros((), f32)
    for r in range(4):
        rows = matrix_rows(tokens, sums_ref, r * PIECE)
        largest = jnp.maximum(largest, jnp.max(jnp.sum(jnp.abs(rows), axis=1)))
    return 1.0 / largest


def eye_rows(start, count):
    row = lax.broadcasted_iota(jnp.int32, (count, TILE), 0) + start
    return (row == lax.broadcasted_iota(jnp.int32, (count, TILE), 1)).astype(f32)


def matrix_rows(tokens, sums_ref, start):
    return sums_ref[start : start + PIECE, :].astype(f32) / tokens + DAMPING * eye_rows(start, PIECE)


def in_inverse_kernel(tokens, at_ref, own_ref, other_ref, out_ref, sums_ref, first_ref, low_ref):
    scale = load_factor(tokens, at_ref[0], own_ref, other_ref, sums_ref)
    for r in range(4):
        here = slice(r * PIECE, (r + 1) * PIECE)
        rows = matrix_rows(tokens, sums_ref, r * PIECE)
        first = 2.0 * scale * eye_rows(r * PIECE, PIECE) - (scale * scale) * rows
        first_ref[here, :] = first
        low_ref[here, :] = first.astype(bf16)
        sums_ref[here, :] = rows.astype(bf16)
    for r in range(4):
        here = slice(r * PIECE, (r + 1) * PIECE)
        product = mdot(low_ref[here, :], sums_ref[...]).astype(bf16)
        out_ref[here, :] = (2.0 * first_ref[here, :] - mdot(product, low_ref[...])).astype(bf16)


def out_inverse_kernel(tokens, count, at_ref, own_ref, other_ref, out_ref, sums_ref, first_ref, low_ref):
    scale = load_factor(tokens, at_ref[0], own_ref, other_ref, sums_ref)
    first_ref[:count, :] = jnp.zeros((count, TILE), f32)
    first_ref[count + TILE :, :] = jnp.zeros((count, TILE), f32)
    for r in range(4):
        here = slice(r * PIECE, (r + 1) * PIECE)
        rows = matrix_rows(tokens, sums_ref, r * PIECE)
        first = 2.0 * scale * eye_rows(r * PIECE, PIECE) - (scale * scale) * rows
        first_ref[count + r * PIECE : count + (r + 1) * PIECE, :] = first
        low_ref[here, :] = first.astype(bf16)
        sums_ref[here, :] = rows.astype(bf16)
    for part in range(2):
        rows = first_ref[pl.ds(pl.multiple_of(at_ref[1 + part], 64), count), :]
        product = mdot(rows.astype(bf16), sums_ref[...]).astype(bf16)
        out_ref[part * count : (part + 1) * count, :] = (
            2.0 * rows - mdot(product, low_ref[...])
        ).astype(bf16)


def call(kernel, outs, *args, scratch=()):
    outs = [jax.ShapeDtypeStruct(shape, dtype) for shape, dtype in outs]
    result = pl.pallas_call(
        kernel,
        out_shape=outs,
        in_specs=[SMEM] + [VMEM] * (len(args) - 1),
        out_specs=[VMEM] * len(outs),
        scratch_shapes=[pltpu.VMEM(shape, dtype) for shape, dtype in scratch],
        compiler_params=PARAMS,
    )(*args)
    return result[0] if len(outs) == 1 else result


def ring_perm(step, delta=0, skip=False):
    pairs = [(i, (i + step) % 8) for i in range(8)]
    if skip:
        pairs = [(i, j) for i, j in pairs if (i + delta) % 4 != 2]
    return pairs


def ring_reduce(chunk, skip):
    far = chunk(4)
    half = far.shape[0] // 2
    low = lax.ppermute(far[:half].astype(bf16), Z, ring_perm(-1, -4, skip))
    high = lax.ppermute(far[half:].astype(bf16), Z, ring_perm(1, 4, skip))
    nothing = jnp.zeros_like(low)
    low = jnp.concatenate([low, nothing], 0)
    high = jnp.concatenate([nothing, high], 0)
    for d in (3, 2, 1):
        send_low = (chunk(-d) + low.astype(f32)).astype(bf16)
        send_high = (chunk(d) + high.astype(f32)).astype(bf16)
        low = lax.ppermute(send_low, Z, ring_perm(-1, -d, skip))
        high = lax.ppermute(send_high, Z, ring_perm(1, d, skip))
    return chunk(0) + low.astype(f32) + high.astype(f32)


def pair_sum(a, axis):
    a = a.astype(bf16)
    return (a.astype(f32) + lax.ppermute(a, axis, SWAP2).astype(f32)).astype(bf16)


def in_order(flag, own, other):
    first = jnp.where(flag == 0, own, other)
    second = jnp.where(flag == 0, other, own)
    return jnp.stack([first, second])


def all_sum(value, axis):
    n = lax.axis_size(axis)
    shares = lax.all_to_all(jnp.full((n, 128), value, f32), axis, 0, 0, tiled=True)
    return jnp.sum(shares[:, 0])


def shards(hidden, norm_gain, cotangent):
    z, yh, core = lax.axis_index(Z), lax.axis_index(YH), lax.axis_index(CORE)
    yl, x = lax.axis_index(YL), lax.axis_index(X)
    k, h = 2 * yl + x // 2, x % 2
    piece, other_piece = 2 * h + core, 2 * h + 1 - core
    here, width = hidden.shape
    out_width = cotangent.shape[1]
    out_blocks = out_width // TILE
    tokens = here * lax.axis_size(DP)

    def numbers(*values):
        return jnp.stack([jnp.asarray(v, jnp.int32) for v in values])

    left, send = call(
        functools.partial(pick_kernel, out_blocks),
        [((here, out_blocks * PIECE), bf16), ((here, 2 * out_blocks * PIECE), bf16)],
        numbers(piece, other_piece, k),
        cotangent,
    )
    recv = lax.ppermute(send, CORE, SWAP2)

    states = hidden.astype(f32)
    rms = lax.rsqrt(jnp.mean(states * states, axis=1, keepdims=True) + 1e-05)
    gain = lax.dynamic_slice_in_dim(norm_gain, k * TILE, TILE)
    mine = lax.dynamic_slice_in_dim(hidden, k * TILE, TILE, 1)
    normed = (mine.astype(f32) * rms * gain).astype(bf16)
    normed_recv = lax.ppermute(normed, CORE, SWAP2)

    in_part, out_part = call(
        functools.partial(factor_kernel, out_blocks),
        [((PIECE, TILE), f32), ((out_blocks, PIECE, PIECE), f32)],
        numbers(piece),
        left,
        send,
        recv,
        normed,
        normed_recv,
    )
    in_part = in_part.reshape(8, 32, TILE)

    tall = pl.BlockSpec((here, PIECE), lambda j: (0, j))
    whole = pl.BlockSpec((here, TILE), lambda j: (0, 0))
    keep, give = pl.pallas_call(
        cross_kernel,
        grid=(out_blocks,),
        out_shape=[
            jax.ShapeDtypeStruct((out_blocks, 128, TILE), f32),
            jax.ShapeDtypeStruct((out_blocks, 128, TILE), bf16),
        ],
        in_specs=[SMEM, tall, tall, whole, whole],
        out_specs=[pl.BlockSpec((1, 128, TILE), lambda j: (j, 0, 0))] * 2,
        compiler_params=PARAMS,
    )(numbers(yh), left, recv, normed, normed_recv)

    def block_of(delta):
        plane = (z + delta + 8) % 8
        m = plane % 4
        return 3 * (plane // 4) + m - m // 2

    def in_chunk(delta):
        return lax.dynamic_index_in_dim(in_part, (z + delta + 8) % 8, 0, False)

    def out_chunk(delta):
        return lax.dynamic_index_in_dim(out_part, block_of(delta), 0, False)

    def cross_of(delta):
        pairs = [(2 * p + a, 2 * p + 1 - a) for p in range(8) for a in range(2)]
        pairs = [(i, j) for i, j in pairs if (i // 2 + delta) % 4 != 2]
        at = block_of(delta)
        got = lax.ppermute(lax.dynamic_index_in_dim(give, at, 0, False), (Z, YH), pairs)
        return lax.dynamic_index_in_dim(keep, at, 0, False) + got.astype(f32)

    in_tile = pair_sum(ring_reduce(in_chunk, False), YH)
    shard = in_order(h, in_tile, lax.ppermute(in_tile, X, SWAP_X))
    pieces = [shard]
    up = down = shard
    for _ in range(3):
        up = lax.ppermute(up, Z, ring_perm(-1))
        down = lax.ppermute(down, Z, ring_perm(1))
        pieces += [up, down]
    pieces += [lax.ppermute(up[:1], Z, ring_perm(-1)), lax.ppermute(down[1:], Z, ring_perm(1))]
    in_half = call(assemble_in_kernel, [((2, PIECE, TILE), bf16)], numbers(z), *pieces)
    in_other = lax.ppermute(in_half, CORE, SWAP2)
    square = (TILE, TILE)
    in_inverse = call(
        functools.partial(in_inverse_kernel, tokens),
        [(square, bf16)],
        numbers(core),
        in_half,
        in_other,
        scratch=[(square, bf16), (square, f32), (square, bf16)],
    )

    out_tile = pair_sum(ring_reduce(out_chunk, True), YH)
    other = lax.ppermute(out_tile, YL, SWAP2)
    both = jnp.stack([out_tile, other])
    got = [lax.ppermute(both, X, [(i, (i + s) % 4) for i in range(4)]) for s in (1, 2, 3)]
    out_half = call(
        assemble_out_kernel, [((2, PIECE, TILE), bf16)], numbers(yl, x), out_tile, other, *got
    )
    out_other = lax.ppermute(out_half, CORE, SWAP2)
    m = z % 4
    row = 2 * yh + core
    slice_rows = out_width // lax.axis_size(DP)
    base = TILE * (m - m // 2)
    near = jnp.where(m == 3, 2, m + 1)
    own_at = jnp.where(m == 2, TILE, slice_rows * (4 * m + row) - base)
    near_at = jnp.where(m == 2, TILE, slice_rows * (4 * near + row) - base)
    own_at, near_at = [jnp.clip(a, -slice_rows, TILE) + slice_rows for a in (own_at, near_at)]
    out_inverse = call(
        functools.partial(out_inverse_kernel, tokens, slice_rows),
        [((2 * slice_rows, TILE), bf16)],
        numbers(core, own_at, near_at),
        out_half,
        out_other,
        scratch=[(square, bf16), ((TILE + 2 * slice_rows, TILE), f32), (square, bf16)],
    )

    cross = ring_reduce(cross_of, True).astype(bf16)
    middle = mdot(cross, in_inverse).astype(bf16)
    mine = lax.dynamic_slice_in_dim(middle, h * HALF, HALF, 1)
    theirs = lax.dynamic_slice_in_dim(middle, (1 - h) * HALF, HALF, 1)
    near_x = lax.ppermute(theirs, X, SWAP_X)
    near_y = lax.ppermute(mine, YH, SWAP2)
    near_xy = lax.ppermute(theirs, (YH, X), SWAP_BOTH)
    middle = in_order(h, in_order(yh, mine, near_y), in_order(yh, near_x, near_xy))
    other = lax.ppermute(middle, CORE, SWAP2)
    middle = jnp.moveaxis(in_order(core, middle, other), 0, 1).reshape(TILE, HALF)
    result = mdot(out_inverse, middle)

    near_part = result[slice_rows:].astype(bf16)
    up = lax.ppermute(near_part, Z, [(0, 1), (1, 2), (4, 5), (5, 6)])
    down = lax.ppermute(near_part, Z, [(3, 2), (7, 6)])
    squares = all_sum(all_sum(jnp.sum(result * result), OWNER), DP)
    summed = result[:slice_rows] + up.astype(f32) + down.astype(f32)
    return (summed * lax.rsqrt(squares / (width * out_width) + 1e-06)).astype(bf16)


def solution(mesh):
    split = Mesh(mesh.devices.reshape(8, 2, 2, 2, 4), DP + OWNER)
    return jax.shard_map(
        shards,
        mesh=split,
        in_specs=(P(DP, None), P(), P(DP, None)),
        out_specs=P(DP, OWNER),
        check_vma=False,
    )
```

```python
import functools

import jax
import jax.numpy as jnp
from jax import lax
from jax.experimental import pallas as pl
from jax.experimental.pallas import tpu as pltpu
from jax.sharding import Mesh
from jax.sharding import PartitionSpec as P

TILE = 1024
PIECE = 256
HALF = 512
Z, YH, CORE, YL, X = "dp_0", "dp_1", "dp_2", "owner_0", "owner_1"
DP = (Z, YH, CORE)
OWNER = (YL, X)
DAMPING = 0.1
bf16, f32 = jnp.bfloat16, jnp.float32
PARAMS = pltpu.CompilerParams(vmem_limit_bytes=48 * 1024 * 1024)
VMEM = pl.BlockSpec(memory_space=pltpu.VMEM)
SMEM = pl.BlockSpec(memory_space=pltpu.SMEM)

FAR, NEAR = (4, 3, -3, 2), (-2, 1, -1, 0)
SWAP2 = [(0, 1), (1, 0)]
SWAP_X = [(0, 1), (1, 0), (2, 3), (3, 2)]
SWAP_BOTH = [(4 * a + b, 4 * (1 - a) + (b ^ 1)) for a in range(2) for b in range(4)]


def tdot(a, b):
    return lax.dot_general(a, b, (((0,), (0,)), ((), ())), preferred_element_type=f32)


def mdot(a, b):
    return jnp.dot(a, b, preferred_element_type=f32)


def aligned(start, size):
    return pl.ds(pl.multiple_of(start, size), size)


def pick_kernel(out_blocks, at_ref, cot_ref, left_ref, send_ref):
    piece, other, k = at_ref[0], at_ref[1], at_ref[2]
    width = out_blocks * PIECE
    for j in range(out_blocks):
        here = slice(j * PIECE, (j + 1) * PIECE)
        there = slice(width + j * PIECE, width + (j + 1) * PIECE)
        left_ref[:, here] = cot_ref[:, aligned(j * TILE + piece * PIECE, PIECE)]
        send_ref[:, here] = cot_ref[:, aligned(j * TILE + other * PIECE, PIECE)]
        send_ref[:, there] = cot_ref[:, aligned(j * TILE + k * PIECE, PIECE)]


def factor_kernel(blocks, at_ref, left_ref, send_ref, recv_ref, own_ref, got_ref, part_ref):
    piece = aligned(at_ref[0] * PIECE, PIECE)
    width = left_ref.shape[1]
    for plane, j in enumerate(blocks):
        here = slice(j * PIECE, (j + 1) * PIECE)
        there = slice(width + j * PIECE, width + (j + 1) * PIECE)
        part_ref[plane, :PIECE] = tdot(left_ref[:, here], send_ref[:, there]) + tdot(
            recv_ref[:, here], recv_ref[:, there]
        )
    for q in range(4):
        there = slice(q * PIECE, (q + 1) * PIECE)
        tile = tdot(own_ref[:, piece], own_ref[:, there]) + tdot(got_ref[:, piece], got_ref[:, there])
        for plane in range(len(blocks)):
            part_ref[plane, PIECE + 32 * q : PIECE + 32 * (q + 1)] = tile[32 * plane : 32 * (plane + 1)]


def cross_kernel(at_ref, left_ref, recv_ref, own_ref, got_ref, keep_ref, give_ref):
    mine = aligned(at_ref[3] * 128, 128)
    other = aligned((1 - at_ref[3]) * 128, 128)
    own, got = own_ref[...], got_ref[...]
    keep_ref[0] = tdot(left_ref[:, mine], own) + tdot(recv_ref[:, mine], got)
    give_ref[0] = (tdot(left_ref[:, other], own) + tdot(recv_ref[:, other], got)).astype(bf16)


def assemble_in_kernel(at_ref, *refs):
    pieces, out_ref = refs[:-1], refs[-1]
    z = at_ref[0]
    for q in range(4):
        there = slice(q * PIECE, (q + 1) * PIECE)
        part = slice(32 * q, 32 * (q + 1))
        for delta, ref in zip((0, 1, -1, 2, -2, 3, -3), pieces):
            out_ref[:, aligned((z + delta + 8) % 8 * 32, 32), there] = ref[:, part]
        far = aligned((z + 4) % 8 * 32, 32)
        out_ref[0, far, there] = pieces[7][0, part]
        out_ref[1, far, there] = pieces[8][0, part]


def assemble_out_kernel(at_ref, own_ref, other_ref, *refs):
    yl, x = at_ref[0], at_ref[1]
    out_ref = refs[-1]
    for s in range(4):
        source = (x - s + 4) % 4
        for b in range(2):
            column = 2 * jnp.where(b == 0, yl, 1 - yl) + source // 2
            value = (own_ref, other_ref)[b][...] if s == 0 else refs[s - 1][b]
            out_ref[source % 2, :, aligned(column * PIECE, PIECE)] = value


def load_factor(tokens, core, own_ref, other_ref, sums_ref):
    for half in range(2):
        sums_ref[aligned((2 * half + core) * PIECE, PIECE), :] = own_ref[half]
        sums_ref[aligned((2 * half + 1 - core) * PIECE, PIECE), :] = other_ref[half]
    largest = jnp.zeros((), f32)
    for r in range(4):
        rows = matrix_rows(tokens, sums_ref, r * PIECE)
        largest = jnp.maximum(largest, jnp.max(jnp.sum(jnp.abs(rows), axis=1)))
    return 1.0 / largest


def eye_rows(start, count):
    row = lax.broadcasted_iota(jnp.int32, (count, TILE), 0) + start
    return (row == lax.broadcasted_iota(jnp.int32, (count, TILE), 1)).astype(f32)


def matrix_rows(tokens, sums_ref, start):
    return sums_ref[start : start + PIECE, :].astype(f32) / tokens + DAMPING * eye_rows(start, PIECE)


def in_inverse_kernel(tokens, at_ref, own_ref, other_ref, out_ref, sums_ref, first_ref, low_ref):
    scale = load_factor(tokens, at_ref[0], own_ref, other_ref, sums_ref)
    for r in range(4):
        here = slice(r * PIECE, (r + 1) * PIECE)
        rows = matrix_rows(tokens, sums_ref, r * PIECE)
        first = 2.0 * scale * eye_rows(r * PIECE, PIECE) - (scale * scale) * rows
        first_ref[here, :] = first
        low_ref[here, :] = first.astype(bf16)
        sums_ref[here, :] = rows.astype(bf16)
    for r in range(4):
        here = slice(r * PIECE, (r + 1) * PIECE)
        product = mdot(low_ref[here, :], sums_ref[...]).astype(bf16)
        out_ref[here, :] = (2.0 * first_ref[here, :] - mdot(product, low_ref[...])).astype(bf16)


def out_inverse_kernel(tokens, count, at_ref, own_ref, other_ref, out_ref, sums_ref, first_ref, low_ref):
    scale = load_factor(tokens, at_ref[0], own_ref, other_ref, sums_ref)
    first_ref[:count, :] = jnp.zeros((count, TILE), f32)
    first_ref[count + TILE :, :] = jnp.zeros((count, TILE), f32)
    for r in range(4):
        here = slice(r * PIECE, (r + 1) * PIECE)
        rows = matrix_rows(tokens, sums_ref, r * PIECE)
        first = 2.0 * scale * eye_rows(r * PIECE, PIECE) - (scale * scale) * rows
        first_ref[count + r * PIECE : count + (r + 1) * PIECE, :] = first
        low_ref[here, :] = first.astype(bf16)
        sums_ref[here, :] = rows.astype(bf16)
    for part in range(2):
        rows = first_ref[pl.ds(pl.multiple_of(at_ref[1 + part], 64), count), :]
        product = mdot(rows.astype(bf16), sums_ref[...]).astype(bf16)
        out_ref[part * count : (part + 1) * count, :] = (
            2.0 * rows - mdot(product, low_ref[...])
        ).astype(bf16)


def call(kernel, outs, *args, scratch=()):
    outs = [jax.ShapeDtypeStruct(shape, dtype) for shape, dtype in outs]
    result = pl.pallas_call(
        kernel,
        out_shape=outs,
        in_specs=[SMEM] + [VMEM] * (len(args) - 1),
        out_specs=[VMEM] * len(outs),
        scratch_shapes=[pltpu.VMEM(shape, dtype) for shape, dtype in scratch],
        compiler_params=PARAMS,
    )(*args)
    return result[0] if len(outs) == 1 else result


def ring_perm(step, delta=0, skip=False):
    pairs = [(i, (i + step) % 8) for i in range(8)]
    if skip:
        pairs = [(i, j) for i, j in pairs if (i + delta) % 4 != 2]
    return pairs


def ring_start(chunk, skip):
    far = chunk(4)
    half = far.shape[0] // 2
    low = lax.ppermute(far[:half].astype(bf16), Z, ring_perm(-1, -4, skip))
    high = lax.ppermute(far[half:].astype(bf16), Z, ring_perm(1, 4, skip))
    nothing = jnp.zeros_like(low)
    return jnp.concatenate([low, nothing], 0), jnp.concatenate([nothing, high], 0)


def ring_step(chunk, d, low, high, skip):
    send_low = (chunk(-d) + low.astype(f32)).astype(bf16)
    send_high = (chunk(d) + high.astype(f32)).astype(bf16)
    low = lax.ppermute(send_low, Z, ring_perm(-1, -d, skip))
    high = lax.ppermute(send_high, Z, ring_perm(1, d, skip))
    return low, high


def ring_end(chunk, low, high):
    return chunk(0) + low.astype(f32) + high.astype(f32)


def after(value, *others):
    return lax.optimization_barrier((value, *others))[0]


def pair_sum(a, axis):
    a = a.astype(bf16)
    return (a.astype(f32) + lax.ppermute(a, axis, SWAP2).astype(f32)).astype(bf16)


def in_order(flag, own, other):
    first = jnp.where(flag == 0, own, other)
    second = jnp.where(flag == 0, other, own)
    return jnp.stack([first, second])


def all_sum(value, axis):
    n = lax.axis_size(axis)
    shares = lax.all_to_all(jnp.full((n, 128), value, f32), axis, 0, 0, tiled=True)
    return jnp.sum(shares[:, 0])


def shards(hidden, norm_gain, cotangent):
    z, yh, core = lax.axis_index(Z), lax.axis_index(YH), lax.axis_index(CORE)
    yl, x = lax.axis_index(YL), lax.axis_index(X)
    k, h = 2 * yl + x // 2, x % 2
    piece, other_piece = 2 * h + core, 2 * h + 1 - core
    here, width = hidden.shape
    out_width = cotangent.shape[1]
    out_blocks = out_width // TILE
    tokens = here * lax.axis_size(DP)

    def numbers(*values):
        return jnp.stack([jnp.asarray(v, jnp.int32) for v in values])

    left, send = call(
        functools.partial(pick_kernel, out_blocks),
        [((here, out_blocks * PIECE), bf16), ((here, 2 * out_blocks * PIECE), bf16)],
        numbers(piece, other_piece, k),
        cotangent,
    )
    recv = lax.ppermute(send, CORE, SWAP2)

    states = hidden.astype(f32)
    rms = lax.rsqrt(jnp.mean(states * states, axis=1, keepdims=True) + 1e-05)
    gain = lax.dynamic_slice_in_dim(norm_gain, k * TILE, TILE)
    mine = lax.dynamic_slice_in_dim(hidden, k * TILE, TILE, 1)
    normed = (mine.astype(f32) * rms * gain).astype(bf16)
    normed_recv = lax.ppermute(normed, CORE, SWAP2)

    blocks = [3 * (p // 4) + p % 4 - p % 4 // 2 for p in range(8)]
    part = call(
        functools.partial(factor_kernel, blocks),
        [((8, PIECE + 128, PIECE), f32)],
        numbers(piece),
        left,
        send,
        recv,
        normed,
        normed_recv,
    )

    def part_chunk(delta):
        return lax.dynamic_index_in_dim(part, (z + delta + 8) % 8, 0, False)

    orders, slots = [], []
    for p in range(8):
        real = [[d for d in group if (p + d) % 4 != 2] for group in (FAR, NEAR)]
        orders.append([blocks[(p + d) % 8] for group in real for d in group])
        slots.append([g.index(d) if d in g else 0 for g, all_of in zip(real, (FAR, NEAR)) for d in all_of])
    table = jnp.asarray([o + s for o, s in zip(orders, slots)], jnp.int32)
    table = lax.dynamic_index_in_dim(table, z, 0, False)
    count = len(orders[0]) // 2

    def cross_part(first):
        at = jnp.concatenate([table[first : first + count], yh[None]])
        tall = pl.BlockSpec((here, PIECE), lambda i, at: (0, at[i]))
        whole = pl.BlockSpec((here, TILE), lambda i, at: (0, 0))
        out = pl.BlockSpec((1, 128, TILE), lambda i, at: (i, 0, 0))
        return pl.pallas_call(
            cross_kernel,
            grid_spec=pltpu.PrefetchScalarGridSpec(
                num_scalar_prefetch=1,
                grid=(count,),
                in_specs=[tall, tall, whole, whole],
                out_specs=[out, out],
            ),
            out_shape=[
                jax.ShapeDtypeStruct((count, 128, TILE), f32),
                jax.ShapeDtypeStruct((count, 128, TILE), bf16),
            ],
            compiler_params=PARAMS,
        )(at, left, recv, normed, normed_recv)

    far_keep, far_give = cross_part(0)
    near_keep, near_give = cross_part(count)
    far_got = lax.ppermute(far_give, YH, SWAP2)

    low, high = ring_start(part_chunk, False)
    for d in (3, 2, 1):
        low, high = ring_step(part_chunk, d, low, high, False)
    tiles = pair_sum(ring_end(part_chunk, low, high), YH)
    near_got = lax.ppermute(after(near_give, tiles), YH, SWAP2)

    def cross_chunk(delta):
        if delta in FAR:
            group, at, keep, got = FAR, 2 * count, far_keep, far_got
        else:
            group, at, keep, got = NEAR, 2 * count + len(FAR), near_keep, near_got
        slot = table[at + group.index(delta)]
        keep = lax.dynamic_index_in_dim(keep, slot, 0, False)
        return keep + lax.dynamic_index_in_dim(got, slot, 0, False).astype(f32)

    out_tile, in_tile = tiles[:PIECE], tiles[PIECE:]
    shard = in_order(h, in_tile, lax.ppermute(in_tile, X, SWAP_X))
    low, high = ring_start(cross_chunk, True)
    low, high = ring_step(cross_chunk, 3, low, high, True)
    shard = after(shard, low, high)
    pieces = [shard]
    up = down = shard
    for _ in range(3):
        up = lax.ppermute(up, Z, ring_perm(-1))
        down = lax.ppermute(down, Z, ring_perm(1))
        pieces += [up, down]
    pieces += [lax.ppermute(up[:1], Z, ring_perm(-1)), lax.ppermute(down[1:], Z, ring_perm(1))]
    low, high = lax.optimization_barrier((low, high, *pieces[-2:]))[:2]
    for d in (2, 1):
        low, high = ring_step(cross_chunk, d, low, high, True)
    cross = ring_end(cross_chunk, low, high).astype(bf16)

    in_half = call(assemble_in_kernel, [((2, PIECE, TILE), bf16)], numbers(z), *pieces)
    in_other = lax.ppermute(in_half, CORE, SWAP2)
    square = (TILE, TILE)
    in_inverse = call(
        functools.partial(in_inverse_kernel, tokens),
        [(square, bf16)],
        numbers(core),
        in_half,
        in_other,
        scratch=[(square, bf16), (square, f32), (square, bf16)],
    )

    other = lax.ppermute(out_tile, YL, SWAP2)
    both = jnp.stack([out_tile, other])
    got = [lax.ppermute(both, X, [(i, (i + s) % 4) for i in range(4)]) for s in (1, 2, 3)]
    out_half = call(
        assemble_out_kernel, [((2, PIECE, TILE), bf16)], numbers(yl, x), out_tile, other, *got
    )
    out_other = lax.ppermute(out_half, CORE, SWAP2)
    m = z % 4
    row = 2 * yh + core
    slice_rows = out_width // lax.axis_size(DP)
    base = TILE * (m - m // 2)
    near = jnp.where(m == 3, 2, m + 1)
    own_at = jnp.where(m == 2, TILE, slice_rows * (4 * m + row) - base)
    near_at = jnp.where(m == 2, TILE, slice_rows * (4 * near + row) - base)
    own_at, near_at = [jnp.clip(a, -slice_rows, TILE) + slice_rows for a in (own_at, near_at)]
    out_inverse = call(
        functools.partial(out_inverse_kernel, tokens, slice_rows),
        [((2 * slice_rows, TILE), bf16)],
        numbers(core, own_at, near_at),
        out_half,
        out_other,
        scratch=[(square, bf16), ((TILE + 2 * slice_rows, TILE), f32), (square, bf16)],
    )

    middle = mdot(cross, in_inverse).astype(bf16)
    mine = lax.dynamic_slice_in_dim(middle, h * HALF, HALF, 1)
    theirs = lax.dynamic_slice_in_dim(middle, (1 - h) * HALF, HALF, 1)
    near_x = lax.ppermute(theirs, X, SWAP_X)
    near_y = lax.ppermute(mine, YH, SWAP2)
    near_xy = lax.ppermute(theirs, (YH, X), SWAP_BOTH)
    middle = in_order(h, in_order(yh, mine, near_y), in_order(yh, near_x, near_xy))
    other = lax.ppermute(middle, CORE, SWAP2)
    middle = jnp.moveaxis(in_order(core, middle, other), 0, 1).reshape(TILE, HALF)
    result = mdot(out_inverse, middle)

    near_part = result[slice_rows:].astype(bf16)
    up = lax.ppermute(near_part, Z, [(0, 1), (1, 2), (4, 5), (5, 6)])
    down = lax.ppermute(near_part, Z, [(3, 2), (7, 6)])
    squares = all_sum(all_sum(jnp.sum(result * result), OWNER), DP)
    summed = result[:slice_rows] + up.astype(f32) + down.astype(f32)
    return (summed * lax.rsqrt(squares / (width * out_width) + 1e-06)).astype(bf16)


def solution(mesh):
    split = Mesh(mesh.devices.reshape(8, 2, 2, 2, 4), DP + OWNER)
    return jax.shard_map(
        shards,
        mesh=split,
        in_specs=(P(DP, None), P(), P(DP, None)),
        out_specs=P(DP, OWNER),
        check_vma=False,
    )
```

```python
import functools

import jax
import jax.numpy as jnp
from jax import lax
from jax.experimental import pallas as pl
from jax.experimental.pallas import tpu as pltpu
from jax.sharding import Mesh
from jax.sharding import PartitionSpec as P

TILE = 1024
PIECE = 256
HALF = 512
Z, YH, CORE, YL, X = "dp_0", "dp_1", "dp_2", "owner_0", "owner_1"
DP = (Z, YH, CORE)
OWNER = (YL, X)
DAMPING = 0.1
bf16, f32 = jnp.bfloat16, jnp.float32
PARAMS = pltpu.CompilerParams(vmem_limit_bytes=48 * 1024 * 1024)
SMEM = pl.BlockSpec(memory_space=pltpu.SMEM)

DELTAS = (4, 3, -3, 2, -2, 1, -1, 0)
SWAP2 = [(0, 1), (1, 0)]
SWAP_X = [(0, 1), (1, 0), (2, 3), (3, 2)]
SWAP_BOTH = [(4 * a + b, 4 * (1 - a) + (b ^ 1)) for a in range(2) for b in range(4)]


def tdot(a, b):
    return lax.dot_general(a, b, (((0,), (0,)), ((), ())), preferred_element_type=f32)


def mdot(a, b):
    return jnp.dot(a, b, preferred_element_type=f32)


def aligned(start, size):
    return pl.ds(pl.multiple_of(start, size), size)


def pick_kernel(out_blocks, at_ref, cot_ref, left_ref, send_ref):
    piece, other, k = at_ref[0], at_ref[1], at_ref[2]
    width = out_blocks * PIECE
    for j in range(out_blocks):
        here = slice(j * PIECE, (j + 1) * PIECE)
        there = slice(width + j * PIECE, width + (j + 1) * PIECE)
        left_ref[:, here] = cot_ref[:, aligned(j * TILE + piece * PIECE, PIECE)]
        send_ref[:, here] = cot_ref[:, aligned(j * TILE + other * PIECE, PIECE)]
        send_ref[:, there] = cot_ref[:, aligned(j * TILE + k * PIECE, PIECE)]


def factor_kernel(blocks, at_ref, left_ref, send_ref, recv_ref, own_ref, got_ref, part_ref):
    piece = aligned(at_ref[0] * PIECE, PIECE)
    width = left_ref.shape[1]
    for plane, j in enumerate(blocks):
        here = slice(j * PIECE, (j + 1) * PIECE)
        there = slice(width + j * PIECE, width + (j + 1) * PIECE)
        part_ref[plane, :PIECE] = (
            tdot(left_ref[:, here], send_ref[:, there]) + tdot(recv_ref[:, here], recv_ref[:, there])
        ).astype(bf16)
    for q in range(4):
        there = slice(q * PIECE, (q + 1) * PIECE)
        tile = tdot(own_ref[:, piece], own_ref[:, there]) + tdot(got_ref[:, piece], got_ref[:, there])
        tile = tile.astype(bf16)
        for plane in range(len(blocks)):
            part_ref[plane, PIECE + 32 * q : PIECE + 32 * (q + 1)] = tile[32 * plane : 32 * (plane + 1)]


def cross_kernel(at_ref, left_ref, recv_ref, own_ref, got_ref, *refs):
    own, got = own_ref[...], got_ref[...]
    for i in range(len(DELTAS)):
        for part in range(2):
            rows = aligned(at_ref[1 + i] * PIECE + (at_ref[0] ^ part) * 128, 128)
            refs[2 * i + part][...] = (
                tdot(left_ref[:, rows], own) + tdot(recv_ref[:, rows], got)
            ).astype(bf16)


def assemble_in_kernel(at_ref, *refs):
    pieces, out_ref = refs[:-1], refs[-1]
    z = at_ref[0]
    for q in range(4):
        there = slice(q * PIECE, (q + 1) * PIECE)
        part = slice(32 * q, 32 * (q + 1))
        for delta, ref in zip((0, 1, -1, 2, -2, 3, -3), pieces):
            out_ref[:, aligned((z + delta + 8) % 8 * 32, 32), there] = ref[:, part]
        far = aligned((z + 4) % 8 * 32, 32)
        out_ref[0, far, there] = pieces[7][0, part]
        out_ref[1, far, there] = pieces[8][0, part]


def assemble_out_kernel(at_ref, own_ref, other_ref, *refs):
    yl, x = at_ref[0], at_ref[1]
    out_ref = refs[-1]
    for s in range(4):
        source = (x - s + 4) % 4
        for b in range(2):
            column = 2 * jnp.where(b == 0, yl, 1 - yl) + source // 2
            value = (own_ref, other_ref)[b][...] if s == 0 else refs[s - 1][b]
            out_ref[source % 2, :, aligned(column * PIECE, PIECE)] = value


def load_factor(tokens, core, own_ref, other_ref, sums_ref):
    for half in range(2):
        sums_ref[aligned((2 * half + core) * PIECE, PIECE), :] = own_ref[half]
        sums_ref[aligned((2 * half + 1 - core) * PIECE, PIECE), :] = other_ref[half]
    largest = jnp.zeros((), f32)
    for r in range(4):
        rows = matrix_rows(tokens, sums_ref, r * PIECE)
        largest = jnp.maximum(largest, jnp.max(jnp.sum(jnp.abs(rows), axis=1)))
    return 1.0 / largest


def eye_rows(start, count):
    row = lax.broadcasted_iota(jnp.int32, (count, TILE), 0) + start
    return (row == lax.broadcasted_iota(jnp.int32, (count, TILE), 1)).astype(f32)


def matrix_rows(tokens, sums_ref, start):
    return sums_ref[start : start + PIECE, :].astype(f32) / tokens + DAMPING * eye_rows(start, PIECE)


def in_inverse_kernel(tokens, at_ref, own_ref, other_ref, out_ref, sums_ref, first_ref, low_ref):
    scale = load_factor(tokens, at_ref[0], own_ref, other_ref, sums_ref)
    for r in range(4):
        here = slice(r * PIECE, (r + 1) * PIECE)
        rows = matrix_rows(tokens, sums_ref, r * PIECE)
        first = 2.0 * scale * eye_rows(r * PIECE, PIECE) - (scale * scale) * rows
        first_ref[here, :] = first
        low_ref[here, :] = first.astype(bf16)
        sums_ref[here, :] = rows.astype(bf16)
    for r in range(4):
        here = slice(r * PIECE, (r + 1) * PIECE)
        product = mdot(low_ref[here, :], sums_ref[...]).astype(bf16)
        out_ref[here, :] = (2.0 * first_ref[here, :] - mdot(product, low_ref[...])).astype(bf16)


def out_inverse_kernel(tokens, count, at_ref, own_ref, other_ref, out_ref, sums_ref, first_ref, low_ref):
    scale = load_factor(tokens, at_ref[0], own_ref, other_ref, sums_ref)
    first_ref[:count, :] = jnp.zeros((count, TILE), f32)
    first_ref[count + TILE :, :] = jnp.zeros((count, TILE), f32)
    for r in range(4):
        here = slice(r * PIECE, (r + 1) * PIECE)
        rows = matrix_rows(tokens, sums_ref, r * PIECE)
        first = 2.0 * scale * eye_rows(r * PIECE, PIECE) - (scale * scale) * rows
        first_ref[count + r * PIECE : count + (r + 1) * PIECE, :] = first
        low_ref[here, :] = first.astype(bf16)
        sums_ref[here, :] = rows.astype(bf16)
    for part in range(2):
        rows = first_ref[pl.ds(pl.multiple_of(at_ref[1 + part], 64), count), :]
        product = mdot(rows.astype(bf16), sums_ref[...]).astype(bf16)
        out_ref[part * count : (part + 1) * count, :] = (
            2.0 * rows - mdot(product, low_ref[...])
        ).astype(bf16)


def call(kernel, outs, *args, scratch=()):
    outs = [jax.ShapeDtypeStruct(shape, dtype) for shape, dtype in outs]

    def whole(a):
        return pl.BlockSpec(a.shape, lambda i: (0,) * len(a.shape))

    result = pl.pallas_call(
        kernel,
        grid=(1,),
        out_shape=outs,
        in_specs=[SMEM] + [whole(a) for a in args[1:]],
        out_specs=[whole(a) for a in outs],
        scratch_shapes=[pltpu.VMEM(shape, dtype) for shape, dtype in scratch],
        compiler_params=PARAMS,
    )(*args)
    return result[0] if len(outs) == 1 else result


def ring_perm(step, delta=0, skip=False):
    pairs = [(i, (i + step) % 8) for i in range(8)]
    if skip:
        pairs = [(i, j) for i, j in pairs if (i + delta) % 4 != 2]
    return pairs


def phase(*sends):
    values = lax.optimization_barrier(tuple(send[0] for send in sends))
    got = [lax.ppermute(value, *send[1:]) for value, send in zip(values, sends)]
    return lax.optimization_barrier(tuple(got))


def ring_start(chunk, skip):
    far = chunk(4).astype(bf16)
    half = far.shape[0] // 2
    return [(far[:half], Z, ring_perm(-1, -4, skip)), (far[half:], Z, ring_perm(1, 4, skip))]


def widened(low, high):
    nothing = jnp.zeros_like(low)
    return jnp.concatenate([low, nothing], 0), jnp.concatenate([nothing, high], 0)


def ring_step(chunk, d, low, high, skip):
    send_low = (chunk(-d) + low.astype(f32)).astype(bf16)
    send_high = (chunk(d) + high.astype(f32)).astype(bf16)
    return [(send_low, Z, ring_perm(-1, -d, skip)), (send_high, Z, ring_perm(1, d, skip))]


def ring_end(chunk, low, high):
    return chunk(0) + low.astype(f32) + high.astype(f32)


def in_order(flag, own, other):
    first = jnp.where(flag == 0, own, other)
    second = jnp.where(flag == 0, other, own)
    return jnp.stack([first, second])


def all_sum(value, axis):
    n = lax.axis_size(axis)
    shares = lax.all_to_all(jnp.full((n, 128), value, f32), axis, 0, 0, tiled=True)
    return jnp.sum(shares[:, 0])


def shards(hidden, norm_gain, cotangent):
    z, yh, core = lax.axis_index(Z), lax.axis_index(YH), lax.axis_index(CORE)
    yl, x = lax.axis_index(YL), lax.axis_index(X)
    k, h = 2 * yl + x // 2, x % 2
    piece, other_piece = 2 * h + core, 2 * h + 1 - core
    here, width = hidden.shape
    out_width = cotangent.shape[1]
    out_blocks = out_width // TILE
    tokens = here * lax.axis_size(DP)

    def numbers(*values):
        return jnp.stack([jnp.asarray(v, jnp.int32) for v in values])

    left, send = call(
        functools.partial(pick_kernel, out_blocks),
        [((here, out_blocks * PIECE), bf16), ((here, 2 * out_blocks * PIECE), bf16)],
        numbers(piece, other_piece, k),
        cotangent,
    )
    recv = lax.ppermute(send, CORE, SWAP2)

    states = hidden.astype(f32)
    rms = lax.rsqrt(jnp.mean(states * states, axis=1, keepdims=True) + 1e-05)
    gain = lax.dynamic_slice_in_dim(norm_gain, k * TILE, TILE)
    mine = lax.dynamic_slice_in_dim(hidden, k * TILE, TILE, 1)
    normed = (mine.astype(f32) * rms * gain).astype(bf16)
    normed_recv = lax.ppermute(normed, CORE, SWAP2)

    blocks = [3 * (p // 4) + p % 4 - p % 4 // 2 for p in range(8)]
    part = call(
        functools.partial(factor_kernel, blocks),
        [((8, PIECE + 128, PIECE), bf16)],
        numbers(piece),
        left,
        send,
        recv,
        normed,
        normed_recv,
    )
    planes = [(z + delta + 8) % 8 for delta in DELTAS]
    rows = (128, TILE)
    cross_parts = call(
        cross_kernel,
        [(rows, bf16)] * (2 * len(DELTAS)),
        numbers(yh, *[3 * (p // 4) + p % 4 - p % 4 // 2 for p in planes]),
        left,
        recv,
        normed,
        normed_recv,
    )
    keep, give = dict(zip(DELTAS, cross_parts[::2])), dict(zip(DELTAS, cross_parts[1::2]))
    got = {}

    def part_chunk(delta):
        return lax.dynamic_index_in_dim(part, (z + delta + 8) % 8, 0, False).astype(f32)

    def y_send(delta):
        pairs = [(2 * p + a, 2 * p + 1 - a) for p in range(8) for a in range(2)]
        return give[delta], (Z, YH), [(i, j) for i, j in pairs if (i // 2 + delta) % 4 != 2]

    def cross_chunk(delta):
        return keep[delta].astype(f32) + got[delta].astype(f32)

    low, high = phase(*ring_start(part_chunk, False))
    low, high = widened(low, high)
    low, high, got[4] = phase(*ring_step(part_chunk, 3, low, high, False), y_send(4))
    low, high, got[3] = phase(*ring_step(part_chunk, 2, low, high, False), y_send(3))
    low, high, got[-3] = phase(*ring_step(part_chunk, 1, low, high, False), y_send(-3))
    got[-4] = got[4]
    tiles = ring_end(part_chunk, low, high).astype(bf16)
    other, low, high = phase((tiles, YH, SWAP2), *ring_start(cross_chunk, True))
    low, high = widened(low, high)
    tiles = (tiles.astype(f32) + other.astype(f32)).astype(bf16)
    out_tile, in_tile = tiles[:PIECE], tiles[PIECE:]
    near_in, near_out, low, high, got[2] = phase(
        (in_tile, X, SWAP_X),
        (out_tile, YL, SWAP2),
        *ring_step(cross_chunk, 3, low, high, True),
        y_send(2),
    )
    up = down = shard = in_order(h, in_tile, near_in)
    both = jnp.stack([out_tile, near_out])
    slow = [(both, X, [(i, (i + s) % 4) for i in range(4)]) for s in (1, 2, 3)]
    slow += [y_send(-2), y_send(1)]
    values = lax.optimization_barrier((shard, *[send[0] for send in slow]))
    up = down = shard = values[0]
    slow = [lax.ppermute(value, *send[1:]) for value, send in zip(values[1:], slow)]
    pieces = [shard]
    for _ in range(3):
        up, down = phase((up, Z, ring_perm(-1)), (down, Z, ring_perm(1)))
        pieces += [up, down]
    pieces += phase((up[:1], Z, ring_perm(-1)), (down[1:], Z, ring_perm(1)))
    *pieces, x1, x2, x3, got[-2], got[1] = lax.optimization_barrier((*pieces, *slow))
    in_half = call(assemble_in_kernel, [((2, PIECE, TILE), bf16)], numbers(z), *pieces)
    in_other, low, high, got[-1] = phase(
        (in_half, CORE, SWAP2), *ring_step(cross_chunk, 2, low, high, True), y_send(-1)
    )
    out_half = call(
        assemble_out_kernel, [((2, PIECE, TILE), bf16)], numbers(yl, x), out_tile, near_out, x1, x2, x3
    )
    out_other, low, high, got[0] = phase(
        (out_half, CORE, SWAP2), *ring_step(cross_chunk, 1, low, high, True), y_send(0)
    )
    cross = ring_end(cross_chunk, low, high).astype(bf16)
    square = (TILE, TILE)
    in_inverse = call(
        functools.partial(in_inverse_kernel, tokens),
        [(square, bf16)],
        numbers(core),
        in_half,
        in_other,
        scratch=[(square, bf16), (square, f32), (square, bf16)],
    )

    m = z % 4
    row = 2 * yh + core
    slice_rows = out_width // lax.axis_size(DP)
    base = TILE * (m - m // 2)
    near = jnp.where(m == 3, 2, m + 1)
    own_at = jnp.where(m == 2, TILE, slice_rows * (4 * m + row) - base)
    near_at = jnp.where(m == 2, TILE, slice_rows * (4 * near + row) - base)
    own_at, near_at = [jnp.clip(a, -slice_rows, TILE) + slice_rows for a in (own_at, near_at)]
    out_inverse = call(
        functools.partial(out_inverse_kernel, tokens, slice_rows),
        [((2 * slice_rows, TILE), bf16)],
        numbers(core, own_at, near_at),
        out_half,
        out_other,
        scratch=[(square, bf16), ((TILE + 2 * slice_rows, TILE), f32), (square, bf16)],
    )

    middle = mdot(cross, in_inverse).astype(bf16)
    mine = lax.dynamic_slice_in_dim(middle, h * HALF, HALF, 1)
    theirs = lax.dynamic_slice_in_dim(middle, (1 - h) * HALF, HALF, 1)
    near_x, near_y, near_xy = phase(
        (theirs, X, SWAP_X), (mine, YH, SWAP2), (theirs, (YH, X), SWAP_BOTH)
    )
    middle = in_order(h, in_order(yh, mine, near_y), in_order(yh, near_x, near_xy))
    other = lax.ppermute(middle, CORE, SWAP2)
    middle = jnp.moveaxis(in_order(core, middle, other), 0, 1).reshape(TILE, HALF)
    result = mdot(out_inverse, middle)

    near_part = result[slice_rows:].astype(bf16)
    up = lax.ppermute(near_part, Z, [(0, 1), (1, 2), (4, 5), (5, 6)])
    down = lax.ppermute(near_part, Z, [(3, 2), (7, 6)])
    squares = all_sum(all_sum(jnp.sum(result * result), OWNER), DP)
    summed = result[:slice_rows] + up.astype(f32) + down.astype(f32)
    return (summed * lax.rsqrt(squares / (width * out_width) + 1e-06)).astype(bf16)


def solution(mesh):
    split = Mesh(mesh.devices.reshape(8, 2, 2, 2, 4), DP + OWNER)
    return jax.shard_map(
        shards,
        mesh=split,
        in_specs=(P(DP, None), P(), P(DP, None)),
        out_specs=P(DP, OWNER),
        check_vma=False,
    )
```

```python
import functools

import jax
import jax.numpy as jnp
from jax import lax
from jax.experimental import pallas as pl
from jax.experimental.pallas import tpu as pltpu
from jax.sharding import Mesh
from jax.sharding import PartitionSpec as P

TILE = 1024
PIECE = 256
HALF = 512
Z, YH, CORE, YL, X = "dp_0", "dp_1", "dp_2", "owner_0", "owner_1"
DP = (Z, YH, CORE)
OWNER = (YL, X)
DAMPING = 0.1
bf16, f32 = jnp.bfloat16, jnp.float32
PARAMS = pltpu.CompilerParams(vmem_limit_bytes=48 * 1024 * 1024)
SMEM = pl.BlockSpec(memory_space=pltpu.SMEM)

AWAY = (4, 3, 3, 2, 2, 1, 1, 0, 0)
SWAP2 = [(0, 1), (1, 0)]
SWAP_X = [(0, 1), (1, 0), (2, 3), (3, 2)]
SWAP_BOTH = [(4 * a + b, 4 * (1 - a) + (b ^ 1)) for a in range(2) for b in range(4)]


def tdot(a, b):
    return lax.dot_general(a, b, (((0,), (0,)), ((), ())), preferred_element_type=f32)


def mdot(a, b):
    return jnp.dot(a, b, preferred_element_type=f32)


def aligned(start, size):
    return pl.ds(pl.multiple_of(start, size), size)


def pick_kernel(out_blocks, at_ref, cot_ref, pick_ref):
    h, k = at_ref[0], at_ref[1]
    for j in range(out_blocks):
        here = slice(j * HALF, (j + 1) * HALF)
        there = slice(out_blocks * HALF + j * PIECE, out_blocks * HALF + (j + 1) * PIECE)
        pick_ref[:, here] = cot_ref[:, aligned(j * TILE + h * HALF, HALF)]
        pick_ref[:, there] = cot_ref[:, aligned(j * TILE + k * PIECE, PIECE)]


def factor_kernel(out_blocks, at_ref, pick_ref, recv_ref, own_ref, got_ref, part_ref):
    i = pl.program_id(0)
    h, plane, block, piece = at_ref[0], at_ref[2 + 3 * i], at_ref[3 + 3 * i], at_ref[4 + 3 * i]
    left = aligned(block * HALF + piece * PIECE, PIECE)
    right = aligned(out_blocks * HALF + block * PIECE, PIECE)
    part_ref[0, :, :PIECE] = (
        tdot(pick_ref[:, left], pick_ref[:, right]) + tdot(recv_ref[:, left], recv_ref[:, right])
    ).astype(bf16)
    rows, here = aligned((2 * h + piece) * PIECE, PIECE), aligned(plane * 128, 128)
    part_ref[0, :, PIECE:] = (
        tdot(own_ref[:, rows], own_ref[:, here]) + tdot(got_ref[:, rows], got_ref[:, here])
    ).astype(bf16)


def cross_kernel(at_ref, pick_ref, recv_ref, own_ref, got_ref, keep_ref, give_ref):
    i = pl.program_id(0)
    yh, block, piece = at_ref[1], at_ref[3 + 3 * i], at_ref[4 + 3 * i]
    for side, ref in ((yh, keep_ref), (1 - yh, give_ref)):
        rows = aligned(block * HALF + piece * PIECE + side * 128, 128)
        ref[0] = (
            tdot(pick_ref[:, rows], own_ref[...]) + tdot(recv_ref[:, rows], got_ref[...])
        ).astype(bf16)


def assemble_out_kernel(at_ref, own_ref, other_ref, *refs):
    yl, x = at_ref[0], at_ref[1]
    out_ref = refs[-1]
    for s in range(4):
        source = (x - s + 4) % 4
        for b in range(2):
            column = 2 * jnp.where(b == 0, yl, 1 - yl) + source // 2
            value = (own_ref, other_ref)[b][...] if s == 0 else refs[s - 1][b]
            out_ref[source % 2, :, aligned(column * PIECE, PIECE)] = value


def scale_of(tokens, sums_ref):
    largest = jnp.zeros((), f32)
    for r in range(4):
        rows = matrix_rows(tokens, sums_ref, r * PIECE)
        largest = jnp.maximum(largest, jnp.max(jnp.sum(jnp.abs(rows), axis=1)))
    return 1.0 / largest


def eye_rows(start, count):
    row = lax.broadcasted_iota(jnp.int32, (count, TILE), 0) + start
    return (row == lax.broadcasted_iota(jnp.int32, (count, TILE), 1)).astype(f32)


def matrix_rows(tokens, sums_ref, start):
    return sums_ref[start : start + PIECE, :].astype(f32) / tokens + DAMPING * eye_rows(start, PIECE)


def in_inverse_kernel(
    tokens, at_ref, shard_ref, one_ref, two_ref, three_ref, far_ref, other_ref,
    out_ref, sums_ref, first_ref, low_ref,
):
    z, core = at_ref[0], at_ref[1]
    back = 1 - 2 * core

    def put(h, away, value):
        here = aligned((z + away + 8) % 8 * 128, 128)
        for piece in range(2):
            rows = aligned((2 * h + piece) * PIECE, PIECE)
            sums_ref[rows, here] = value[:, piece * 128 : (piece + 1) * 128]

    for h in range(2):
        put(h, 0, shard_ref[h])
        for d, ref in ((1, one_ref), (2, two_ref), (3, three_ref)):
            put(h, back * d, ref[h])
            put(h, -back * d, other_ref[2 * (d - 1) + h])
    put(core, 4, far_ref[0])
    put(1 - core, 4, other_ref[6])
    scale = scale_of(tokens, sums_ref)
    for r in range(4):
        here = slice(r * PIECE, (r + 1) * PIECE)
        rows = matrix_rows(tokens, sums_ref, r * PIECE)
        first = 2.0 * scale * eye_rows(r * PIECE, PIECE) - (scale * scale) * rows
        first_ref[here, :] = first
        low_ref[here, :] = first.astype(bf16)
        sums_ref[here, :] = rows.astype(bf16)
    for r in range(4):
        here = slice(r * PIECE, (r + 1) * PIECE)
        product = mdot(low_ref[here, :], sums_ref[...]).astype(bf16)
        out_ref[here, :] = (2.0 * first_ref[here, :] - mdot(product, low_ref[...])).astype(bf16)


def out_inverse_kernel(tokens, count, at_ref, own_ref, other_ref, out_ref, sums_ref, first_ref, low_ref):
    core = at_ref[0]
    for half in range(2):
        sums_ref[aligned((2 * half + core) * PIECE, PIECE), :] = own_ref[half]
        sums_ref[aligned((2 * half + 1 - core) * PIECE, PIECE), :] = other_ref[half]
    scale = scale_of(tokens, sums_ref)
    first_ref[:count, :] = jnp.zeros((count, TILE), f32)
    first_ref[count + TILE :, :] = jnp.zeros((count, TILE), f32)
    for r in range(4):
        here = slice(r * PIECE, (r + 1) * PIECE)
        rows = matrix_rows(tokens, sums_ref, r * PIECE)
        first = 2.0 * scale * eye_rows(r * PIECE, PIECE) - (scale * scale) * rows
        first_ref[count + r * PIECE : count + (r + 1) * PIECE, :] = first
        low_ref[here, :] = first.astype(bf16)
        sums_ref[here, :] = rows.astype(bf16)
    for part in range(2):
        rows = first_ref[pl.ds(pl.multiple_of(at_ref[1 + part], 64), count), :]
        product = mdot(rows.astype(bf16), sums_ref[...]).astype(bf16)
        out_ref[part * count : (part + 1) * count, :] = (
            2.0 * rows - mdot(product, low_ref[...])
        ).astype(bf16)


def call(kernel, outs, *args, scratch=()):
    outs = [jax.ShapeDtypeStruct(shape, dtype) for shape, dtype in outs]

    def whole(a):
        return pl.BlockSpec(a.shape, lambda i: (0,) * len(a.shape))

    result = pl.pallas_call(
        kernel,
        grid=(1,),
        out_shape=outs,
        in_specs=[SMEM] + [whole(a) for a in args[1:]],
        out_specs=[whole(a) for a in outs],
        scratch_shapes=[pltpu.VMEM(shape, dtype) for shape, dtype in scratch],
        compiler_params=PARAMS,
    )(*args)
    return result[0] if len(outs) == 1 else result


def ring_pairs(away=0, skip=False):
    pairs = []
    for plane in range(8):
        for core, way in ((0, -1), (1, 1)):
            if not skip or (plane + way * away) % 4 != 2:
                pairs.append((2 * plane + core, 2 * ((plane + way) % 8) + core))
    return pairs


def phase(*sends):
    values = lax.optimization_barrier(tuple(send[0] for send in sends))
    got = [lax.ppermute(value, *send[1:]) for value, send in zip(values, sends)]
    return lax.optimization_barrier(tuple(got))


def added(*parts):
    return functools.reduce(jnp.add, [p.astype(f32) for p in parts])


def in_order(flag, own, other):
    first = jnp.where(flag == 0, own, other)
    second = jnp.where(flag == 0, other, own)
    return jnp.stack([first, second])


def all_sum(value, axis):
    n = lax.axis_size(axis)
    shares = lax.all_to_all(jnp.full((n, 128), value, f32), axis, 0, 0, tiled=True)
    return jnp.sum(shares[:, 0])


def shards(hidden, norm_gain, cotangent):
    z, yh, core = lax.axis_index(Z), lax.axis_index(YH), lax.axis_index(CORE)
    yl, x = lax.axis_index(YL), lax.axis_index(X)
    k, h = 2 * yl + x // 2, x % 2
    here, width = hidden.shape
    out_width = cotangent.shape[1]
    out_blocks = out_width // TILE
    tokens = here * lax.axis_size(DP)

    def numbers(*values):
        return jnp.stack([jnp.asarray(v, jnp.int32) for v in values])

    pick = call(
        functools.partial(pick_kernel, out_blocks),
        [((here, out_blocks * (HALF + PIECE)), bf16)],
        numbers(h, k),
        cotangent,
    )
    recv = lax.ppermute(pick, CORE, SWAP2)

    states = hidden.astype(f32)
    rms = lax.rsqrt(jnp.mean(states * states, axis=1, keepdims=True) + 1e-05)
    gain = lax.dynamic_slice_in_dim(norm_gain, k * TILE, TILE)
    mine = lax.dynamic_slice_in_dim(hidden, k * TILE, TILE, 1)
    normed = (mine.astype(f32) * rms * gain).astype(bf16)
    normed_recv = lax.ppermute(normed, CORE, SWAP2)

    way = 2 * core - 1
    table = []
    for i, away in enumerate(AWAY):
        plane = (z + way * away + 8) % 8
        piece = core if i in (0, 7) else 1 - core if i == 8 else (i + 1) % 2
        table += [plane, 3 * (plane // 4) + plane % 4 - plane % 4 // 2, piece]
    table = numbers(h, yh, *table)

    def slots(kernel, count, block, n_out):
        tokens_in = (pick, recv, normed, normed_recv)
        return pl.pallas_call(
            kernel,
            grid_spec=pltpu.PrefetchScalarGridSpec(
                num_scalar_prefetch=1,
                grid=(count,),
                in_specs=[pl.BlockSpec(a.shape, lambda i, at: (0, 0)) for a in tokens_in],
                out_specs=[pl.BlockSpec((1, *block), lambda i, at: (i, 0, 0))] * n_out,
            ),
            out_shape=[jax.ShapeDtypeStruct((count, *block), bf16)] * n_out,
            compiler_params=PARAMS,
        )(table, *tokens_in)

    (part,) = slots(functools.partial(factor_kernel, out_blocks), 9, (PIECE, PIECE + 128), 1)
    keep, give = slots(cross_kernel, 8, (128, TILE), 2)

    def y_send(slot):
        return give[slot], YH, SWAP2

    def ring(value, *args):
        return value, (Z, CORE), ring_pairs(*args)

    def widened(got):
        nothing = jnp.zeros_like(got)
        return in_order(core, got, nothing)

    (far,) = phase(ring(part[0]))
    far, y0 = phase(ring(added(part[1:3], widened(far)).astype(bf16)), y_send(0))
    far, y1 = phase(ring(added(part[3:5], far).astype(bf16)), y_send(1))
    far, y2 = phase(ring(added(part[5:7], far).astype(bf16)), y_send(2))
    both_in = jnp.concatenate([far[0, :, PIECE:], far[1, :, PIECE:]], 1)
    out_own = jnp.where(core == 0, far[0, :, :PIECE], far[1, :, :PIECE])
    out_other = jnp.where(core == 0, far[1, :, :PIECE], far[0, :, :PIECE])
    (other,) = phase((jnp.concatenate([out_other, both_in], 1), CORE, SWAP2))
    here_in = in_order(core, part[7, :, PIECE:], part[8, :, PIECE:])
    local = jnp.concatenate([part[7, :, :PIECE], here_in[0], here_in[1]], 1)
    tiles = (added(jnp.concatenate([out_own, both_in], 1), other) + local.astype(f32)).astype(bf16)
    other, far = phase((tiles, YH, SWAP2), ring(added(keep[0], y0).astype(bf16), 4, True))
    tiles = added(tiles, other).astype(bf16)
    out_tile, in_tile = tiles[:, :PIECE], tiles[:, PIECE:]
    near_in, near_out, far, y3 = phase(
        (in_tile, X, SWAP_X),
        (out_tile, YL, SWAP2),
        ring(added(keep[1:3], jnp.stack([y1, y2]), widened(far)).astype(bf16), 3, True),
        y_send(3),
    )
    shard = in_order(h, in_tile, near_in)
    both = jnp.stack([out_tile, near_out])

    def x_send(s):
        return both, X, [(i, (i + s) % 4) for i in range(4)]

    one, x1 = phase(ring(shard), x_send(1))
    two, x2 = phase(ring(one), x_send(2))
    three, x3 = phase(ring(two), x_send(3))
    last, y4 = phase(ring(jnp.where(core == 0, three[:1], three[1:])), y_send(4))
    out_half = call(
        assemble_out_kernel, [((2, PIECE, TILE), bf16)], numbers(yl, x), out_tile, near_out, x1, x2, x3
    )
    cross, in_other, y5, y6 = phase(
        ring(added(keep[3:5], jnp.stack([y3, y4]), far).astype(bf16), 2, True),
        (jnp.concatenate([one, two, three, last], 0), CORE, SWAP2),
        y_send(5),
        y_send(6),
    )
    cross, out_other, y7 = phase(
        ring(added(keep[5:7], jnp.stack([y5, y6]), cross).astype(bf16), 1, True),
        (out_half, CORE, SWAP2),
        y_send(7),
    )
    (other,) = phase((jnp.where(core == 0, cross[1], cross[0]), CORE, SWAP2))
    cross = added(jnp.where(core == 0, cross[0], cross[1]), other, keep[7], y7).astype(bf16)
    square = (TILE, TILE)
    in_inverse = call(
        functools.partial(in_inverse_kernel, tokens),
        [(square, bf16)],
        numbers(z, core),
        shard,
        one,
        two,
        three,
        last,
        in_other,
        scratch=[(square, bf16), (square, f32), (square, bf16)],
    )

    m = z % 4
    row = 2 * yh + core
    slice_rows = out_width // lax.axis_size(DP)
    base = TILE * (m - m // 2)
    near = jnp.where(m == 3, 2, m + 1)
    own_at = jnp.where(m == 2, TILE, slice_rows * (4 * m + row) - base)
    near_at = jnp.where(m == 2, TILE, slice_rows * (4 * near + row) - base)
    own_at, near_at = [jnp.clip(a, -slice_rows, TILE) + slice_rows for a in (own_at, near_at)]
    out_inverse = call(
        functools.partial(out_inverse_kernel, tokens, slice_rows),
        [((2 * slice_rows, TILE), bf16)],
        numbers(core, own_at, near_at),
        out_half,
        out_other,
        scratch=[(square, bf16), ((TILE + 2 * slice_rows, TILE), f32), (square, bf16)],
    )

    middle = mdot(cross, in_inverse).astype(bf16)
    mine = lax.dynamic_slice_in_dim(middle, h * HALF, HALF, 1)
    theirs = lax.dynamic_slice_in_dim(middle, (1 - h) * HALF, HALF, 1)
    near_x, near_y, near_xy = phase(
        (theirs, X, SWAP_X), (mine, YH, SWAP2), (theirs, (YH, X), SWAP_BOTH)
    )
    middle = in_order(h, in_order(yh, mine, near_y), in_order(yh, near_x, near_xy))
    other = lax.ppermute(middle, CORE, SWAP2)
    middle = jnp.moveaxis(in_order(core, middle, other), 0, 1).reshape(TILE, HALF)
    result = mdot(out_inverse, middle)

    near_part = result[slice_rows:].astype(bf16)
    up = lax.ppermute(near_part, Z, [(0, 1), (1, 2), (4, 5), (5, 6)])
    down = lax.ppermute(near_part, Z, [(3, 2), (7, 6)])
    squares = all_sum(all_sum(jnp.sum(result * result), OWNER), DP)
    summed = result[:slice_rows] + up.astype(f32) + down.astype(f32)
    return (summed * lax.rsqrt(squares / (width * out_width) + 1e-06)).astype(bf16)


def solution(mesh):
    split = Mesh(mesh.devices.reshape(8, 2, 2, 2, 4), DP + OWNER)
    return jax.shard_map(
        shards,
        mesh=split,
        in_specs=(P(DP, None), P(), P(DP, None)),
        out_specs=P(DP, OWNER),
        check_vma=False,
    )
```

```python
import functools

import jax
import jax.numpy as jnp
from jax import lax
from jax.experimental import pallas as pl
from jax.experimental.pallas import tpu as pltpu
from jax.sharding import Mesh
from jax.sharding import PartitionSpec as P

TILE = 1024
PIECE = 256
HALF = 512
Z, YH, CORE, YL, X = "dp_0", "dp_1", "dp_2", "owner_0", "owner_1"
DP = (Z, YH, CORE)
OWNER = (YL, X)
DAMPING = 0.1
bf16, f32 = jnp.bfloat16, jnp.float32
PARAMS = pltpu.CompilerParams(vmem_limit_bytes=48 * 1024 * 1024)

AWAY = (4, 3, 3, 2, 2, 1, 1, 0, 0)
GIVE_SLOT = (0, 1, 2, 3, 4, 4, 5, 5, 6, 7)
GIVE_START = (0, 0, 0, 0, 0, 64, 0, 64, 0, 0)
GIVE_ROWS = (128, 128, 128, 128, 64, 64, 64, 64, 128, 128)
SWAP2 = [(0, 1), (1, 0)]
SWAP_X = [(0, 1), (1, 0), (2, 3), (3, 2)]
SWAP_BOTH = [(4 * a + b, 4 * (1 - a) + (b ^ 1)) for a in range(2) for b in range(4)]


def tdot(a, b):
    return lax.dot_general(a, b, (((0,), (0,)), ((), ())), preferred_element_type=f32)


def mdot(a, b):
    return jnp.dot(a, b, preferred_element_type=f32)


def aligned(start, size):
    return pl.ds(pl.multiple_of(start, size), size)


def pick_kernel(out_blocks, at_ref, cot_ref, pick_ref):
    h, k = at_ref[0], at_ref[1]
    rows = pl.ds(pl.multiple_of(pl.program_id(0) * pick_ref.shape[0], 8), pick_ref.shape[0])
    for j in range(out_blocks):
        here = slice(j * HALF, (j + 1) * HALF)
        there = slice(out_blocks * HALF + j * PIECE, out_blocks * HALF + (j + 1) * PIECE)
        pick_ref[:, here] = cot_ref[rows, aligned(j * TILE + h * HALF, HALF)]
        pick_ref[:, there] = cot_ref[rows, aligned(j * TILE + k * PIECE, PIECE)]


def factor_kernel(out_blocks, at_ref, pick_ref, recv_ref, own_ref, got_ref, part_ref):
    i = pl.program_id(0)
    h, plane, block, piece = at_ref[0], at_ref[2 + 3 * i], at_ref[3 + 3 * i], at_ref[4 + 3 * i]
    left = aligned(block * HALF + piece * PIECE, PIECE)
    right = aligned(out_blocks * HALF + block * PIECE, PIECE)
    part_ref[0, :, :PIECE] = (
        tdot(pick_ref[:, left], pick_ref[:, right]) + tdot(recv_ref[:, left], recv_ref[:, right])
    ).astype(bf16)
    rows, here = aligned((2 * h + piece) * PIECE, PIECE), aligned(plane * 128, 128)
    part_ref[0, :, PIECE:] = (
        tdot(own_ref[:, rows], own_ref[:, here]) + tdot(got_ref[:, rows], got_ref[:, here])
    ).astype(bf16)


def cross_kernel(at_ref, pick_ref, recv_ref, own_ref, got_ref, keep_ref, *give_refs):
    i = pl.program_id(0)
    yh, block, piece = at_ref[1], at_ref[3 + 3 * i], at_ref[4 + 3 * i]

    def rows_of(side):
        rows = aligned(block * HALF + piece * PIECE + side * 128, 128)
        return (
            tdot(pick_ref[:, rows], own_ref[...]) + tdot(recv_ref[:, rows], got_ref[...])
        ).astype(bf16)

    keep_ref[0] = rows_of(yh)
    give = rows_of(1 - yh)
    for slot, start, ref in zip(GIVE_SLOT, GIVE_START, give_refs):

        @pl.when(i == slot)
        def _():
            ref[...] = give[start : start + ref.shape[0]]


def scale_of(tokens, sums_ref):
    largest = jnp.zeros((), f32)
    for r in range(4):
        rows = matrix_rows(tokens, sums_ref, r * PIECE)
        largest = jnp.maximum(largest, jnp.max(jnp.sum(jnp.abs(rows), axis=1)))
    return 1.0 / largest


def eye_rows(start, count):
    row = lax.broadcasted_iota(jnp.int32, (count, TILE), 0) + start
    return (row == lax.broadcasted_iota(jnp.int32, (count, TILE), 1)).astype(f32)


def matrix_rows(tokens, sums_ref, start):
    return sums_ref[start : start + PIECE, :].astype(f32) / tokens + DAMPING * eye_rows(start, PIECE)


def split_factor(tokens, sums_ref, first_ref, low_ref, offset):
    scale = scale_of(tokens, sums_ref)
    for r in range(4):
        here = slice(r * PIECE, (r + 1) * PIECE)
        rows = matrix_rows(tokens, sums_ref, r * PIECE)
        first = 2.0 * scale * eye_rows(r * PIECE, PIECE) - (scale * scale) * rows
        first_ref[offset + r * PIECE : offset + (r + 1) * PIECE, :] = first
        low_ref[here, :] = first.astype(bf16)
        sums_ref[here, :] = rows.astype(bf16)


def inverse_rows(rows, sums_ref, low_ref):
    product = mdot(rows.astype(bf16), sums_ref[...]).astype(bf16)
    return (2.0 * rows - mdot(product, low_ref[...])).astype(bf16)


def in_inverse_kernel(
    tokens, at_ref, shard_ref, one_ref, two_ref, three_ref, far_ref, other_ref,
    out_ref, sums_ref, first_ref, low_ref,
):
    i = pl.program_id(0)

    @pl.when(i == 0)
    def _():
        z, core = at_ref[0], at_ref[1]
        back = 1 - 2 * core

        def put(h, away, value):
            here = aligned((z + away + 8) % 8 * 128, 128)
            for piece in range(2):
                rows = aligned((2 * h + piece) * PIECE, PIECE)
                sums_ref[rows, here] = value[:, piece * 128 : (piece + 1) * 128]

        for h in range(2):
            put(h, 0, shard_ref[h])
            for d, ref in ((1, one_ref), (2, two_ref), (3, three_ref)):
                put(h, back * d, ref[h])
                put(h, -back * d, other_ref[2 * (d - 1) + h])
        put(core, 4, far_ref[0])
        put(1 - core, 4, other_ref[6])
        split_factor(tokens, sums_ref, first_ref, low_ref, 0)

    out_ref[...] = inverse_rows(first_ref[aligned(i * PIECE, PIECE), :], sums_ref, low_ref)


def out_inverse_kernel(tokens, count, at_ref, own_ref, other_ref, out_ref, sums_ref, first_ref, low_ref):
    i = pl.program_id(0)

    @pl.when(i == 0)
    def _():
        core = at_ref[0]
        for owner in range(8):
            here = slice(owner // 2 * PIECE, (owner // 2 + 1) * PIECE)
            for piece, ref in ((core, own_ref), (1 - core, other_ref)):
                sums_ref[aligned((2 * (owner % 2) + piece) * PIECE, PIECE), here] = ref[owner]
        first_ref[:count, :] = jnp.zeros((count, TILE), f32)
        first_ref[count + TILE :, :] = jnp.zeros((count, TILE), f32)
        split_factor(tokens, sums_ref, first_ref, low_ref, count)

    rows = first_ref[pl.ds(pl.multiple_of(at_ref[1 + i], 64), count), :]
    out_ref[...] = inverse_rows(rows, sums_ref, low_ref)


def call(kernel, steps, block, out_shape, at, *args, scratch=()):
    def whole(a):
        return pl.BlockSpec(a.shape, lambda i, at: (0,) * len(a.shape))

    return pl.pallas_call(
        kernel,
        grid_spec=pltpu.PrefetchScalarGridSpec(
            num_scalar_prefetch=1,
            grid=(steps,),
            in_specs=[whole(a) for a in args],
            out_specs=pl.BlockSpec(block, lambda i, at: (i, 0)),
            scratch_shapes=[pltpu.VMEM(shape, dtype) for shape, dtype in scratch],
        ),
        out_shape=jax.ShapeDtypeStruct(out_shape, bf16),
        compiler_params=PARAMS,
    )(at, *args)


def ring_pairs(away=0, skip=False):
    pairs = []
    for plane in range(8):
        for core, way in ((0, -1), (1, 1)):
            if not skip or (plane + way * away) % 4 != 2:
                pairs.append((2 * plane + core, 2 * ((plane + way) % 8) + core))
    return pairs


def phase(*sends):
    values = lax.optimization_barrier(tuple(send[0] for send in sends))
    got = [lax.ppermute(value, *send[1:]) for value, send in zip(values, sends)]
    return lax.optimization_barrier(tuple(got))


def added(*parts):
    return functools.reduce(jnp.add, [p.astype(f32) for p in parts])


def in_order(flag, own, other):
    first = jnp.where(flag == 0, own, other)
    second = jnp.where(flag == 0, other, own)
    return jnp.stack([first, second])


def all_sum(value, axis):
    n = lax.axis_size(axis)
    shares = lax.all_to_all(jnp.full((n, 128), value, f32), axis, 0, 0, tiled=True)
    return jnp.sum(shares[:, 0])


def shards(hidden, norm_gain, cotangent):
    z, yh, core = lax.axis_index(Z), lax.axis_index(YH), lax.axis_index(CORE)
    yl, x = lax.axis_index(YL), lax.axis_index(X)
    k, h = 2 * yl + x // 2, x % 2
    here, width = hidden.shape
    out_width = cotangent.shape[1]
    out_blocks = out_width // TILE
    tokens = here * lax.axis_size(DP)

    def numbers(*values):
        return jnp.stack([jnp.asarray(v, jnp.int32) for v in values])

    pick = call(
        functools.partial(pick_kernel, out_blocks),
        4,
        (here // 4, out_blocks * (HALF + PIECE)),
        (here, out_blocks * (HALF + PIECE)),
        numbers(h, k),
        cotangent,
    )
    recv = lax.ppermute(pick, CORE, SWAP2)

    states = hidden.astype(f32)
    rms = lax.rsqrt(jnp.mean(states * states, axis=1, keepdims=True) + 1e-05)
    gain = lax.dynamic_slice_in_dim(norm_gain, k * TILE, TILE)
    mine = lax.dynamic_slice_in_dim(hidden, k * TILE, TILE, 1)
    normed = (mine.astype(f32) * rms * gain).astype(bf16)
    normed_recv = lax.ppermute(normed, CORE, SWAP2)

    way = 2 * core - 1
    table = []
    for i, away in enumerate(AWAY):
        plane = (z + way * away + 8) % 8
        piece = core if i in (0, 7) else 1 - core if i == 8 else (i + 1) % 2
        table += [plane, 3 * (plane // 4) + plane % 4 - plane % 4 // 2, piece]
    table = numbers(h, yh, *table)

    def slots(kernel, count, block, gives=()):
        tokens_in = (pick, recv, normed, normed_recv)
        rows = [(n, TILE) for n in gives]
        return pl.pallas_call(
            kernel,
            grid_spec=pltpu.PrefetchScalarGridSpec(
                num_scalar_prefetch=1,
                grid=(count,),
                in_specs=[pl.BlockSpec(a.shape, lambda i, at: (0, 0)) for a in tokens_in],
                out_specs=[pl.BlockSpec((1, *block), lambda i, at: (i, 0, 0))]
                + [pl.BlockSpec(r, lambda i, at: (0, 0)) for r in rows],
            ),
            out_shape=[jax.ShapeDtypeStruct(r, bf16) for r in [(count, *block)] + rows],
            compiler_params=PARAMS,
        )(table, *tokens_in)

    (part,) = slots(functools.partial(factor_kernel, out_blocks), 9, (PIECE, PIECE + 128))
    keep, *give = slots(cross_kernel, 8, (128, TILE), GIVE_ROWS)

    def y_send(i):
        return give[i], YH, SWAP2

    def ring(value, *args):
        return value, (Z, CORE), ring_pairs(*args)

    def widened(got):
        nothing = jnp.zeros_like(got)
        return in_order(core, got, nothing)

    (far,) = phase(ring(part[0]))
    far, y0 = phase(ring(added(part[1:3], widened(far)).astype(bf16)), y_send(0))
    far, y1 = phase(ring(added(part[3:5], far).astype(bf16)), y_send(1))
    far, y2 = phase(ring(added(part[5:7], far).astype(bf16)), y_send(2))
    both_in = jnp.concatenate([far[0, :, PIECE:], far[1, :, PIECE:]], 1)
    out_own = jnp.where(core == 0, far[0, :, :PIECE], far[1, :, :PIECE])
    out_other = jnp.where(core == 0, far[1, :, :PIECE], far[0, :, :PIECE])
    (other,) = phase((jnp.concatenate([out_other, both_in], 1), CORE, SWAP2))
    here_in = in_order(core, part[7, :, PIECE:], part[8, :, PIECE:])
    local = jnp.concatenate([part[7, :, :PIECE], here_in[0], here_in[1]], 1)
    tiles = (added(jnp.concatenate([out_own, both_in], 1), other) + local.astype(f32)).astype(bf16)
    other, far = phase((tiles, YH, SWAP2), ring(added(keep[0], y0).astype(bf16), 4, True))
    tiles = added(tiles, other).astype(bf16)
    out_tile, in_tile = tiles[:, :PIECE], tiles[:, PIECE:]
    out_tiles = lax.all_gather(out_tile, OWNER)
    near_in, far, y3 = phase(
        (in_tile, X, SWAP_X),
        ring(added(keep[1:3], jnp.stack([y1, y2]), widened(far)).astype(bf16), 3, True),
        y_send(3),
    )
    shard = in_order(h, in_tile, near_in)
    one, y4 = phase(ring(shard), y_send(4))
    two, y5 = phase(ring(one), y_send(5))
    three, y6 = phase(ring(two), y_send(6))
    last, y7 = phase(ring(jnp.where(core == 0, three[:1], three[1:])), y_send(7))
    y4, y5 = jnp.concatenate([y4, y5]), jnp.concatenate([y6, y7])
    cross, in_other, y6 = phase(
        ring(added(keep[3:5], jnp.stack([y3, y4]), far).astype(bf16), 2, True),
        (jnp.concatenate([one, two, three, last], 0), CORE, SWAP2),
        y_send(8),
    )
    square = (TILE, TILE)
    in_inverse = call(
        functools.partial(in_inverse_kernel, tokens),
        4,
        (PIECE, TILE),
        square,
        numbers(z, core),
        shard,
        one,
        two,
        three,
        last,
        in_other,
        scratch=[(square, bf16), (square, f32), (square, bf16)],
    )
    cross, out_other, y7 = phase(
        ring(added(keep[5:7], jnp.stack([y5, y6]), cross).astype(bf16), 1, True),
        (out_tiles, CORE, SWAP2),
        y_send(9),
    )
    cross, in_inverse = lax.optimization_barrier((cross, in_inverse))
    (other,) = phase((jnp.where(core == 0, cross[1], cross[0]), CORE, SWAP2))
    cross = added(jnp.where(core == 0, cross[0], cross[1]), other, keep[7], y7).astype(bf16)
    m = z % 4
    row = 2 * yh + core
    slice_rows = out_width // lax.axis_size(DP)
    base = TILE * (m - m // 2)
    near = jnp.where(m == 3, 2, m + 1)
    own_at = jnp.where(m == 2, TILE, slice_rows * (4 * m + row) - base)
    near_at = jnp.where(m == 2, TILE, slice_rows * (4 * near + row) - base)
    own_at, near_at = [jnp.clip(a, -slice_rows, TILE) + slice_rows for a in (own_at, near_at)]
    out_inverse = call(
        functools.partial(out_inverse_kernel, tokens, slice_rows),
        2,
        (slice_rows, TILE),
        (2 * slice_rows, TILE),
        numbers(core, own_at, near_at),
        out_tiles,
        out_other,
        scratch=[(square, bf16), ((TILE + 2 * slice_rows, TILE), f32), (square, bf16)],
    )

    middle = mdot(cross, in_inverse).astype(bf16)
    mine = lax.dynamic_slice_in_dim(middle, h * HALF, HALF, 1)
    theirs = lax.dynamic_slice_in_dim(middle, (1 - h) * HALF, HALF, 1)
    near_x, near_y, near_xy = phase(
        (theirs, X, SWAP_X), (mine, YH, SWAP2), (theirs, (YH, X), SWAP_BOTH)
    )
    middle = in_order(h, in_order(yh, mine, near_y), in_order(yh, near_x, near_xy))
    other = lax.ppermute(middle, CORE, SWAP2)
    middle = jnp.moveaxis(in_order(core, middle, other), 0, 1).reshape(TILE, HALF)
    result = mdot(out_inverse, middle)

    near_part = result[slice_rows:].astype(bf16)
    up = lax.ppermute(near_part, Z, [(0, 1), (1, 2), (4, 5), (5, 6)])
    down = lax.ppermute(near_part, Z, [(3, 2), (7, 6)])
    squares = all_sum(all_sum(jnp.sum(result * result), OWNER), DP)
    summed = result[:slice_rows] + up.astype(f32) + down.astype(f32)
    return (summed * lax.rsqrt(squares / (width * out_width) + 1e-06)).astype(bf16)


def solution(mesh):
    split = Mesh(mesh.devices.reshape(8, 2, 2, 2, 4), DP + OWNER)
    return jax.shard_map(
        shards,
        mesh=split,
        in_specs=(P(DP, None), P(), P(DP, None)),
        out_specs=P(DP, OWNER),
        check_vma=False,
    )
```

```python
import functools

import jax
import jax.numpy as jnp
from jax import lax
from jax.experimental import pallas as pl
from jax.experimental.pallas import tpu as pltpu
from jax.sharding import Mesh
from jax.sharding import PartitionSpec as P

TILE = 1024
PIECE = 256
HALF = 512
Z, YH, CORE, YL, X = "dp_0", "dp_1", "dp_2", "owner_0", "owner_1"
DP = (Z, YH, CORE)
OWNER = (YL, X)
DAMPING = 0.1
bf16, f32 = jnp.bfloat16, jnp.float32
PARAMS = pltpu.CompilerParams(vmem_limit_bytes=48 * 1024 * 1024)

AWAY = (4, 3, 3, 2, 2, 1, 1, 0, 0)
GIVE_SLOTS = ((0,), (1,), (2,), (3, 4), (5, 6), (7,))
SWAP2 = [(0, 1), (1, 0)]
SWAP_X = [(0, 1), (1, 0), (2, 3), (3, 2)]
SWAP_BOTH = [(4 * a + b, 4 * (1 - a) + (b ^ 1)) for a in range(2) for b in range(4)]


def tdot(a, b):
    return lax.dot_general(a, b, (((0,), (0,)), ((), ())), preferred_element_type=f32)


def mdot(a, b):
    return jnp.dot(a, b, preferred_element_type=f32)


def aligned(start, size):
    return pl.ds(pl.multiple_of(start, size), size)


def pick_kernel(out_blocks, at_ref, cot_ref, pick_ref):
    h, k = at_ref[0], at_ref[1]
    rows = pl.ds(pl.multiple_of(pl.program_id(0) * pick_ref.shape[0], 8), pick_ref.shape[0])
    for j in range(out_blocks):
        here = slice(j * HALF, (j + 1) * HALF)
        there = slice(out_blocks * HALF + j * PIECE, out_blocks * HALF + (j + 1) * PIECE)
        pick_ref[:, here] = cot_ref[rows, aligned(j * TILE + h * HALF, HALF)]
        pick_ref[:, there] = cot_ref[rows, aligned(j * TILE + k * PIECE, PIECE)]


def load_tokens(pick_ref, recv_ref, own_ref, got_ref, out_ref, in_ref, sems):
    count = pick_ref.shape[0]
    copies = [
        pltpu.make_async_copy(src, dst.at[pl.ds(start, count)], sems.at[n])
        for n, (src, dst, start) in enumerate(
            (
                (pick_ref, out_ref, 0),
                (recv_ref, out_ref, count),
                (own_ref, in_ref, 0),
                (got_ref, in_ref, count),
            )
        )
    ]
    for copy in copies:
        copy.start()
    for copy in copies:
        copy.wait()


def factor_kernel(out_blocks, at_ref, pick_ref, recv_ref, own_ref, got_ref, part_ref, out_ref, in_ref, sems):
    i = pl.program_id(0)

    @pl.when(i == 0)
    def _():
        load_tokens(pick_ref, recv_ref, own_ref, got_ref, out_ref, in_ref, sems)

    h, plane, block, piece = at_ref[0], at_ref[2 + 3 * i], at_ref[3 + 3 * i], at_ref[4 + 3 * i]
    left = out_ref[:, aligned(block * HALF + piece * PIECE, PIECE)]
    right = out_ref[:, aligned(out_blocks * HALF + block * PIECE, PIECE)]
    part_ref[0, :, :PIECE] = tdot(left, right).astype(bf16)
    rows = in_ref[:, aligned((2 * h + piece) * PIECE, PIECE)]
    part_ref[0, :, PIECE:] = tdot(rows, in_ref[:, aligned(plane * 128, 128)]).astype(bf16)


def cross_kernel(at_ref, pick_ref, recv_ref, own_ref, got_ref, keep_ref, *refs):
    give_refs, (out_ref, in_ref, sems) = refs[:-3], refs[-3:]
    i = pl.program_id(0)

    @pl.when(i == 0)
    def _():
        load_tokens(pick_ref, recv_ref, own_ref, got_ref, out_ref, in_ref, sems)

    yh, block, piece = at_ref[1], at_ref[3 + 3 * i], at_ref[4 + 3 * i]

    def rows_of(side):
        rows = out_ref[:, aligned(block * HALF + piece * PIECE + side * 128, 128)]
        return tdot(rows, in_ref[...]).astype(bf16)

    keep_ref[0] = rows_of(yh)
    give = rows_of(1 - yh)
    for slots, ref in zip(GIVE_SLOTS, give_refs):
        for n, slot in enumerate(slots):

            @pl.when(i == slot)
            def _():
                ref[n] = give


def scale_of(tokens, sums_ref):
    largest = jnp.zeros((), f32)
    for r in range(4):
        rows = matrix_rows(tokens, sums_ref, r * PIECE)
        largest = jnp.maximum(largest, jnp.max(jnp.sum(jnp.abs(rows), axis=1)))
    return 1.0 / largest


def eye_rows(start, count):
    row = lax.broadcasted_iota(jnp.int32, (count, TILE), 0) + start
    return (row == lax.broadcasted_iota(jnp.int32, (count, TILE), 1)).astype(f32)


def matrix_rows(tokens, sums_ref, start):
    return sums_ref[start : start + PIECE, :].astype(f32) / tokens + DAMPING * eye_rows(start, PIECE)


def split_factor(tokens, sums_ref, first_ref, low_ref, offset):
    scale = scale_of(tokens, sums_ref)
    for r in range(4):
        here = slice(r * PIECE, (r + 1) * PIECE)
        rows = matrix_rows(tokens, sums_ref, r * PIECE)
        first = 2.0 * scale * eye_rows(r * PIECE, PIECE) - (scale * scale) * rows
        first_ref[offset + r * PIECE : offset + (r + 1) * PIECE, :] = first
        low_ref[here, :] = first.astype(bf16)
        sums_ref[here, :] = rows.astype(bf16)


def inverse_rows(rows, sums_ref, low_ref):
    product = mdot(rows.astype(bf16), sums_ref[...]).astype(bf16)
    return (2.0 * rows - mdot(product, low_ref[...])).astype(bf16)


def in_inverse_kernel(
    tokens, at_ref, shard_ref, own_ref, other_ref,
    out_ref, sums_ref, first_ref, low_ref,
):
    i = pl.program_id(0)

    @pl.when(i == 0)
    def _():
        z, core = at_ref[0], at_ref[1]
        back = 1 - 2 * core

        def put(h, away, value):
            here = aligned((z + away + 8) % 8 * 128, 128)
            for piece in range(2):
                rows = aligned((2 * h + piece) * PIECE, PIECE)
                sums_ref[rows, here] = value[:, piece * 128 : (piece + 1) * 128]

        for h in range(2):
            put(h, 0, shard_ref[h])
            for d in (1, 2, 3):
                put(h, back * d, own_ref[2 * (d - 1) + h])
                put(h, -back * d, other_ref[2 * (d - 1) + h])
        put(core, 4, own_ref[6])
        put(1 - core, 4, other_ref[6])
        split_factor(tokens, sums_ref, first_ref, low_ref, 0)

    out_ref[...] = inverse_rows(first_ref[aligned(i * PIECE, PIECE), :], sums_ref, low_ref)


def out_inverse_kernel(tokens, count, at_ref, own_ref, other_ref, out_ref, sums_ref, first_ref, low_ref):
    i = pl.program_id(0)

    @pl.when(i == 0)
    def _():
        core = at_ref[0]
        for owner in range(8):
            here = slice(owner // 2 * PIECE, (owner // 2 + 1) * PIECE)
            for piece, ref in ((core, own_ref), (1 - core, other_ref)):
                sums_ref[aligned((2 * (owner % 2) + piece) * PIECE, PIECE), here] = ref[owner]
        first_ref[:count, :] = jnp.zeros((count, TILE), f32)
        first_ref[count + TILE :, :] = jnp.zeros((count, TILE), f32)
        split_factor(tokens, sums_ref, first_ref, low_ref, count)

    rows = first_ref[pl.ds(pl.multiple_of(at_ref[1 + i], 64), count), :]
    out_ref[...] = inverse_rows(rows, sums_ref, low_ref)


def call(kernel, steps, block, out_shape, at, *args, scratch=()):
    def whole(a):
        return pl.BlockSpec(a.shape, lambda i, at: (0,) * len(a.shape))

    return pl.pallas_call(
        kernel,
        grid_spec=pltpu.PrefetchScalarGridSpec(
            num_scalar_prefetch=1,
            grid=(steps,),
            in_specs=[whole(a) for a in args],
            out_specs=pl.BlockSpec(block, lambda i, at: (i, 0)),
            scratch_shapes=[pltpu.VMEM(shape, dtype) for shape, dtype in scratch],
        ),
        out_shape=jax.ShapeDtypeStruct(out_shape, bf16),
        compiler_params=PARAMS,
    )(at, *args)


def ring_pairs(away=0, skip=False):
    pairs = []
    for plane in range(8):
        for core, way in ((0, -1), (1, 1)):
            if not skip or (plane + way * away) % 4 != 2:
                pairs.append((2 * plane + core, 2 * ((plane + way) % 8) + core))
    return pairs


def phase(*sends):
    values = lax.optimization_barrier(tuple(send[0] for send in sends))
    got = [lax.ppermute(value, *send[1:]) for value, send in zip(values, sends)]
    return lax.optimization_barrier(tuple(got))


def added(*parts):
    return functools.reduce(jnp.add, [p.astype(f32) for p in parts])


def in_order(flag, own, other):
    first = jnp.where(flag == 0, own, other)
    second = jnp.where(flag == 0, other, own)
    return jnp.stack([first, second])


def all_sum(value, axis):
    n = lax.axis_size(axis)
    shares = lax.all_to_all(jnp.full((n, 128), value, f32), axis, 0, 0, tiled=True)
    return jnp.sum(shares[:, 0])


def shards(hidden, norm_gain, cotangent):
    z, yh, core = lax.axis_index(Z), lax.axis_index(YH), lax.axis_index(CORE)
    yl, x = lax.axis_index(YL), lax.axis_index(X)
    k, h = 2 * yl + x // 2, x % 2
    here, width = hidden.shape
    out_width = cotangent.shape[1]
    out_blocks = out_width // TILE
    tokens = here * lax.axis_size(DP)

    def numbers(*values):
        return jnp.stack([jnp.asarray(v, jnp.int32) for v in values])

    pick = call(
        functools.partial(pick_kernel, out_blocks),
        4,
        (here // 4, out_blocks * (HALF + PIECE)),
        (here, out_blocks * (HALF + PIECE)),
        numbers(h, k),
        cotangent,
    )
    recv = lax.ppermute(pick, CORE, SWAP2)

    states = hidden.astype(f32)
    rms = lax.rsqrt(jnp.mean(states * states, axis=1, keepdims=True) + 1e-05)
    gain = lax.dynamic_slice_in_dim(norm_gain, k * TILE, TILE)
    mine = lax.dynamic_slice_in_dim(hidden, k * TILE, TILE, 1)
    normed = (mine.astype(f32) * rms * gain).astype(bf16)
    normed_recv = lax.ppermute(normed, CORE, SWAP2)

    way = 2 * core - 1
    table = []
    for i, away in enumerate(AWAY):
        plane = (z + way * away + 8) % 8
        piece = core if i in (0, 7) else 1 - core if i == 8 else (i + 1) % 2
        table += [plane, 3 * (plane // 4) + plane % 4 - plane % 4 // 2, piece]
    table = numbers(h, yh, *table)

    def slots(kernel, count, block, gives=()):
        tokens_in = (pick, recv, normed, normed_recv)
        more = [(len(slots), *block) for slots in gives]
        return pl.pallas_call(
            kernel,
            grid_spec=pltpu.PrefetchScalarGridSpec(
                num_scalar_prefetch=1,
                grid=(count,),
                in_specs=[pl.BlockSpec(memory_space=pl.ANY) for _ in tokens_in],
                out_specs=[pl.BlockSpec((1, *block), lambda i, at: (i, 0, 0))]
                + [pl.BlockSpec(m, lambda i, at: (0, 0, 0)) for m in more],
                scratch_shapes=[
                    pltpu.VMEM((2 * here, pick.shape[1]), bf16),
                    pltpu.VMEM((2 * here, TILE), bf16),
                    pltpu.SemaphoreType.DMA((4,)),
                ],
            ),
            out_shape=[jax.ShapeDtypeStruct(m, bf16) for m in [(count, *block)] + more],
            compiler_params=PARAMS,
        )(table, *tokens_in)

    (part,) = slots(functools.partial(factor_kernel, out_blocks), 9, (PIECE, PIECE + 128))
    keep, *give = slots(cross_kernel, 8, (128, TILE), GIVE_SLOTS)

    def y_send(i):
        return give[i], YH, SWAP2

    def ring(value, *args):
        return value, (Z, CORE), ring_pairs(*args)

    def widened(got):
        nothing = jnp.zeros_like(got)
        return in_order(core, got, nothing)

    (far,) = phase(ring(part[0]))
    far, y0 = phase(ring(added(part[1:3], widened(far)).astype(bf16)), y_send(0))
    far, y1 = phase(ring(added(part[3:5], far).astype(bf16)), y_send(1))
    far, y2 = phase(ring(added(part[5:7], far).astype(bf16)), y_send(2))
    both_in = jnp.concatenate([far[0, :, PIECE:], far[1, :, PIECE:]], 1)
    out_own = jnp.where(core == 0, far[0, :, :PIECE], far[1, :, :PIECE])
    out_other = jnp.where(core == 0, far[1, :, :PIECE], far[0, :, :PIECE])
    (other,) = phase((jnp.concatenate([out_other, both_in], 1), CORE, SWAP2))
    here_in = in_order(core, part[7, :, PIECE:], part[8, :, PIECE:])
    local = jnp.concatenate([part[7, :, :PIECE], here_in[0], here_in[1]], 1)
    tiles = (added(jnp.concatenate([out_own, both_in], 1), other) + local.astype(f32)).astype(bf16)
    other, far = phase((tiles, YH, SWAP2), ring(added(keep[0], y0[0]).astype(bf16), 4, True))
    tiles = added(tiles, other).astype(bf16)
    out_tile, in_tile = tiles[:, :PIECE], tiles[:, PIECE:]
    copies = jnp.broadcast_to(out_tile[None], (8, PIECE, PIECE))
    out_tiles = lax.all_to_all(copies, OWNER, 0, 0, tiled=True)
    near_in, far, y34 = phase(
        (in_tile, X, SWAP_X),
        ring(added(keep[1:3], jnp.concatenate([y1, y2]), widened(far)).astype(bf16), 3, True),
        y_send(3),
    )
    shard = in_order(h, in_tile, near_in)
    (one,) = phase(ring(shard))
    (two,) = phase(ring(one))
    (three,) = phase(ring(two))
    (last,) = phase(ring(jnp.where(core == 0, three[:1], three[1:])))
    in_own = jnp.concatenate([one, two, three, last], 0)
    cross, in_other, y56 = phase(
        ring(added(keep[3:5], y34, far).astype(bf16), 2, True),
        (in_own, CORE, SWAP2),
        y_send(4),
    )
    square = (TILE, TILE)
    in_inverse = call(
        functools.partial(in_inverse_kernel, tokens),
        4,
        (PIECE, TILE),
        square,
        numbers(z, core),
        shard,
        in_own,
        in_other,
        scratch=[(square, bf16), (square, f32), (square, bf16)],
    )
    cross, out_other, y7 = phase(
        ring(added(keep[5:7], y56, cross).astype(bf16), 1, True),
        (out_tiles, CORE, SWAP2),
        y_send(5),
    )
    cross, in_inverse = lax.optimization_barrier((cross, in_inverse))
    (other,) = phase((jnp.where(core == 0, cross[1], cross[0]), CORE, SWAP2))
    cross = added(jnp.where(core == 0, cross[0], cross[1]), other, keep[7], y7[0]).astype(bf16)
    m = z % 4
    row = 2 * yh + core
    slice_rows = out_width // lax.axis_size(DP)
    base = TILE * (m - m // 2)
    near = jnp.where(m == 3, 2, m + 1)
    own_at = jnp.where(m == 2, TILE, slice_rows * (4 * m + row) - base)
    near_at = jnp.where(m == 2, TILE, slice_rows * (4 * near + row) - base)
    own_at, near_at = [jnp.clip(a, -slice_rows, TILE) + slice_rows for a in (own_at, near_at)]
    out_inverse = call(
        functools.partial(out_inverse_kernel, tokens, slice_rows),
        2,
        (slice_rows, TILE),
        (2 * slice_rows, TILE),
        numbers(core, own_at, near_at),
        out_tiles,
        out_other,
        scratch=[(square, bf16), ((TILE + 2 * slice_rows, TILE), f32), (square, bf16)],
    )

    middle = mdot(cross, in_inverse).astype(bf16)
    mine = lax.dynamic_slice_in_dim(middle, h * HALF, HALF, 1)
    theirs = lax.dynamic_slice_in_dim(middle, (1 - h) * HALF, HALF, 1)
    near_x, near_y, near_xy = phase(
        (theirs, X, SWAP_X), (mine, YH, SWAP2), (theirs, (YH, X), SWAP_BOTH)
    )
    middle = in_order(h, in_order(yh, mine, near_y), in_order(yh, near_x, near_xy))
    other = lax.ppermute(middle, CORE, SWAP2)
    middle = jnp.moveaxis(in_order(core, middle, other), 0, 1).reshape(TILE, HALF)
    result = mdot(out_inverse, middle)

    near_part = result[slice_rows:].astype(bf16)
    up = lax.ppermute(near_part, Z, [(0, 1), (1, 2), (4, 5), (5, 6)])
    down = lax.ppermute(near_part, Z, [(3, 2), (7, 6)])
    squares = all_sum(all_sum(jnp.sum(result * result), OWNER), DP)
    summed = result[:slice_rows] + up.astype(f32) + down.astype(f32)
    return (summed * lax.rsqrt(squares / (width * out_width) + 1e-06)).astype(bf16)


def solution(mesh):
    split = Mesh(mesh.devices.reshape(8, 2, 2, 2, 4), DP + OWNER)
    return jax.shard_map(
        shards,
        mesh=split,
        in_specs=(P(DP, None), P(), P(DP, None)),
        out_specs=P(DP, OWNER),
        check_vma=False,
    )
```

```python
import functools

import jax
import jax.numpy as jnp
from jax import lax
from jax.experimental import pallas as pl
from jax.experimental.pallas import tpu as pltpu
from jax.sharding import Mesh
from jax.sharding import PartitionSpec as P

TILE = 1024
PIECE = 256
HALF = 512
Z, YH, CORE, YL, X = "dp_0", "dp_1", "dp_2", "owner_0", "owner_1"
DP = (Z, YH, CORE)
OWNER = (YL, X)
DAMPING = 0.1
bf16, f32 = jnp.bfloat16, jnp.float32
PARAMS = pltpu.CompilerParams(vmem_limit_bytes=48 * 1024 * 1024)

AWAY = (4, 3, 3, 2, 2, 1, 1, 0, 0)
SWAP2 = [(0, 1), (1, 0)]
SWAP_X = [(0, 1), (1, 0), (2, 3), (3, 2)]
SWAP_BOTH = [(4 * a + b, 4 * (1 - a) + (b ^ 1)) for a in range(2) for b in range(4)]


def tdot(a, b):
    return lax.dot_general(a, b, (((0,), (0,)), ((), ())), preferred_element_type=f32)


def mdot(a, b):
    return jnp.dot(a, b, preferred_element_type=f32)


def aligned(start, size):
    return pl.ds(pl.multiple_of(start, size), size)


def pick_kernel(out_blocks, at_ref, cot_ref, pick_ref):
    h, k = at_ref[0], at_ref[1]
    rows = pl.ds(pl.multiple_of(pl.program_id(0) * pick_ref.shape[0], 8), pick_ref.shape[0])
    for j in range(out_blocks):
        here = slice(j * HALF, (j + 1) * HALF)
        there = slice(out_blocks * HALF + j * PIECE, out_blocks * HALF + (j + 1) * PIECE)
        pick_ref[:, here] = cot_ref[rows, aligned(j * TILE + h * HALF, HALF)]
        pick_ref[:, there] = cot_ref[rows, aligned(j * TILE + k * PIECE, PIECE)]


def load_tokens(pick_ref, recv_ref, own_ref, got_ref, out_ref, in_ref, sems):
    count = pick_ref.shape[0]
    copies = [
        pltpu.make_async_copy(src, dst.at[pl.ds(start, count)], sems.at[n])
        for n, (src, dst, start) in enumerate(
            (
                (pick_ref, out_ref, 0),
                (recv_ref, out_ref, count),
                (own_ref, in_ref, 0),
                (got_ref, in_ref, count),
            )
        )
    ]
    for copy in copies:
        copy.start()
    for copy in copies:
        copy.wait()


def factor_kernel(out_blocks, at_ref, pick_ref, recv_ref, own_ref, got_ref, part_ref, out_ref, in_ref, sems):
    i = pl.program_id(0)

    @pl.when(i == 0)
    def _():
        load_tokens(pick_ref, recv_ref, own_ref, got_ref, out_ref, in_ref, sems)

    h, plane, block, piece = at_ref[0], at_ref[1 + 3 * i], at_ref[2 + 3 * i], at_ref[3 + 3 * i]
    left = out_ref[:, aligned(block * HALF + piece * PIECE, PIECE)]
    right = out_ref[:, aligned(out_blocks * HALF + block * PIECE, PIECE)]
    part_ref[0, :, :PIECE] = tdot(left, right).astype(bf16)
    rows = in_ref[:, aligned((2 * h + piece) * PIECE, PIECE)]
    part_ref[0, :, PIECE:] = tdot(rows, in_ref[:, aligned(plane * 128, 128)]).astype(bf16)


def cross_kernel(at_ref, pick_ref, recv_ref, own_ref, got_ref, cross_ref, out_ref, in_ref, sems):
    i = pl.program_id(0)

    @pl.when(i == 0)
    def _():
        load_tokens(pick_ref, recv_ref, own_ref, got_ref, out_ref, in_ref, sems)

    block, piece = at_ref[2 + 3 * i], at_ref[3 + 3 * i]
    rows = out_ref[:, aligned(block * HALF + piece * PIECE, PIECE)]
    cross_ref[0] = tdot(rows, in_ref[...]).astype(bf16)


def scale_of(tokens, sums_ref):
    largest = jnp.zeros((), f32)
    for r in range(4):
        rows = matrix_rows(tokens, sums_ref, r * PIECE)
        largest = jnp.maximum(largest, jnp.max(jnp.sum(jnp.abs(rows), axis=1)))
    return 1.0 / largest


def eye_rows(start, count):
    row = lax.broadcasted_iota(jnp.int32, (count, TILE), 0) + start
    return (row == lax.broadcasted_iota(jnp.int32, (count, TILE), 1)).astype(f32)


def matrix_rows(tokens, sums_ref, start):
    return sums_ref[start : start + PIECE, :].astype(f32) / tokens + DAMPING * eye_rows(start, PIECE)


def split_factor(tokens, sums_ref, first_ref, low_ref, offset):
    scale = scale_of(tokens, sums_ref)
    for r in range(4):
        here = slice(r * PIECE, (r + 1) * PIECE)
        rows = matrix_rows(tokens, sums_ref, r * PIECE)
        first = 2.0 * scale * eye_rows(r * PIECE, PIECE) - (scale * scale) * rows
        first_ref[offset + r * PIECE : offset + (r + 1) * PIECE, :] = first
        low_ref[here, :] = first.astype(bf16)
        sums_ref[here, :] = rows.astype(bf16)


def inverse_rows(rows, sums_ref, low_ref):
    product = mdot(rows.astype(bf16), sums_ref[...]).astype(bf16)
    return (2.0 * rows - mdot(product, low_ref[...])).astype(bf16)


def in_inverse_kernel(
    tokens, at_ref, shard_ref, own_ref, other_ref,
    out_ref, sums_ref, first_ref, low_ref,
):
    i = pl.program_id(0)

    @pl.when(i == 0)
    def _():
        z, core = at_ref[0], at_ref[1]
        back = 1 - 2 * core

        def put(h, away, value):
            here = aligned((z + away + 8) % 8 * 128, 128)
            for piece in range(2):
                rows = aligned((2 * h + piece) * PIECE, PIECE)
                sums_ref[rows, here] = value[:, piece * 128 : (piece + 1) * 128]

        for h in range(2):
            put(h, 0, shard_ref[h])
            for d in (1, 2, 3):
                put(h, back * d, own_ref[2 * (d - 1) + h])
                put(h, -back * d, other_ref[2 * (d - 1) + h])
        put(core, 4, own_ref[6])
        put(1 - core, 4, other_ref[6])
        split_factor(tokens, sums_ref, first_ref, low_ref, 0)

    out_ref[...] = inverse_rows(first_ref[aligned(i * PIECE, PIECE), :], sums_ref, low_ref)


def out_inverse_kernel(tokens, count, at_ref, own_ref, other_ref, out_ref, sums_ref, first_ref, low_ref):
    i = pl.program_id(0)

    @pl.when(i == 0)
    def _():
        core = at_ref[0]
        for owner in range(8):
            here = slice(owner // 2 * PIECE, (owner // 2 + 1) * PIECE)
            for piece, ref in ((core, own_ref), (1 - core, other_ref)):
                sums_ref[aligned((2 * (owner % 2) + piece) * PIECE, PIECE), here] = ref[owner]
        first_ref[:count, :] = jnp.zeros((count, TILE), f32)
        first_ref[count + TILE :, :] = jnp.zeros((count, TILE), f32)
        split_factor(tokens, sums_ref, first_ref, low_ref, count)

    rows = first_ref[pl.ds(pl.multiple_of(at_ref[1 + i], 64), count), :]
    out_ref[...] = inverse_rows(rows, sums_ref, low_ref)


def call(kernel, steps, block, out_shape, at, *args, scratch=()):
    def whole(a):
        return pl.BlockSpec(a.shape, lambda i, at: (0,) * len(a.shape))

    return pl.pallas_call(
        kernel,
        grid_spec=pltpu.PrefetchScalarGridSpec(
            num_scalar_prefetch=1,
            grid=(steps,),
            in_specs=[whole(a) for a in args],
            out_specs=pl.BlockSpec(block, lambda i, at: (i, 0)),
            scratch_shapes=[pltpu.VMEM(shape, dtype) for shape, dtype in scratch],
        ),
        out_shape=jax.ShapeDtypeStruct(out_shape, bf16),
        compiler_params=PARAMS,
    )(at, *args)


def ring_pairs(away=0, skip=False):
    pairs = []
    for plane in range(8):
        for core, way in ((0, -1), (1, 1)):
            if not skip or (plane + way * away) % 4 != 2:
                pairs.append((2 * plane + core, 2 * ((plane + way) % 8) + core))
    return pairs


def phase(*sends):
    values = lax.optimization_barrier(tuple(send[0] for send in sends))
    got = [lax.ppermute(value, *send[1:]) for value, send in zip(values, sends)]
    return lax.optimization_barrier(tuple(got))


def added(*parts):
    return functools.reduce(jnp.add, [p.astype(f32) for p in parts])


def in_order(flag, own, other):
    first = jnp.where(flag == 0, own, other)
    second = jnp.where(flag == 0, other, own)
    return jnp.stack([first, second])


def all_sum(value, axis):
    n = lax.axis_size(axis)
    shares = lax.all_to_all(jnp.full((n, 128), value, f32), axis, 0, 0, tiled=True)
    return jnp.sum(shares[:, 0])


def shards(hidden, norm_gain, cotangent):
    z, yh, core = lax.axis_index(Z), lax.axis_index(YH), lax.axis_index(CORE)
    yl, x = lax.axis_index(YL), lax.axis_index(X)
    k, h = 2 * yl + x // 2, x % 2
    here, width = hidden.shape
    out_width = cotangent.shape[1]
    out_blocks = out_width // TILE
    tokens = here * lax.axis_size(DP)

    def numbers(*values):
        return jnp.stack([jnp.asarray(v, jnp.int32) for v in values])

    pick = call(
        functools.partial(pick_kernel, out_blocks),
        4,
        (here // 4, out_blocks * (HALF + PIECE)),
        (here, out_blocks * (HALF + PIECE)),
        numbers(h, k),
        cotangent,
    )
    recv = lax.ppermute(pick, CORE, SWAP2)

    states = hidden.astype(f32)
    rms = lax.rsqrt(jnp.mean(states * states, axis=1, keepdims=True) + 1e-05)
    gain = lax.dynamic_slice_in_dim(norm_gain, k * TILE, TILE)
    mine = lax.dynamic_slice_in_dim(hidden, k * TILE, TILE, 1)
    normed = (mine.astype(f32) * rms * gain).astype(bf16)
    normed_recv = lax.ppermute(normed, CORE, SWAP2)

    way = 2 * core - 1
    table = []
    for i, away in enumerate(AWAY):
        plane = (z + way * away + 8) % 8
        piece = core if i in (0, 7) else 1 - core if i == 8 else (i + 1) % 2
        table += [plane, 3 * (plane // 4) + plane % 4 - plane % 4 // 2, piece]
    table = numbers(h, *table)

    def slots(kernel, count, block):
        tokens_in = (pick, recv, normed, normed_recv)
        return pl.pallas_call(
            kernel,
            grid_spec=pltpu.PrefetchScalarGridSpec(
                num_scalar_prefetch=1,
                grid=(count,),
                in_specs=[pl.BlockSpec(memory_space=pl.ANY) for _ in tokens_in],
                out_specs=pl.BlockSpec((1, *block), lambda i, at: (i, 0, 0)),
                scratch_shapes=[
                    pltpu.VMEM((2 * here, pick.shape[1]), bf16),
                    pltpu.VMEM((2 * here, TILE), bf16),
                    pltpu.SemaphoreType.DMA((4,)),
                ],
            ),
            out_shape=jax.ShapeDtypeStruct((count, *block), bf16),
            compiler_params=PARAMS,
        )(table, *tokens_in)

    part = slots(functools.partial(factor_kernel, out_blocks), 9, (PIECE, PIECE + 128))
    keep = slots(cross_kernel, 8, (PIECE, TILE))

    def ring(value, *args):
        return value, (Z, CORE), ring_pairs(*args)

    def widened(got):
        nothing = jnp.zeros_like(got)
        return in_order(core, got, nothing)

    (far,) = phase(ring(part[0]))
    (far,) = phase(ring(added(part[1:3], widened(far)).astype(bf16)))
    (far,) = phase(ring(added(part[3:5], far).astype(bf16)))
    (far,) = phase(ring(added(part[5:7], far).astype(bf16)))
    both_in = jnp.concatenate([far[0, :, PIECE:], far[1, :, PIECE:]], 1)
    out_own = jnp.where(core == 0, far[0, :, :PIECE], far[1, :, :PIECE])
    out_other = jnp.where(core == 0, far[1, :, :PIECE], far[0, :, :PIECE])
    (other,) = phase((jnp.concatenate([out_other, both_in], 1), CORE, SWAP2))
    here_in = in_order(core, part[7, :, PIECE:], part[8, :, PIECE:])
    local = jnp.concatenate([part[7, :, :PIECE], here_in[0], here_in[1]], 1)
    tiles = (added(jnp.concatenate([out_own, both_in], 1), other) + local.astype(f32)).astype(bf16)
    other, far = phase((tiles, YH, SWAP2), ring(keep[0], 4, True))
    tiles = added(tiles, other).astype(bf16)
    out_tile, in_tile = tiles[:, :PIECE], tiles[:, PIECE:]
    copies = jnp.broadcast_to(out_tile[None], (8, PIECE, PIECE))
    in_tile, copies = lax.optimization_barrier((in_tile, copies))
    near_in, far = phase(
        (in_tile, X, SWAP_X),
        ring(added(keep[1:3], widened(far)).astype(bf16), 3, True),
    )
    out_tiles = lax.all_to_all(copies, OWNER, 0, 0, tiled=True)
    near_in, far, out_tiles = lax.optimization_barrier((near_in, far, out_tiles))
    shard = in_order(h, in_tile, near_in)
    (one,) = phase(ring(shard))
    (two,) = phase(ring(one))
    (three,) = phase(ring(two))
    (last,) = phase(ring(jnp.where(core == 0, three[:1], three[1:])))
    in_own = jnp.concatenate([one, two, three, last], 0)
    cross, in_other = phase(
        ring(added(keep[3:5], far).astype(bf16), 2, True), (in_own, CORE, SWAP2)
    )
    square = (TILE, TILE)
    in_inverse = call(
        functools.partial(in_inverse_kernel, tokens),
        4,
        (PIECE, TILE),
        square,
        numbers(z, core),
        shard,
        in_own,
        in_other,
        scratch=[(square, bf16), (square, f32), (square, bf16)],
    )
    cross, out_other = phase(
        ring(added(keep[5:7], cross).astype(bf16), 1, True), (out_tiles, CORE, SWAP2)
    )
    cross, in_inverse = lax.optimization_barrier((cross, in_inverse))
    (other,) = phase((jnp.where(core == 0, cross[1], cross[0]), CORE, SWAP2))
    cross = added(jnp.where(core == 0, cross[0], cross[1]), other, keep[7])
    give = lax.dynamic_slice_in_dim(cross, (1 - yh) * 128, 128, 0).astype(bf16)
    (other,) = phase((give, YH, SWAP2))
    cross = added(lax.dynamic_slice_in_dim(cross, yh * 128, 128, 0), other).astype(bf16)
    m = z % 4
    row = 2 * yh + core
    slice_rows = out_width // lax.axis_size(DP)
    base = TILE * (m - m // 2)
    near = jnp.where(m == 3, 2, m + 1)
    own_at = jnp.where(m == 2, TILE, slice_rows * (4 * m + row) - base)
    near_at = jnp.where(m == 2, TILE, slice_rows * (4 * near + row) - base)
    own_at, near_at = [jnp.clip(a, -slice_rows, TILE) + slice_rows for a in (own_at, near_at)]
    out_inverse = call(
        functools.partial(out_inverse_kernel, tokens, slice_rows),
        2,
        (slice_rows, TILE),
        (2 * slice_rows, TILE),
        numbers(core, own_at, near_at),
        out_tiles,
        out_other,
        scratch=[(square, bf16), ((TILE + 2 * slice_rows, TILE), f32), (square, bf16)],
    )

    middle = mdot(cross, in_inverse).astype(bf16)
    mine = lax.dynamic_slice_in_dim(middle, h * HALF, HALF, 1)
    theirs = lax.dynamic_slice_in_dim(middle, (1 - h) * HALF, HALF, 1)
    near_x, near_y, near_xy = phase(
        (theirs, X, SWAP_X), (mine, YH, SWAP2), (theirs, (YH, X), SWAP_BOTH)
    )
    middle = in_order(h, in_order(yh, mine, near_y), in_order(yh, near_x, near_xy))
    other = lax.ppermute(middle, CORE, SWAP2)
    middle = jnp.moveaxis(in_order(core, middle, other), 0, 1).reshape(TILE, HALF)
    result = mdot(out_inverse, middle)

    near_part = result[slice_rows:].astype(bf16)
    up = lax.ppermute(near_part, Z, [(0, 1), (1, 2), (4, 5), (5, 6)])
    down = lax.ppermute(near_part, Z, [(3, 2), (7, 6)])
    squares = all_sum(all_sum(jnp.sum(result * result), OWNER), DP)
    summed = result[:slice_rows] + up.astype(f32) + down.astype(f32)
    return (summed * lax.rsqrt(squares / (width * out_width) + 1e-06)).astype(bf16)


def solution(mesh):
    split = Mesh(mesh.devices.reshape(8, 2, 2, 2, 4), DP + OWNER)
    return jax.shard_map(
        shards,
        mesh=split,
        in_specs=(P(DP, None), P(), P(DP, None)),
        out_specs=P(DP, OWNER),
        check_vma=False,
    )
```

```python
import functools

import jax
import jax.numpy as jnp
from jax import lax
from jax.experimental import pallas as pl
from jax.experimental.pallas import tpu as pltpu
from jax.sharding import Mesh
from jax.sharding import PartitionSpec as P

TILE = 1024
PIECE = 256
HALF = 512
Z, YH, CORE, YL, X = "dp_0", "dp_1", "dp_2", "owner_0", "owner_1"
DP = (Z, YH, CORE)
OWNER = (YL, X)
DAMPING = 0.1
bf16, f32 = jnp.bfloat16, jnp.float32
PARAMS = pltpu.CompilerParams(vmem_limit_bytes=48 * 1024 * 1024)

AWAY = (4, 3, 3, 2, 2, 1, 1, 0, 0)
SWAP2 = [(0, 1), (1, 0)]
SWAP_X = [(0, 1), (1, 0), (2, 3), (3, 2)]
SWAP_BOTH = [(4 * a + b, 4 * (1 - a) + (b ^ 1)) for a in range(2) for b in range(4)]


def tdot(a, b):
    return lax.dot_general(a, b, (((0,), (0,)), ((), ())), preferred_element_type=f32)


def mdot(a, b):
    return jnp.dot(a, b, preferred_element_type=f32)


def aligned(start, size):
    return pl.ds(pl.multiple_of(start, size), size)


def pick_kernel(out_blocks, at_ref, cot_ref, pick_ref):
    h, k = at_ref[0], at_ref[1]
    rows = pl.ds(pl.multiple_of(pl.program_id(0) * pick_ref.shape[0], 8), pick_ref.shape[0])
    for j in range(out_blocks):
        here = slice(j * HALF, (j + 1) * HALF)
        there = slice(out_blocks * HALF + j * PIECE, out_blocks * HALF + (j + 1) * PIECE)
        pick_ref[:, here] = cot_ref[rows, aligned(j * TILE + h * HALF, HALF)]
        pick_ref[:, there] = cot_ref[rows, aligned(j * TILE + k * PIECE, PIECE)]


def load_tokens(pick_ref, recv_ref, own_ref, got_ref, out_ref, in_ref, sems):
    count = pick_ref.shape[0]
    copies = [
        pltpu.make_async_copy(src, dst.at[pl.ds(start, count)], sems.at[n])
        for n, (src, dst, start) in enumerate(
            (
                (pick_ref, out_ref, 0),
                (recv_ref, out_ref, count),
                (own_ref, in_ref, 0),
                (got_ref, in_ref, count),
            )
        )
    ]
    for copy in copies:
        copy.start()
    for copy in copies:
        copy.wait()


def factor_kernel(out_blocks, at_ref, pick_ref, recv_ref, own_ref, got_ref, part_ref, out_ref, in_ref, sems):
    i = pl.program_id(0)

    @pl.when(i == 0)
    def _():
        load_tokens(pick_ref, recv_ref, own_ref, got_ref, out_ref, in_ref, sems)

    h, plane, block, piece = at_ref[0], at_ref[1 + 3 * i], at_ref[2 + 3 * i], at_ref[3 + 3 * i]
    left = out_ref[:, aligned(block * HALF + piece * PIECE, PIECE)]
    right = out_ref[:, aligned(out_blocks * HALF + block * PIECE, PIECE)]
    part_ref[0, :, :PIECE] = tdot(left, right).astype(bf16)
    rows = in_ref[:, aligned((2 * h + piece) * PIECE, PIECE)]
    part_ref[0, :, PIECE:] = tdot(rows, in_ref[:, aligned(plane * 128, 128)]).astype(bf16)


def cross_kernel(base, at_ref, pick_ref, recv_ref, own_ref, got_ref, cross_ref, out_ref, in_ref, sems):
    i = pl.program_id(0)

    @pl.when(i == 0)
    def _():
        load_tokens(pick_ref, recv_ref, own_ref, got_ref, out_ref, in_ref, sems)

    block, piece = at_ref[2 + 3 * (base + i)], at_ref[3 + 3 * (base + i)]
    rows = out_ref[:, aligned(block * HALF + piece * PIECE, PIECE)]
    cross_ref[0] = tdot(rows, in_ref[...]).astype(bf16)


def scale_of(tokens, sums_ref):
    largest = jnp.zeros((), f32)
    for r in range(4):
        rows = matrix_rows(tokens, sums_ref, r * PIECE)
        largest = jnp.maximum(largest, jnp.max(jnp.sum(jnp.abs(rows), axis=1)))
    return 1.0 / largest


def eye_rows(start, count):
    row = lax.broadcasted_iota(jnp.int32, (count, TILE), 0) + start
    return (row == lax.broadcasted_iota(jnp.int32, (count, TILE), 1)).astype(f32)


def matrix_rows(tokens, sums_ref, start):
    return sums_ref[start : start + PIECE, :].astype(f32) / tokens + DAMPING * eye_rows(start, PIECE)


def split_factor(tokens, sums_ref, first_ref, low_ref, offset):
    scale = scale_of(tokens, sums_ref)
    for r in range(4):
        here = slice(r * PIECE, (r + 1) * PIECE)
        rows = matrix_rows(tokens, sums_ref, r * PIECE)
        first = 2.0 * scale * eye_rows(r * PIECE, PIECE) - (scale * scale) * rows
        first_ref[offset + r * PIECE : offset + (r + 1) * PIECE, :] = first
        low_ref[here, :] = first.astype(bf16)
        sums_ref[here, :] = rows.astype(bf16)


def inverse_rows(rows, sums_ref, low_ref):
    product = mdot(rows.astype(bf16), sums_ref[...]).astype(bf16)
    return (2.0 * rows - mdot(product, low_ref[...])).astype(bf16)


def in_inverse_kernel(
    tokens, at_ref, shard_ref, own_ref, other_ref,
    out_ref, sums_ref, first_ref, low_ref,
):
    i = pl.program_id(0)

    @pl.when(i == 0)
    def _():
        z, core = at_ref[0], at_ref[1]
        back = 1 - 2 * core

        def put(h, away, value):
            here = aligned((z + away + 8) % 8 * 128, 128)
            for piece in range(2):
                rows = aligned((2 * h + piece) * PIECE, PIECE)
                sums_ref[rows, here] = value[:, piece * 128 : (piece + 1) * 128]

        for h in range(2):
            put(h, 0, shard_ref[h])
            for d in (1, 2, 3):
                put(h, back * d, own_ref[2 * (d - 1) + h])
                put(h, -back * d, other_ref[2 * (d - 1) + h])
        put(core, 4, own_ref[6])
        put(1 - core, 4, other_ref[6])
        split_factor(tokens, sums_ref, first_ref, low_ref, 0)

    out_ref[...] = inverse_rows(first_ref[aligned(i * PIECE, PIECE), :], sums_ref, low_ref)


def out_inverse_kernel(tokens, at_ref, own_ref, other_ref, out_ref, sums_ref, first_ref, low_ref):
    i = pl.program_id(0)

    @pl.when(i == 0)
    def _():
        core = at_ref[0]
        for owner in range(8):
            here = slice(owner // 2 * PIECE, (owner // 2 + 1) * PIECE)
            for piece, ref in ((core, own_ref), (1 - core, other_ref)):
                sums_ref[aligned((2 * (owner % 2) + piece) * PIECE, PIECE), here] = ref[owner]
        split_factor(tokens, sums_ref, first_ref, low_ref, 0)

    outside = jnp.logical_or(i == 0, i == 5)

    @pl.when(outside)
    def _():
        out_ref[...] = jnp.zeros_like(out_ref)

    @pl.when(jnp.logical_not(outside))
    def _():
        out_ref[...] = inverse_rows(first_ref[aligned((i - 1) * PIECE, PIECE), :], sums_ref, low_ref)


def call(kernel, steps, block, out_shape, at, *args, scratch=()):
    def whole(a):
        return pl.BlockSpec(a.shape, lambda i, at: (0,) * len(a.shape))

    return pl.pallas_call(
        kernel,
        grid_spec=pltpu.PrefetchScalarGridSpec(
            num_scalar_prefetch=1,
            grid=(steps,),
            in_specs=[whole(a) for a in args],
            out_specs=pl.BlockSpec(block, lambda i, at: (i, 0)),
            scratch_shapes=[pltpu.VMEM(shape, dtype) for shape, dtype in scratch],
        ),
        out_shape=jax.ShapeDtypeStruct(out_shape, bf16),
        compiler_params=PARAMS,
    )(at, *args)


def join_kernel(at_ref, own_ref, other_ref, here_ref, give_ref, keep_ref):
    total = added(own_ref[0], other_ref[0], here_ref[0]).astype(bf16)

    @pl.when(pl.program_id(0) == 0)
    def _():
        give_ref[...] = total

    @pl.when(pl.program_id(0) == 1)
    def _():
        keep_ref[...] = total


def join(at, own, other, here):
    block = (1, 128, TILE)
    rows = (128, TILE)
    piece = pl.BlockSpec(block, lambda i, at: (at[0], (1 - at[1]) ^ i, 0))
    last = pl.BlockSpec(block, lambda i, at: (here.shape[0] - 1, (1 - at[1]) ^ i, 0))
    return pl.pallas_call(
        join_kernel,
        grid_spec=pltpu.PrefetchScalarGridSpec(
            num_scalar_prefetch=1,
            grid=(2,),
            in_specs=[piece, piece, last],
            out_specs=[pl.BlockSpec(rows, lambda i, at: (0, 0))] * 2,
        ),
        out_shape=[jax.ShapeDtypeStruct(rows, bf16)] * 2,
        compiler_params=PARAMS,
    )(at, own, other, here)


def ring_pairs(away=0, skip=False):
    pairs = []
    for plane in range(8):
        for core, way in ((0, -1), (1, 1)):
            if not skip or (plane + way * away) % 4 != 2:
                pairs.append((2 * plane + core, 2 * ((plane + way) % 8) + core))
    return pairs


def phase(*sends):
    values = lax.optimization_barrier(tuple(send[0] for send in sends))
    got = [lax.ppermute(value, *send[1:]) for value, send in zip(values, sends)]
    return lax.optimization_barrier(tuple(got))


def added(*parts):
    return functools.reduce(jnp.add, [p.astype(f32) for p in parts])


def in_order(flag, own, other):
    first = jnp.where(flag == 0, own, other)
    second = jnp.where(flag == 0, other, own)
    return jnp.stack([first, second])


def all_sum(value, axis):
    n = lax.axis_size(axis)
    shares = lax.all_to_all(jnp.full((n, 128), value, f32), axis, 0, 0, tiled=True)
    return jnp.sum(shares[:, 0])


def shards(hidden, norm_gain, cotangent):
    z, yh, core = lax.axis_index(Z), lax.axis_index(YH), lax.axis_index(CORE)
    yl, x = lax.axis_index(YL), lax.axis_index(X)
    k, h = 2 * yl + x // 2, x % 2
    here, width = hidden.shape
    out_width = cotangent.shape[1]
    out_blocks = out_width // TILE
    tokens = here * lax.axis_size(DP)

    def numbers(*values):
        return jnp.stack([jnp.asarray(v, jnp.int32) for v in values])

    pick = call(
        functools.partial(pick_kernel, out_blocks),
        4,
        (here // 4, out_blocks * (HALF + PIECE)),
        (here, out_blocks * (HALF + PIECE)),
        numbers(h, k),
        cotangent,
    )
    recv = lax.ppermute(pick, CORE, SWAP2)

    states = hidden.astype(f32)
    rms = lax.rsqrt(jnp.mean(states * states, axis=1, keepdims=True) + 1e-05)
    gain = lax.dynamic_slice_in_dim(norm_gain, k * TILE, TILE)
    mine = lax.dynamic_slice_in_dim(hidden, k * TILE, TILE, 1)
    normed = (mine.astype(f32) * rms * gain).astype(bf16)
    normed_recv = lax.ppermute(normed, CORE, SWAP2)

    way = 2 * core - 1
    table = []
    for i, away in enumerate(AWAY):
        plane = (z + way * away + 8) % 8
        piece = core if i in (0, 7) else 1 - core if i == 8 else (i + 1) % 2
        table += [plane, 3 * (plane // 4) + plane % 4 - plane % 4 // 2, piece]
    table = numbers(h, *table)

    def slots(kernel, count, block):
        tokens_in = (pick, recv, normed, normed_recv)
        return pl.pallas_call(
            kernel,
            grid_spec=pltpu.PrefetchScalarGridSpec(
                num_scalar_prefetch=1,
                grid=(count,),
                in_specs=[pl.BlockSpec(memory_space=pl.ANY) for _ in tokens_in],
                out_specs=pl.BlockSpec((1, *block), lambda i, at: (i, 0, 0)),
                scratch_shapes=[
                    pltpu.VMEM((2 * here, pick.shape[1]), bf16),
                    pltpu.VMEM((2 * here, TILE), bf16),
                    pltpu.SemaphoreType.DMA((4,)),
                ],
            ),
            out_shape=jax.ShapeDtypeStruct((count, *block), bf16),
            compiler_params=PARAMS,
        )(table, *tokens_in)

    part = slots(functools.partial(factor_kernel, out_blocks), 9, (PIECE, PIECE + 128))
    first_cross = slots(functools.partial(cross_kernel, 0), 3, (PIECE, TILE))
    last_cross = slots(functools.partial(cross_kernel, 3), 5, (PIECE, TILE))

    def ring(value, *args):
        return value, (Z, CORE), ring_pairs(*args)

    def widened(got):
        nothing = jnp.zeros_like(got)
        return in_order(core, got, nothing)

    (far,) = phase(ring(part[0]))
    (far,) = phase(ring(added(part[1:3], widened(far)).astype(bf16)))
    far, first_cross = lax.optimization_barrier((far, first_cross))
    (far,) = phase(ring(added(part[3:5], far).astype(bf16)))
    (far,) = phase(ring(added(part[5:7], far).astype(bf16)))
    far, last_cross = lax.optimization_barrier((far, last_cross))
    both_in = jnp.concatenate([far[0, :, PIECE:], far[1, :, PIECE:]], 1)
    out_own = jnp.where(core == 0, far[0, :, :PIECE], far[1, :, :PIECE])
    out_other = jnp.where(core == 0, far[1, :, :PIECE], far[0, :, :PIECE])
    (other,) = phase((jnp.concatenate([out_other, both_in], 1), CORE, SWAP2))
    here_in = in_order(core, part[7, :, PIECE:], part[8, :, PIECE:])
    local = jnp.concatenate([part[7, :, :PIECE], here_in[0], here_in[1]], 1)
    tiles = (added(jnp.concatenate([out_own, both_in], 1), other) + local.astype(f32)).astype(bf16)
    other, far = phase((tiles, YH, SWAP2), ring(first_cross[0], 4, True))
    tiles = added(tiles, other).astype(bf16)
    out_tile, in_tile = tiles[:, :PIECE], tiles[:, PIECE:]
    copies = jnp.broadcast_to(out_tile[None], (8, PIECE, PIECE))
    (near_in,) = phase((in_tile, X, SWAP_X))
    shard = in_order(h, in_tile, near_in)
    shard, copies = lax.optimization_barrier((shard, copies))
    one, far = phase(
        ring(shard), ring(added(first_cross[1:3], widened(far)).astype(bf16), 3, True)
    )
    out_tiles = lax.all_to_all(copies, OWNER, 0, 0, tiled=True)
    one, far, out_tiles = lax.optimization_barrier((one, far, out_tiles))
    (two,) = phase(ring(one))
    (three,) = phase(ring(two))
    (last,) = phase(ring(jnp.where(core == 0, three[:1], three[1:])))
    in_own = jnp.concatenate([one, two, three, last], 0)
    cross, in_other = phase(
        ring(added(last_cross[0:2], far).astype(bf16), 2, True), (in_own, CORE, SWAP2)
    )
    square = (TILE, TILE)
    in_inverse = call(
        functools.partial(in_inverse_kernel, tokens),
        4,
        (PIECE, TILE),
        square,
        numbers(z, core),
        shard,
        in_own,
        in_other,
        scratch=[(square, bf16), (square, f32), (square, bf16)],
    )
    (cross,) = phase(ring(added(last_cross[2:4], cross).astype(bf16), 1, True))
    cross, in_inverse = lax.optimization_barrier((cross, in_inverse))
    (other,) = phase((cross, CORE, SWAP2))
    give, keep = join(numbers(core, yh), cross, other, last_cross)
    (other, out_other) = phase((give, YH, SWAP2), (out_tiles, CORE, SWAP2))
    cross = added(keep, other).astype(bf16)
    m = z % 4
    row = 2 * yh + core
    slice_rows = out_width // lax.axis_size(DP)
    base = TILE * (m - m // 2)
    near = jnp.where(m == 3, 2, m + 1)
    own_at = jnp.where(m == 2, TILE, slice_rows * (4 * m + row) - base)
    near_at = jnp.where(m == 2, TILE, slice_rows * (4 * near + row) - base)
    own_at, near_at = [jnp.clip(a, -slice_rows, TILE) + PIECE for a in (own_at, near_at)]
    padded = call(
        functools.partial(out_inverse_kernel, tokens),
        6,
        (PIECE, TILE),
        (6 * PIECE, TILE),
        numbers(core),
        out_tiles,
        out_other,
        scratch=[(square, bf16), (square, f32), (square, bf16)],
    )
    middle = mdot(cross, in_inverse).astype(bf16)
    mine = lax.dynamic_slice_in_dim(middle, h * HALF, HALF, 1)
    theirs = lax.dynamic_slice_in_dim(middle, (1 - h) * HALF, HALF, 1)
    near_x, near_y, near_xy = phase(
        (theirs, X, SWAP_X), (mine, YH, SWAP2), (theirs, (YH, X), SWAP_BOTH)
    )
    middle = in_order(h, in_order(yh, mine, near_y), in_order(yh, near_x, near_xy))
    middle, padded = lax.optimization_barrier((middle, padded))
    other = lax.ppermute(middle, CORE, SWAP2)
    middle = jnp.moveaxis(in_order(core, middle, other), 0, 1).reshape(TILE, HALF)
    out_inverse = jnp.concatenate(
        [lax.dynamic_slice_in_dim(padded, at, slice_rows, 0) for at in (own_at, near_at)], 0
    )
    result = mdot(out_inverse, middle)

    near_part = result[slice_rows:].astype(bf16)
    up = lax.ppermute(near_part, Z, [(0, 1), (1, 2), (4, 5), (5, 6)])
    down = lax.ppermute(near_part, Z, [(3, 2), (7, 6)])
    whole = mdot(padded[PIECE : PIECE + TILE], middle)
    squares = jnp.where(m == 2, 0.0, jnp.sum(whole * whole))
    squares = all_sum(all_sum(squares, OWNER), Z)
    summed = result[:slice_rows] + up.astype(f32) + down.astype(f32)
    return (summed * lax.rsqrt(squares / (width * out_width) + 1e-06)).astype(bf16)


def solution(mesh):
    split = Mesh(mesh.devices.reshape(8, 2, 2, 2, 4), DP + OWNER)
    return jax.shard_map(
        shards,
        mesh=split,
        in_specs=(P(DP, None), P(), P(DP, None)),
        out_specs=P(DP, OWNER),
        check_vma=False,
    )
```

```python
import functools

import jax
import jax.numpy as jnp
from jax import lax
from jax.experimental import pallas as pl
from jax.experimental.pallas import tpu as pltpu
from jax.sharding import Mesh
from jax.sharding import PartitionSpec as P

TILE = 1024
PIECE = 256
HALF = 512
Z, YH, CORE, YL, X = "dp_0", "dp_1", "dp_2", "owner_0", "owner_1"
DP = (Z, YH, CORE)
OWNER = (YL, X)
DAMPING = 0.1
bf16, f32 = jnp.bfloat16, jnp.float32
PARAMS = pltpu.CompilerParams(vmem_limit_bytes=48 * 1024 * 1024)

AWAY = (4, 3, 3, 2, 2, 1, 1, 0, 0)
SWAP2 = [(0, 1), (1, 0)]
SWAP_X = [(0, 1), (1, 0), (2, 3), (3, 2)]
SWAP_BOTH = [(4 * a + b, 4 * (1 - a) + (b ^ 1)) for a in range(2) for b in range(4)]


def tdot(a, b):
    return lax.dot_general(a, b, (((0,), (0,)), ((), ())), preferred_element_type=f32)


def mdot(a, b):
    return jnp.dot(a, b, preferred_element_type=f32)


def aligned(start, size):
    return pl.ds(pl.multiple_of(start, size), size)


def pick_kernel(out_blocks, at_ref, cot_ref, pick_ref):
    h, k = at_ref[0], at_ref[1]
    rows = pl.ds(pl.multiple_of(pl.program_id(0) * pick_ref.shape[0], 8), pick_ref.shape[0])
    for j in range(out_blocks):
        here = slice(j * HALF, (j + 1) * HALF)
        there = slice(out_blocks * HALF + j * PIECE, out_blocks * HALF + (j + 1) * PIECE)
        pick_ref[:, here] = cot_ref[rows, aligned(j * TILE + h * HALF, HALF)]
        pick_ref[:, there] = cot_ref[rows, aligned(j * TILE + k * PIECE, PIECE)]


def load_tokens(pick_ref, recv_ref, own_ref, got_ref, out_ref, in_ref, sems):
    count = pick_ref.shape[0]
    copies = [
        pltpu.make_async_copy(src, dst.at[pl.ds(start, count)], sems.at[n])
        for n, (src, dst, start) in enumerate(
            (
                (pick_ref, out_ref, 0),
                (recv_ref, out_ref, count),
                (own_ref, in_ref, 0),
                (got_ref, in_ref, count),
            )
        )
    ]
    for copy in copies:
        copy.start()
    for copy in copies:
        copy.wait()


def factor_kernel(out_blocks, at_ref, pick_ref, recv_ref, own_ref, got_ref, part_ref, out_ref, in_ref, sems):
    i = pl.program_id(0)

    @pl.when(i == 0)
    def _():
        load_tokens(pick_ref, recv_ref, own_ref, got_ref, out_ref, in_ref, sems)

    h, plane, block, piece = at_ref[0], at_ref[2 + 3 * i], at_ref[3 + 3 * i], at_ref[4 + 3 * i]
    left = out_ref[:, aligned(block * HALF + piece * PIECE, PIECE)]
    right = out_ref[:, aligned(out_blocks * HALF + block * PIECE, PIECE)]
    part_ref[0, :, :PIECE] = tdot(left, right).astype(bf16)
    rows = in_ref[:, aligned((2 * h + piece) * PIECE, PIECE)]
    part_ref[0, :, PIECE:] = tdot(rows, in_ref[:, aligned(plane * 128, 128)]).astype(bf16)


def cross_kernel(base, gives, at_ref, pick_ref, recv_ref, own_ref, got_ref, keep_ref, *refs):
    give_refs, (out_ref, in_ref, sems) = refs[:-3], refs[-3:]
    i = pl.program_id(0)

    @pl.when(i == 0)
    def _():
        load_tokens(pick_ref, recv_ref, own_ref, got_ref, out_ref, in_ref, sems)

    yh, block, piece = at_ref[1], at_ref[3 + 3 * (base + i)], at_ref[4 + 3 * (base + i)]

    def rows_of(side):
        rows = out_ref[:, aligned(block * HALF + piece * PIECE + side * 128, 128)]
        return tdot(rows, in_ref[...]).astype(bf16)

    keep_ref[0] = rows_of(yh)
    give = rows_of(1 - yh)
    for slots, ref in zip(gives, give_refs):
        for n, slot in enumerate(slots):

            @pl.when(i + base == slot)
            def _():
                ref[n] = give


def scale_of(tokens, sums_ref):
    largest = jnp.zeros((), f32)
    for r in range(4):
        rows = matrix_rows(tokens, sums_ref, r * PIECE)
        largest = jnp.maximum(largest, jnp.max(jnp.sum(jnp.abs(rows), axis=1)))
    return 1.0 / largest


def eye_rows(start, count):
    row = lax.broadcasted_iota(jnp.int32, (count, TILE), 0) + start
    return (row == lax.broadcasted_iota(jnp.int32, (count, TILE), 1)).astype(f32)


def matrix_rows(tokens, sums_ref, start):
    return sums_ref[start : start + PIECE, :].astype(f32) / tokens + DAMPING * eye_rows(start, PIECE)


def split_factor(tokens, sums_ref, first_ref, low_ref, offset):
    scale = scale_of(tokens, sums_ref)
    for r in range(4):
        here = slice(r * PIECE, (r + 1) * PIECE)
        rows = matrix_rows(tokens, sums_ref, r * PIECE)
        first = 2.0 * scale * eye_rows(r * PIECE, PIECE) - (scale * scale) * rows
        first_ref[offset + r * PIECE : offset + (r + 1) * PIECE, :] = first
        low_ref[here, :] = first.astype(bf16)
        sums_ref[here, :] = rows.astype(bf16)


def inverse_rows(rows, sums_ref, low_ref):
    product = mdot(rows.astype(bf16), sums_ref[...]).astype(bf16)
    return (2.0 * rows - mdot(product, low_ref[...])).astype(bf16)


def in_inverse_kernel(
    tokens, at_ref, shard_ref, own_ref, other_ref,
    out_ref, sums_ref, first_ref, low_ref,
):
    i = pl.program_id(0)

    @pl.when(i == 0)
    def _():
        z, core = at_ref[0], at_ref[1]
        back = 1 - 2 * core

        def put(h, away, value):
            here = aligned((z + away + 8) % 8 * 128, 128)
            for piece in range(2):
                rows = aligned((2 * h + piece) * PIECE, PIECE)
                sums_ref[rows, here] = value[:, piece * 128 : (piece + 1) * 128]

        for h in range(2):
            put(h, 0, shard_ref[h])
            for d in (1, 2, 3):
                put(h, back * d, own_ref[2 * (d - 1) + h])
                put(h, -back * d, other_ref[2 * (d - 1) + h])
        put(core, 4, own_ref[6])
        put(1 - core, 4, other_ref[6])
        split_factor(tokens, sums_ref, first_ref, low_ref, 0)

    out_ref[...] = inverse_rows(first_ref[aligned(i * PIECE, PIECE), :], sums_ref, low_ref)


def out_inverse_kernel(tokens, at_ref, own_ref, other_ref, out_ref, sums_ref, first_ref, low_ref):
    i = pl.program_id(0)

    @pl.when(i == 0)
    def _():
        core = at_ref[0]
        for owner in range(8):
            here = slice(owner // 2 * PIECE, (owner // 2 + 1) * PIECE)
            for piece, ref in ((core, own_ref), (1 - core, other_ref)):
                sums_ref[aligned((2 * (owner % 2) + piece) * PIECE, PIECE), here] = ref[owner]
        split_factor(tokens, sums_ref, first_ref, low_ref, 0)

    outside = jnp.logical_or(i == 0, i == 5)

    @pl.when(outside)
    def _():
        out_ref[...] = jnp.zeros_like(out_ref)

    @pl.when(jnp.logical_not(outside))
    def _():
        out_ref[...] = inverse_rows(first_ref[aligned((i - 1) * PIECE, PIECE), :], sums_ref, low_ref)


def call(kernel, steps, block, out_shape, at, *args, scratch=()):
    def whole(a):
        return pl.BlockSpec(a.shape, lambda i, at: (0,) * len(a.shape))

    return pl.pallas_call(
        kernel,
        grid_spec=pltpu.PrefetchScalarGridSpec(
            num_scalar_prefetch=1,
            grid=(steps,),
            in_specs=[whole(a) for a in args],
            out_specs=pl.BlockSpec(block, lambda i, at: (i, 0)),
            scratch_shapes=[pltpu.VMEM(shape, dtype) for shape, dtype in scratch],
        ),
        out_shape=jax.ShapeDtypeStruct(out_shape, bf16),
        compiler_params=PARAMS,
    )(at, *args)


def ring_pairs(away=0, skip=False):
    pairs = []
    for plane in range(8):
        for core, way in ((0, -1), (1, 1)):
            if not skip or (plane + way * away) % 4 != 2:
                pairs.append((2 * plane + core, 2 * ((plane + way) % 8) + core))
    return pairs


def phase(*sends):
    values = lax.optimization_barrier(tuple(send[0] for send in sends))
    got = [lax.ppermute(value, *send[1:]) for value, send in zip(values, sends)]
    return lax.optimization_barrier(tuple(got))


def added(*parts):
    return functools.reduce(jnp.add, [p.astype(f32) for p in parts])


def in_order(flag, own, other):
    first = jnp.where(flag == 0, own, other)
    second = jnp.where(flag == 0, other, own)
    return jnp.stack([first, second])


def all_sum(value, axis):
    n = lax.axis_size(axis)
    shares = lax.all_to_all(jnp.full((n, 128), value, f32), axis, 0, 0, tiled=True)
    return jnp.sum(shares[:, 0])


def shards(hidden, norm_gain, cotangent):
    z, yh, core = lax.axis_index(Z), lax.axis_index(YH), lax.axis_index(CORE)
    yl, x = lax.axis_index(YL), lax.axis_index(X)
    k, h = 2 * yl + x // 2, x % 2
    here, width = hidden.shape
    out_width = cotangent.shape[1]
    out_blocks = out_width // TILE
    tokens = here * lax.axis_size(DP)

    def numbers(*values):
        return jnp.stack([jnp.asarray(v, jnp.int32) for v in values])

    pick = call(
        functools.partial(pick_kernel, out_blocks),
        4,
        (here // 4, out_blocks * (HALF + PIECE)),
        (here, out_blocks * (HALF + PIECE)),
        numbers(h, k),
        cotangent,
    )
    recv = lax.ppermute(pick, CORE, SWAP2)

    states = hidden.astype(f32)
    rms = lax.rsqrt(jnp.mean(states * states, axis=1, keepdims=True) + 1e-05)
    gain = lax.dynamic_slice_in_dim(norm_gain, k * TILE, TILE)
    mine = lax.dynamic_slice_in_dim(hidden, k * TILE, TILE, 1)
    normed = (mine.astype(f32) * rms * gain).astype(bf16)
    normed_recv = lax.ppermute(normed, CORE, SWAP2)

    way = 2 * core - 1
    table = []
    for i, away in enumerate(AWAY):
        plane = (z + way * away + 8) % 8
        piece = core if i in (0, 7) else 1 - core if i == 8 else (i + 1) % 2
        table += [plane, 3 * (plane // 4) + plane % 4 - plane % 4 // 2, piece]
    table = numbers(h, yh, *table)

    def slots(kernel, count, block, gives=()):
        tokens_in = (pick, recv, normed, normed_recv)
        more = [(len(slots), *block) for slots in gives]
        return pl.pallas_call(
            kernel,
            grid_spec=pltpu.PrefetchScalarGridSpec(
                num_scalar_prefetch=1,
                grid=(count,),
                in_specs=[pl.BlockSpec(memory_space=pl.ANY) for _ in tokens_in],
                out_specs=[pl.BlockSpec((1, *block), lambda i, at: (i, 0, 0))]
                + [pl.BlockSpec(m, lambda i, at: (0, 0, 0)) for m in more],
                scratch_shapes=[
                    pltpu.VMEM((2 * here, pick.shape[1]), bf16),
                    pltpu.VMEM((2 * here, TILE), bf16),
                    pltpu.SemaphoreType.DMA((4,)),
                ],
            ),
            out_shape=[jax.ShapeDtypeStruct(m, bf16) for m in [(count, *block)] + more],
            compiler_params=PARAMS,
        )(table, *tokens_in)

    def cross_part(base, count, gives):
        return slots(functools.partial(cross_kernel, base, gives), count, (128, TILE), gives)

    (part,) = slots(functools.partial(factor_kernel, out_blocks), 9, (PIECE, PIECE + 128))
    keep_a, give_0, give_1, give_2 = cross_part(0, 3, ((0,), (1,), (2,)))
    keep_b, give_34, give_5, give_6, give_7 = cross_part(3, 5, ((3, 4), (5,), (6,), (7,)))

    def to_other_y(value):
        return value, YH, SWAP2

    def ring(value, *args):
        return value, (Z, CORE), ring_pairs(*args)

    def widened(got):
        nothing = jnp.zeros_like(got)
        return in_order(core, got, nothing)

    (far,) = phase(ring(part[0]))
    far, y0 = phase(ring(added(part[1:3], widened(far)).astype(bf16)), to_other_y(give_0))
    far, y1 = phase(ring(added(part[3:5], far).astype(bf16)), to_other_y(give_1))
    far, y2 = phase(ring(added(part[5:7], far).astype(bf16)), to_other_y(give_2))
    far, keep_b = lax.optimization_barrier((far, keep_b))
    both_in = jnp.concatenate([far[0, :, PIECE:], far[1, :, PIECE:]], 1)
    out_own = jnp.where(core == 0, far[0, :, :PIECE], far[1, :, :PIECE])
    out_other = jnp.where(core == 0, far[1, :, :PIECE], far[0, :, :PIECE])
    (other,) = phase((jnp.concatenate([out_other, both_in], 1), CORE, SWAP2))
    here_in = in_order(core, part[7, :, PIECE:], part[8, :, PIECE:])
    local = jnp.concatenate([part[7, :, :PIECE], here_in[0], here_in[1]], 1)
    tiles = (added(jnp.concatenate([out_own, both_in], 1), other) + local.astype(f32)).astype(bf16)
    other, far = phase((tiles, YH, SWAP2), ring(added(keep_a[0], y0[0]).astype(bf16), 4, True))
    tiles = added(tiles, other).astype(bf16)
    out_tile, in_tile = tiles[:, :PIECE], tiles[:, PIECE:]
    copies = jnp.broadcast_to(out_tile[None], (8, PIECE, PIECE))
    (near_in,) = phase((in_tile, X, SWAP_X))
    shard = in_order(h, in_tile, near_in)
    shard, copies = lax.optimization_barrier((shard, copies))
    both_y = jnp.concatenate([y1, y2])
    one, far, y34 = phase(
        ring(shard),
        ring(added(keep_a[1:3], both_y, widened(far)).astype(bf16), 3, True),
        to_other_y(give_34),
    )
    out_tiles = lax.all_to_all(copies, OWNER, 0, 0, tiled=True)
    one, far, y34, out_tiles = lax.optimization_barrier((one, far, y34, out_tiles))
    two, y5 = phase(ring(one), to_other_y(give_5))
    three, y6 = phase(ring(two), to_other_y(give_6))
    last, y7 = phase(ring(jnp.where(core == 0, three[:1], three[1:])), to_other_y(give_7))
    in_own = jnp.concatenate([one, two, three, last], 0)
    cross, in_other = phase(
        ring(added(keep_b[0:2], y34, far).astype(bf16), 2, True), (in_own, CORE, SWAP2)
    )
    square = (TILE, TILE)
    in_inverse = call(
        functools.partial(in_inverse_kernel, tokens),
        4,
        (PIECE, TILE),
        square,
        numbers(z, core),
        shard,
        in_own,
        in_other,
        scratch=[(square, bf16), (square, f32), (square, bf16)],
    )
    both_y = jnp.concatenate([y5, y6])
    (cross,) = phase(ring(added(keep_b[2:4], both_y, cross).astype(bf16), 1, True))
    cross, in_inverse = lax.optimization_barrier((cross, in_inverse))
    other, out_other = phase((cross, CORE, SWAP2), (out_tiles, CORE, SWAP2))
    own, other = [jnp.where(core == 0, a[0], a[1]) for a in (cross, other)]
    cross = added(own, other, keep_b[4], y7[0]).astype(bf16)
    m = z % 4
    row = 2 * yh + core
    slice_rows = out_width // lax.axis_size(DP)
    base = TILE * (m - m // 2)
    near = jnp.where(m == 3, 2, m + 1)
    own_at = jnp.where(m == 2, TILE, slice_rows * (4 * m + row) - base)
    near_at = jnp.where(m == 2, TILE, slice_rows * (4 * near + row) - base)
    own_at, near_at = [jnp.clip(a, -slice_rows, TILE) + PIECE for a in (own_at, near_at)]
    padded = call(
        functools.partial(out_inverse_kernel, tokens),
        6,
        (PIECE, TILE),
        (6 * PIECE, TILE),
        numbers(core),
        out_tiles,
        out_other,
        scratch=[(square, bf16), (square, f32), (square, bf16)],
    )
    middle = mdot(cross, in_inverse).astype(bf16)
    mine = lax.dynamic_slice_in_dim(middle, h * HALF, HALF, 1)
    theirs = lax.dynamic_slice_in_dim(middle, (1 - h) * HALF, HALF, 1)
    near_x, near_y, near_xy = phase(
        (theirs, X, SWAP_X), (mine, YH, SWAP2), (theirs, (YH, X), SWAP_BOTH)
    )
    middle = in_order(h, in_order(yh, mine, near_y), in_order(yh, near_x, near_xy))
    middle, padded = lax.optimization_barrier((middle, padded))
    other = lax.ppermute(middle, CORE, SWAP2)
    middle = jnp.moveaxis(in_order(core, middle, other), 0, 1).reshape(TILE, HALF)
    out_inverse = jnp.concatenate(
        [lax.dynamic_slice_in_dim(padded, at, slice_rows, 0) for at in (own_at, near_at)], 0
    )
    result = mdot(out_inverse, middle)

    near_part = result[slice_rows:].astype(bf16)
    up = lax.ppermute(near_part, Z, [(0, 1), (1, 2), (4, 5), (5, 6)])
    down = lax.ppermute(near_part, Z, [(3, 2), (7, 6)])
    whole = mdot(padded[PIECE : PIECE + TILE], middle)
    squares = jnp.where(m == 2, 0.0, jnp.sum(whole * whole))
    squares = all_sum(all_sum(squares, Z), OWNER)
    summed = result[:slice_rows] + up.astype(f32) + down.astype(f32)
    return (summed * lax.rsqrt(squares / (width * out_width) + 1e-06)).astype(bf16)


def solution(mesh):
    split = Mesh(mesh.devices.reshape(8, 2, 2, 2, 4), DP + OWNER)
    return jax.shard_map(
        shards,
        mesh=split,
        in_specs=(P(DP, None), P(), P(DP, None)),
        out_specs=P(DP, OWNER),
        check_vma=False,
    )
```

```python
import functools

import jax
import jax.numpy as jnp
from jax import lax
from jax.experimental import pallas as pl
from jax.experimental.pallas import tpu as pltpu
from jax.sharding import Mesh
from jax.sharding import PartitionSpec as P

TILE = 1024
PIECE = 256
HALF = 512
Z, YH, CORE, YL, X = "dp_0", "dp_1", "dp_2", "owner_0", "owner_1"
DP = (Z, YH, CORE)
OWNER = (YL, X)
DAMPING = 0.1
bf16, f32 = jnp.bfloat16, jnp.float32
PARAMS = pltpu.CompilerParams(vmem_limit_bytes=48 * 1024 * 1024)

AWAY = (4, 3, 3, 2, 2, 1, 1, 0, 0)
SWAP2 = [(0, 1), (1, 0)]
SWAP_X = [(0, 1), (1, 0), (2, 3), (3, 2)]
SWAP_BOTH = [(4 * a + b, 4 * (1 - a) + (b ^ 1)) for a in range(2) for b in range(4)]


def tdot(a, b):
    return lax.dot_general(a, b, (((0,), (0,)), ((), ())), preferred_element_type=f32)


def mdot(a, b):
    return jnp.dot(a, b, preferred_element_type=f32)


def aligned(start, size):
    return pl.ds(pl.multiple_of(start, size), size)


def pick_kernel(out_blocks, at_ref, cot_ref, pick_ref):
    h, k = at_ref[0], at_ref[1]
    rows = pl.ds(pl.multiple_of(pl.program_id(0) * pick_ref.shape[0], 8), pick_ref.shape[0])
    for j in range(out_blocks):
        here = slice(j * HALF, (j + 1) * HALF)
        there = slice(out_blocks * HALF + j * PIECE, out_blocks * HALF + (j + 1) * PIECE)
        pick_ref[:, here] = cot_ref[rows, aligned(j * TILE + h * HALF, HALF)]
        pick_ref[:, there] = cot_ref[rows, aligned(j * TILE + k * PIECE, PIECE)]


def load_tokens(pick_ref, recv_ref, own_ref, got_ref, out_ref, in_ref, sems):
    count = pick_ref.shape[0]
    copies = [
        pltpu.make_async_copy(src, dst.at[pl.ds(start, count)], sems.at[n])
        for n, (src, dst, start) in enumerate(
            (
                (pick_ref, out_ref, 0),
                (recv_ref, out_ref, count),
                (own_ref, in_ref, 0),
                (got_ref, in_ref, count),
            )
        )
    ]
    for copy in copies:
        copy.start()
    for copy in copies:
        copy.wait()


def factor_kernel(
    out_blocks, at_ref, pick_ref, recv_ref, own_ref, got_ref,
    part_ref, first_ref, out_ref, in_ref, sems,
):
    i = pl.program_id(0)

    @pl.when(i == 0)
    def _():
        load_tokens(pick_ref, recv_ref, own_ref, got_ref, out_ref, in_ref, sems)

    h, plane, block, piece = at_ref[0], at_ref[2 + 3 * i], at_ref[3 + 3 * i], at_ref[4 + 3 * i]
    left = out_ref[:, aligned(block * HALF + piece * PIECE, PIECE)]
    right = out_ref[:, aligned(out_blocks * HALF + block * PIECE, PIECE)]
    rows = in_ref[:, aligned((2 * h + piece) * PIECE, PIECE)]
    tiles = (
        tdot(left, right).astype(bf16),
        tdot(rows, in_ref[:, aligned(plane * 128, 128)]).astype(bf16),
    )
    for here, ref in ((i == 0, first_ref), (i > 0, part_ref)):

        @pl.when(here)
        def _():
            ref[0, :, :PIECE], ref[0, :, PIECE:] = tiles


def cross_kernel(base, gives, at_ref, pick_ref, recv_ref, own_ref, got_ref, keep_ref, *refs):
    give_refs, (out_ref, in_ref, sems) = refs[:-3], refs[-3:]
    i = pl.program_id(0)

    @pl.when(i == 0)
    def _():
        load_tokens(pick_ref, recv_ref, own_ref, got_ref, out_ref, in_ref, sems)

    yh, block, piece = at_ref[1], at_ref[3 + 3 * (base + i)], at_ref[4 + 3 * (base + i)]

    def rows_of(side):
        rows = out_ref[:, aligned(block * HALF + piece * PIECE + side * 128, 128)]
        return tdot(rows, in_ref[...]).astype(bf16)

    keep_ref[0] = rows_of(yh)
    give = rows_of(1 - yh)
    for slots, ref in zip(gives, give_refs):
        for n, slot in enumerate(slots):

            @pl.when(i + base == slot)
            def _():
                ref[n] = give


def scale_of(tokens, sums_ref):
    largest = jnp.zeros((), f32)
    for r in range(4):
        rows = matrix_rows(tokens, sums_ref, r * PIECE)
        largest = jnp.maximum(largest, jnp.max(jnp.sum(jnp.abs(rows), axis=1)))
    return 1.0 / largest


def eye_rows(start, count):
    row = lax.broadcasted_iota(jnp.int32, (count, TILE), 0) + start
    return (row == lax.broadcasted_iota(jnp.int32, (count, TILE), 1)).astype(f32)


def matrix_rows(tokens, sums_ref, start):
    return sums_ref[start : start + PIECE, :].astype(f32) / tokens + DAMPING * eye_rows(start, PIECE)


def split_factor(tokens, sums_ref, first_ref, low_ref, offset):
    scale = scale_of(tokens, sums_ref)
    for r in range(4):
        here = slice(r * PIECE, (r + 1) * PIECE)
        rows = matrix_rows(tokens, sums_ref, r * PIECE)
        first = 2.0 * scale * eye_rows(r * PIECE, PIECE) - (scale * scale) * rows
        first_ref[offset + r * PIECE : offset + (r + 1) * PIECE, :] = first
        low_ref[here, :] = first.astype(bf16)
        sums_ref[here, :] = rows.astype(bf16)


def inverse_rows(rows, sums_ref, low_ref):
    product = mdot(rows.astype(bf16), sums_ref[...]).astype(bf16)
    return (2.0 * rows - mdot(product, low_ref[...])).astype(bf16)


def in_inverse_kernel(
    tokens, at_ref, shard_ref, own_ref, other_ref,
    out_ref, sums_ref, first_ref, low_ref,
):
    i = pl.program_id(0)

    @pl.when(i == 0)
    def _():
        z, core = at_ref[0], at_ref[1]
        back = 1 - 2 * core

        def put(h, away, value):
            here = aligned((z + away + 8) % 8 * 128, 128)
            for piece in range(2):
                rows = aligned((2 * h + piece) * PIECE, PIECE)
                sums_ref[rows, here] = value[:, piece * 128 : (piece + 1) * 128]

        for h in range(2):
            put(h, 0, shard_ref[h])
            for d in (1, 2, 3):
                put(h, back * d, own_ref[2 * (d - 1) + h])
                put(h, -back * d, other_ref[2 * (d - 1) + h])
        put(core, 4, own_ref[6])
        put(1 - core, 4, other_ref[6])
        split_factor(tokens, sums_ref, first_ref, low_ref, 0)

    out_ref[...] = inverse_rows(first_ref[aligned(i * PIECE, PIECE), :], sums_ref, low_ref)


def out_inverse_kernel(tokens, at_ref, own_ref, other_ref, out_ref, sums_ref, first_ref, low_ref):
    i = pl.program_id(0)

    @pl.when(i == 0)
    def _():
        core = at_ref[0]
        for owner in range(8):
            here = slice(owner // 2 * PIECE, (owner // 2 + 1) * PIECE)
            for piece, ref in ((core, own_ref), (1 - core, other_ref)):
                sums_ref[aligned((2 * (owner % 2) + piece) * PIECE, PIECE), here] = ref[owner]
        split_factor(tokens, sums_ref, first_ref, low_ref, 0)

    outside = jnp.logical_or(i == 0, i == 5)

    @pl.when(outside)
    def _():
        out_ref[...] = jnp.zeros_like(out_ref)

    @pl.when(jnp.logical_not(outside))
    def _():
        out_ref[...] = inverse_rows(first_ref[aligned((i - 1) * PIECE, PIECE), :], sums_ref, low_ref)


def call(kernel, steps, block, out_shape, at, *args, scratch=()):
    def whole(a):
        return pl.BlockSpec(a.shape, lambda i, at: (0,) * len(a.shape))

    return pl.pallas_call(
        kernel,
        grid_spec=pltpu.PrefetchScalarGridSpec(
            num_scalar_prefetch=1,
            grid=(steps,),
            in_specs=[whole(a) for a in args],
            out_specs=pl.BlockSpec(block, lambda i, at: (i, 0)),
            scratch_shapes=[pltpu.VMEM(shape, dtype) for shape, dtype in scratch],
        ),
        out_shape=jax.ShapeDtypeStruct(out_shape, bf16),
        compiler_params=PARAMS,
    )(at, *args)


def ring_pairs(away=0, skip=False):
    pairs = []
    for plane in range(8):
        for core, way in ((0, -1), (1, 1)):
            if not skip or (plane + way * away) % 4 != 2:
                pairs.append((2 * plane + core, 2 * ((plane + way) % 8) + core))
    return pairs


def phase(*sends):
    values = lax.optimization_barrier(tuple(send[0] for send in sends))
    got = [lax.ppermute(value, *send[1:]) for value, send in zip(values, sends)]
    return lax.optimization_barrier(tuple(got))


def added(*parts):
    return functools.reduce(jnp.add, [p.astype(f32) for p in parts])


def in_order(flag, own, other):
    first = jnp.where(flag == 0, own, other)
    second = jnp.where(flag == 0, other, own)
    return jnp.stack([first, second])


def all_sum(value, axis):
    n = lax.axis_size(axis)
    shares = lax.all_to_all(jnp.full((n, 128), value, f32), axis, 0, 0, tiled=True)
    return jnp.sum(shares[:, 0])


def shards(hidden, norm_gain, cotangent):
    z, yh, core = lax.axis_index(Z), lax.axis_index(YH), lax.axis_index(CORE)
    yl, x = lax.axis_index(YL), lax.axis_index(X)
    k, h = 2 * yl + x // 2, x % 2
    here, width = hidden.shape
    out_width = cotangent.shape[1]
    out_blocks = out_width // TILE
    tokens = here * lax.axis_size(DP)

    def numbers(*values):
        return jnp.stack([jnp.asarray(v, jnp.int32) for v in values])

    pick = call(
        functools.partial(pick_kernel, out_blocks),
        4,
        (here // 4, out_blocks * (HALF + PIECE)),
        (here, out_blocks * (HALF + PIECE)),
        numbers(h, k),
        cotangent,
    )
    recv = lax.ppermute(pick, CORE, SWAP2)

    states = hidden.astype(f32)
    rms = lax.rsqrt(jnp.mean(states * states, axis=1, keepdims=True) + 1e-05)
    gain = lax.dynamic_slice_in_dim(norm_gain, k * TILE, TILE)
    mine = lax.dynamic_slice_in_dim(hidden, k * TILE, TILE, 1)
    normed = (mine.astype(f32) * rms * gain).astype(bf16)
    normed_recv = lax.ppermute(normed, CORE, SWAP2)

    way = 2 * core - 1
    table = []
    for i, away in enumerate(AWAY):
        plane = (z + way * away + 8) % 8
        piece = core if i in (0, 7) else 1 - core if i == 8 else (i + 1) % 2
        table += [plane, 3 * (plane // 4) + plane % 4 - plane % 4 // 2, piece]
    table = numbers(h, yh, *table)

    def slots(kernel, count, block, gives, skip=0):
        tokens_in = (pick, recv, normed, normed_recv)
        more = [(len(slots), *block) for slots in gives]
        return pl.pallas_call(
            kernel,
            grid_spec=pltpu.PrefetchScalarGridSpec(
                num_scalar_prefetch=1,
                grid=(count,),
                in_specs=[pl.BlockSpec(memory_space=pl.ANY) for _ in tokens_in],
                out_specs=[pl.BlockSpec((1, *block), lambda i, at: (jnp.maximum(i - skip, 0), 0, 0))]
                + [pl.BlockSpec(m, lambda i, at: (0, 0, 0)) for m in more],
                scratch_shapes=[
                    pltpu.VMEM((2 * here, pick.shape[1]), bf16),
                    pltpu.VMEM((2 * here, TILE), bf16),
                    pltpu.SemaphoreType.DMA((4,)),
                ],
            ),
            out_shape=[jax.ShapeDtypeStruct(m, bf16) for m in [(count - skip, *block)] + more],
            compiler_params=PARAMS,
        )(table, *tokens_in)

    def cross_part(base, count, gives):
        return slots(functools.partial(cross_kernel, base, gives), count, (128, TILE), gives)

    block = (PIECE, PIECE + 128)
    part, part_0 = slots(functools.partial(factor_kernel, out_blocks), 9, block, ((0,),), 1)
    keep_a, give_0, give_1, give_2 = cross_part(0, 3, ((0,), (1,), (2,)))
    keep_b, *give_b = cross_part(3, 5, ((3,), (4,), (5,), (6,), (7,)))

    def to_other_y(value):
        return value, YH, SWAP2

    def ring(value, *args):
        return value, (Z, CORE), ring_pairs(*args)

    def widened(got):
        nothing = jnp.zeros_like(got)
        return in_order(core, got, nothing)

    (far,) = phase(ring(part_0[0]))
    far, y0 = phase(ring(added(part[0:2], widened(far)).astype(bf16)), to_other_y(give_0))
    far, y1 = phase(ring(added(part[2:4], far).astype(bf16)), to_other_y(give_1))
    far, y2 = phase(ring(added(part[4:6], far).astype(bf16)), to_other_y(give_2))
    far, keep_b = lax.optimization_barrier((far, keep_b))
    both_in = jnp.concatenate([far[0, :, PIECE:], far[1, :, PIECE:]], 1)
    out_own = jnp.where(core == 0, far[0, :, :PIECE], far[1, :, :PIECE])
    out_other = jnp.where(core == 0, far[1, :, :PIECE], far[0, :, :PIECE])
    (other,) = phase((jnp.concatenate([out_other, both_in], 1), CORE, SWAP2))
    here_in = in_order(core, part[6, :, PIECE:], part[7, :, PIECE:])
    local = jnp.concatenate([part[6, :, :PIECE], here_in[0], here_in[1]], 1)
    tiles = (added(jnp.concatenate([out_own, both_in], 1), other) + local.astype(f32)).astype(bf16)
    other, far = phase((tiles, YH, SWAP2), ring(added(keep_a[0], y0[0]).astype(bf16), 4, True))
    tiles = added(tiles, other).astype(bf16)
    out_tile, in_tile = tiles[:, :PIECE], tiles[:, PIECE:]
    copies = jnp.broadcast_to(out_tile[None], (8, PIECE, PIECE))
    (near_in,) = phase((in_tile, X, SWAP_X))
    shard = in_order(h, in_tile, near_in)
    both_y = jnp.concatenate([y1, y2])
    one, far, y3 = phase(
        ring(shard),
        ring(added(keep_a[1:3], both_y, widened(far)).astype(bf16), 3, True),
        to_other_y(give_b[0]),
    )
    two, y4 = phase(ring(one), to_other_y(give_b[1]))
    three, y5 = phase(ring(two), to_other_y(give_b[2]))
    last, y6 = phase(ring(jnp.where(core == 0, three[:1], three[1:])), to_other_y(give_b[3]))
    in_own = jnp.concatenate([one, two, three, last], 0)
    in_own, copies = lax.optimization_barrier((in_own, copies))
    out_tiles = lax.all_to_all(copies, OWNER, 0, 0, tiled=True)
    both_y = jnp.concatenate([y3, y4])
    cross, in_other = phase(
        ring(added(keep_b[0:2], both_y, far).astype(bf16), 2, True), (in_own, CORE, SWAP2)
    )
    square = (TILE, TILE)
    in_inverse = call(
        functools.partial(in_inverse_kernel, tokens),
        4,
        (PIECE, TILE),
        square,
        numbers(z, core),
        shard,
        in_own,
        in_other,
        scratch=[(square, bf16), (square, f32), (square, bf16)],
    )
    both_y = jnp.concatenate([y5, y6])
    cross, y7 = phase(
        ring(added(keep_b[2:4], both_y, cross).astype(bf16), 1, True), to_other_y(give_b[4])
    )
    cross, in_inverse = lax.optimization_barrier((cross, in_inverse))
    other, out_other = phase((cross, CORE, SWAP2), (out_tiles, CORE, SWAP2))
    own, other = [jnp.where(core == 0, a[0], a[1]) for a in (cross, other)]
    cross = added(own, other, keep_b[4], y7[0]).astype(bf16)
    m = z % 4
    row = 2 * yh + core
    slice_rows = out_width // lax.axis_size(DP)
    base = TILE * (m - m // 2)
    near = jnp.where(m == 3, 2, m + 1)
    own_at = jnp.where(m == 2, TILE, slice_rows * (4 * m + row) - base)
    near_at = jnp.where(m == 2, TILE, slice_rows * (4 * near + row) - base)
    own_at, near_at = [jnp.clip(a, -slice_rows, TILE) + PIECE for a in (own_at, near_at)]
    padded = call(
        functools.partial(out_inverse_kernel, tokens),
        6,
        (PIECE, TILE),
        (6 * PIECE, TILE),
        numbers(core),
        out_tiles,
        out_other,
        scratch=[(square, bf16), (square, f32), (square, bf16)],
    )
    middle = mdot(cross, in_inverse).astype(bf16)
    mine = lax.dynamic_slice_in_dim(middle, h * HALF, HALF, 1)
    theirs = lax.dynamic_slice_in_dim(middle, (1 - h) * HALF, HALF, 1)
    near_x, near_y, near_xy = phase(
        (theirs, X, SWAP_X), (mine, YH, SWAP2), (theirs, (YH, X), SWAP_BOTH)
    )
    middle = in_order(h, in_order(yh, mine, near_y), in_order(yh, near_x, near_xy))
    middle, padded = lax.optimization_barrier((middle, padded))
    other = lax.ppermute(middle, CORE, SWAP2)
    middle = jnp.moveaxis(in_order(core, middle, other), 0, 1).reshape(TILE, HALF)
    out_inverse = jnp.concatenate(
        [lax.dynamic_slice_in_dim(padded, at, slice_rows, 0) for at in (own_at, near_at)], 0
    )
    result = mdot(out_inverse, middle)

    near_part = result[slice_rows:].astype(bf16)
    up = lax.ppermute(near_part, Z, [(0, 1), (1, 2), (4, 5), (5, 6)])
    down = lax.ppermute(near_part, Z, [(3, 2), (7, 6)])
    whole = mdot(padded[PIECE : PIECE + TILE], middle)
    squares = jnp.where(m == 2, 0.0, jnp.sum(whole * whole))
    squares = all_sum(all_sum(squares, Z), OWNER)
    summed = result[:slice_rows] + up.astype(f32) + down.astype(f32)
    return (summed * lax.rsqrt(squares / (width * out_width) + 1e-06)).astype(bf16)


def solution(mesh):
    split = Mesh(mesh.devices.reshape(8, 2, 2, 2, 4), DP + OWNER)
    return jax.shard_map(
        shards,
        mesh=split,
        in_specs=(P(DP, None), P(), P(DP, None)),
        out_specs=P(DP, OWNER),
        check_vma=False,
    )
```

```python
import functools

import jax
import jax.numpy as jnp
from jax import lax
from jax.experimental import pallas as pl
from jax.experimental.pallas import tpu as pltpu
from jax.sharding import Mesh
from jax.sharding import PartitionSpec as P

TILE = 1024
PIECE = 256
HALF = 512
Z, YH, CORE, YL, X = "dp_0", "dp_1", "dp_2", "owner_0", "owner_1"
DP = (Z, YH, CORE)
OWNER = (YL, X)
DAMPING = 0.1
bf16, f32 = jnp.bfloat16, jnp.float32
MIB = 1024 * 1024

AWAY = (4, 3, 3, 2, 2, 1, 1, 0, 0)
SWAP2 = [(0, 1), (1, 0)]
SWAP_X = [(0, 1), (1, 0), (2, 3), (3, 2)]
SWAP_BOTH = [(4 * a + b, 4 * (1 - a) + (b ^ 1)) for a in range(2) for b in range(4)]


def tdot(a, b):
    return lax.dot_general(a, b, (((0,), (0,)), ((), ())), preferred_element_type=f32)


def mdot(a, b):
    return jnp.dot(a, b, preferred_element_type=f32)


def aligned(start, size):
    return pl.ds(pl.multiple_of(start, size), size)


def pick_kernel(out_blocks, at_ref, cot_ref, pick_ref):
    h, k = at_ref[0], at_ref[1]
    rows = pl.ds(pl.multiple_of(pl.program_id(0) * pick_ref.shape[0], 8), pick_ref.shape[0])
    for j in range(out_blocks):
        here = slice(j * HALF, (j + 1) * HALF)
        there = slice(out_blocks * HALF + j * PIECE, out_blocks * HALF + (j + 1) * PIECE)
        pick_ref[:, here] = cot_ref[rows, aligned(j * TILE + h * HALF, HALF)]
        pick_ref[:, there] = cot_ref[rows, aligned(j * TILE + k * PIECE, PIECE)]


def load_tokens(pick_ref, recv_ref, own_ref, got_ref, out_ref, in_ref, sems):
    count = pick_ref.shape[0]
    copies = [
        pltpu.make_async_copy(src, dst.at[pl.ds(start, count)], sems.at[n])
        for n, (src, dst, start) in enumerate(
            (
                (pick_ref, out_ref, 0),
                (recv_ref, out_ref, count),
                (own_ref, in_ref, 0),
                (got_ref, in_ref, count),
            )
        )
    ]
    for copy in copies:
        copy.start()
    for copy in copies:
        copy.wait()


def factor_kernel(
    out_blocks, at_ref, pick_ref, recv_ref, own_ref, got_ref,
    part_ref, first_ref, out_ref, in_ref, sems,
):
    i = pl.program_id(0)

    @pl.when(i == 0)
    def _():
        load_tokens(pick_ref, recv_ref, own_ref, got_ref, out_ref, in_ref, sems)

    h, plane, block, piece = at_ref[0], at_ref[2 + 3 * i], at_ref[3 + 3 * i], at_ref[4 + 3 * i]
    left = out_ref[:, aligned(block * HALF + piece * PIECE, PIECE)]
    right = out_ref[:, aligned(out_blocks * HALF + block * PIECE, PIECE)]
    rows = in_ref[:, aligned((2 * h + piece) * PIECE, PIECE)]
    tiles = (
        tdot(left, right).astype(bf16),
        tdot(rows, in_ref[:, aligned(plane * 128, 128)]).astype(bf16),
    )
    for here, ref in ((i == 0, first_ref), (i > 0, part_ref)):

        @pl.when(here)
        def _():
            ref[0, :, :PIECE], ref[0, :, PIECE:] = tiles


def cross_kernel(base, gives, at_ref, pick_ref, recv_ref, own_ref, got_ref, keep_ref, *refs):
    give_refs, (out_ref, in_ref, sems) = refs[:-3], refs[-3:]
    i = pl.program_id(0)

    @pl.when(i == 0)
    def _():
        load_tokens(pick_ref, recv_ref, own_ref, got_ref, out_ref, in_ref, sems)

    yh, block, piece = at_ref[1], at_ref[3 + 3 * (base + i)], at_ref[4 + 3 * (base + i)]

    def rows_of(side):
        rows = out_ref[:, aligned(block * HALF + piece * PIECE + side * 128, 128)]
        return tdot(rows, in_ref[...]).astype(bf16)

    keep_ref[0] = rows_of(yh)
    give = rows_of(1 - yh)
    for slots, ref in zip(gives, give_refs):
        for n, slot in enumerate(slots):

            @pl.when(i + base == slot)
            def _():
                ref[n] = give


def split_factor(tokens, sums_ref, first_ref, low_ref):
    row = lax.broadcasted_iota(jnp.int32, (PIECE, PIECE), 0)
    eye = (row == lax.broadcasted_iota(jnp.int32, (PIECE, PIECE), 1)).astype(f32)
    largest = jnp.zeros((1, TILE), f32)
    for r in range(4):
        here = slice(r * PIECE, (r + 1) * PIECE)
        first_ref[here, :] = sums_ref[here, :].astype(f32) / tokens
        first_ref[here, here] += DAMPING * eye
        largest += jnp.sum(jnp.abs(first_ref[here, :]), axis=0, keepdims=True)
    scale = 1.0 / jnp.max(largest)
    for r in range(4):
        here = slice(r * PIECE, (r + 1) * PIECE)
        matrix = first_ref[here, :]
        sums_ref[here, :] = matrix.astype(bf16)
        first_ref[here, :] = -(scale * scale) * matrix
        first_ref[here, here] += (2.0 * scale) * eye
        low_ref[here, :] = first_ref[here, :].astype(bf16)


def inverse_rows(rows, sums_ref, low_ref):
    product = mdot(rows.astype(bf16), sums_ref[...]).astype(bf16)
    return (2.0 * rows - mdot(product, low_ref[...])).astype(bf16)


def in_inverse_kernel(
    tokens, at_ref, shard_ref, own_ref, other_ref,
    out_ref, sums_ref, first_ref, low_ref,
):
    i = pl.program_id(0)

    @pl.when(i == 0)
    def _():
        z, core = at_ref[0], at_ref[1]
        back = 1 - 2 * core

        def put(h, away, value):
            here = aligned((z + away + 8) % 8 * 128, 128)
            for piece in range(2):
                rows = aligned((2 * h + piece) * PIECE, PIECE)
                sums_ref[rows, here] = value[:, piece * 128 : (piece + 1) * 128]

        for h in range(2):
            put(h, 0, shard_ref[h])
            for d in (1, 2, 3):
                put(h, back * d, own_ref[2 * (d - 1) + h])
                put(h, -back * d, other_ref[2 * (d - 1) + h])
        put(core, 4, own_ref[6])
        put(1 - core, 4, other_ref[6])
        split_factor(tokens, sums_ref, first_ref, low_ref)

    out_ref[...] = inverse_rows(first_ref[aligned(i * PIECE, PIECE), :], sums_ref, low_ref)


def out_inverse_kernel(tokens, at_ref, own_ref, other_ref, out_ref, sums_ref, first_ref, low_ref):
    i = pl.program_id(0)

    @pl.when(i == 0)
    def _():
        core = at_ref[0]
        for owner in range(8):
            here = slice(owner // 2 * PIECE, (owner // 2 + 1) * PIECE)
            for piece, ref in ((core, own_ref), (1 - core, other_ref)):
                sums_ref[aligned((2 * (owner % 2) + piece) * PIECE, PIECE), here] = ref[owner]
        split_factor(tokens, sums_ref, first_ref, low_ref)

    outside = jnp.logical_or(i == 0, i == 5)

    @pl.when(outside)
    def _():
        out_ref[...] = jnp.zeros_like(out_ref)

    @pl.when(jnp.logical_not(outside))
    def _():
        out_ref[...] = inverse_rows(first_ref[aligned((i - 1) * PIECE, PIECE), :], sums_ref, low_ref)


def call(kernel, steps, block, out_shape, at, *args, limit, scratch=()):
    def whole(a):
        return pl.BlockSpec(a.shape, lambda i, at: (0,) * len(a.shape))

    return pl.pallas_call(
        kernel,
        grid_spec=pltpu.PrefetchScalarGridSpec(
            num_scalar_prefetch=1,
            grid=(steps,),
            in_specs=[whole(a) for a in args],
            out_specs=pl.BlockSpec(block, lambda i, at: (i, 0)),
            scratch_shapes=[pltpu.VMEM(shape, dtype) for shape, dtype in scratch],
        ),
        out_shape=jax.ShapeDtypeStruct(out_shape, bf16),
        compiler_params=pltpu.CompilerParams(vmem_limit_bytes=limit * MIB),
    )(at, *args)


def ring_pairs(away=0, skip=False):
    pairs = []
    for plane in range(8):
        for core, way in ((0, -1), (1, 1)):
            if not skip or (plane + way * away) % 4 != 2:
                pairs.append((2 * plane + core, 2 * ((plane + way) % 8) + core))
    return pairs


def phase(*sends):
    values = lax.optimization_barrier(tuple(send[0] for send in sends))
    got = [lax.ppermute(value, *send[1:]) for value, send in zip(values, sends)]
    return lax.optimization_barrier(tuple(got))


def added(*parts):
    return functools.reduce(jnp.add, [p.astype(f32) for p in parts])


def in_order(flag, own, other):
    first = jnp.where(flag == 0, own, other)
    second = jnp.where(flag == 0, other, own)
    return jnp.stack([first, second])


def all_sum(value, axis):
    n = lax.axis_size(axis)
    shares = lax.all_to_all(jnp.full((n, 128), value, f32), axis, 0, 0, tiled=True)
    return jnp.sum(shares[:, 0])


def shards(hidden, norm_gain, cotangent):
    z, yh, core = lax.axis_index(Z), lax.axis_index(YH), lax.axis_index(CORE)
    yl, x = lax.axis_index(YL), lax.axis_index(X)
    k, h = 2 * yl + x // 2, x % 2
    here, width = hidden.shape
    out_width = cotangent.shape[1]
    out_blocks = out_width // TILE
    tokens = here * lax.axis_size(DP)

    def numbers(*values):
        return jnp.stack([jnp.asarray(v, jnp.int32) for v in values])

    pick = call(
        functools.partial(pick_kernel, out_blocks),
        4,
        (here // 4, out_blocks * (HALF + PIECE)),
        (here, out_blocks * (HALF + PIECE)),
        numbers(h, k),
        cotangent,
        limit=8,
    )
    recv = lax.ppermute(pick, CORE, SWAP2)

    states = hidden.astype(f32)
    rms = lax.rsqrt(jnp.mean(states * states, axis=1, keepdims=True) + 1e-05)
    gain = lax.dynamic_slice_in_dim(norm_gain, k * TILE, TILE)
    mine = lax.dynamic_slice_in_dim(hidden, k * TILE, TILE, 1)
    normed = (mine.astype(f32) * rms * gain).astype(bf16)
    normed_recv = lax.ppermute(normed, CORE, SWAP2)

    way = 2 * core - 1
    table = []
    for i, away in enumerate(AWAY):
        plane = (z + way * away + 8) % 8
        piece = core if i in (0, 7) else 1 - core if i == 8 else (i + 1) % 2
        table += [plane, 3 * (plane // 4) + plane % 4 - plane % 4 // 2, piece]
    table = numbers(h, yh, *table)

    def slots(kernel, count, block, gives, skip=0):
        tokens_in = (pick, recv, normed, normed_recv)
        more = [(len(slots), *block) for slots in gives]
        return pl.pallas_call(
            kernel,
            grid_spec=pltpu.PrefetchScalarGridSpec(
                num_scalar_prefetch=1,
                grid=(count,),
                in_specs=[pl.BlockSpec(memory_space=pl.ANY) for _ in tokens_in],
                out_specs=[pl.BlockSpec((1, *block), lambda i, at: (jnp.maximum(i - skip, 0), 0, 0))]
                + [pl.BlockSpec(m, lambda i, at: (0, 0, 0)) for m in more],
                scratch_shapes=[
                    pltpu.VMEM((2 * here, pick.shape[1]), bf16),
                    pltpu.VMEM((2 * here, TILE), bf16),
                    pltpu.SemaphoreType.DMA((4,)),
                ],
            ),
            out_shape=[jax.ShapeDtypeStruct(m, bf16) for m in [(count - skip, *block)] + more],
            compiler_params=pltpu.CompilerParams(vmem_limit_bytes=12 * MIB),
        )(table, *tokens_in)

    def cross_part(base, count, gives):
        return slots(functools.partial(cross_kernel, base, gives), count, (128, TILE), gives)

    block = (PIECE, PIECE + 128)
    part, part_0 = slots(functools.partial(factor_kernel, out_blocks), 9, block, ((0,),), 1)
    keep_a, give_0, give_1, give_2 = cross_part(0, 3, ((0,), (1,), (2,)))
    keep_b, *give_b = cross_part(3, 5, ((3,), (4,), (5,), (6,), (7,)))

    def to_other_y(value):
        return value, YH, SWAP2

    def ring(value, *args):
        return value, (Z, CORE), ring_pairs(*args)

    def widened(got):
        nothing = jnp.zeros_like(got)
        return in_order(core, got, nothing)

    (far,) = phase(ring(part_0[0]))
    far, y0 = phase(ring(added(part[0:2], widened(far)).astype(bf16)), to_other_y(give_0))
    far, y1 = phase(ring(added(part[2:4], far).astype(bf16)), to_other_y(give_1))
    far, y2 = phase(ring(added(part[4:6], far).astype(bf16)), to_other_y(give_2))
    far, keep_b = lax.optimization_barrier((far, keep_b))
    both_in = jnp.concatenate([far[0, :, PIECE:], far[1, :, PIECE:]], 1)
    out_own = jnp.where(core == 0, far[0, :, :PIECE], far[1, :, :PIECE])
    out_other = jnp.where(core == 0, far[1, :, :PIECE], far[0, :, :PIECE])
    (other,) = phase((jnp.concatenate([out_other, both_in], 1), CORE, SWAP2))
    here_in = in_order(core, part[6, :, PIECE:], part[7, :, PIECE:])
    local = jnp.concatenate([part[6, :, :PIECE], here_in[0], here_in[1]], 1)
    tiles = (added(jnp.concatenate([out_own, both_in], 1), other) + local.astype(f32)).astype(bf16)
    other, far = phase((tiles, YH, SWAP2), ring(added(keep_a[0], y0[0]).astype(bf16), 4, True))
    tiles = added(tiles, other).astype(bf16)
    out_tile, in_tile = tiles[:, :PIECE], tiles[:, PIECE:]
    copies = jnp.broadcast_to(out_tile[None], (8, PIECE, PIECE))
    (near_in,) = phase((in_tile, X, SWAP_X))
    shard = in_order(h, in_tile, near_in)
    both_y = jnp.concatenate([y1, y2])
    one, far, y3 = phase(
        ring(shard),
        ring(added(keep_a[1:3], both_y, widened(far)).astype(bf16), 3, True),
        to_other_y(give_b[0]),
    )
    two, y4 = phase(ring(one), to_other_y(give_b[1]))
    three, y5 = phase(ring(two), to_other_y(give_b[2]))
    last, y6 = phase(ring(jnp.where(core == 0, three[:1], three[1:])), to_other_y(give_b[3]))
    in_own = jnp.concatenate([one, two, three, last], 0)
    in_own, copies = lax.optimization_barrier((in_own, copies))
    out_tiles = lax.all_to_all(copies, OWNER, 0, 0, tiled=True)
    both_y = jnp.concatenate([y3, y4])
    cross, in_other = phase(
        ring(added(keep_b[0:2], both_y, far).astype(bf16), 2, True), (in_own, CORE, SWAP2)
    )
    square = (TILE, TILE)
    in_inverse = call(
        functools.partial(in_inverse_kernel, tokens),
        4,
        (PIECE, TILE),
        square,
        numbers(z, core),
        shard,
        in_own,
        in_other,
        limit=26,
        scratch=[(square, bf16), (square, f32), (square, bf16)],
    )
    both_y = jnp.concatenate([y5, y6])
    cross, y7 = phase(
        ring(added(keep_b[2:4], both_y, cross).astype(bf16), 1, True), to_other_y(give_b[4])
    )
    cross, in_inverse = lax.optimization_barrier((cross, in_inverse))
    other, out_other = phase((cross, CORE, SWAP2), (out_tiles, CORE, SWAP2))
    own, other = [jnp.where(core == 0, a[0], a[1]) for a in (cross, other)]
    cross = added(own, other, keep_b[4], y7[0]).astype(bf16)
    m = z % 4
    row = 2 * yh + core
    slice_rows = out_width // lax.axis_size(DP)
    base = TILE * (m - m // 2)
    near = jnp.where(m == 3, 2, m + 1)
    own_at = jnp.where(m == 2, TILE, slice_rows * (4 * m + row) - base)
    near_at = jnp.where(m == 2, TILE, slice_rows * (4 * near + row) - base)
    own_at, near_at = [jnp.clip(a, -slice_rows, TILE) + PIECE for a in (own_at, near_at)]
    padded = call(
        functools.partial(out_inverse_kernel, tokens),
        6,
        (PIECE, TILE),
        (6 * PIECE, TILE),
        numbers(core),
        out_tiles,
        out_other,
        limit=26,
        scratch=[(square, bf16), (square, f32), (square, bf16)],
    )
    middle = mdot(cross, in_inverse).astype(bf16)
    mine = lax.dynamic_slice_in_dim(middle, h * HALF, HALF, 1)
    theirs = lax.dynamic_slice_in_dim(middle, (1 - h) * HALF, HALF, 1)
    near_x, near_y, near_xy = phase(
        (theirs, X, SWAP_X), (mine, YH, SWAP2), (theirs, (YH, X), SWAP_BOTH)
    )
    middle = in_order(h, in_order(yh, mine, near_y), in_order(yh, near_x, near_xy))
    middle, padded = lax.optimization_barrier((middle, padded))
    other = lax.ppermute(middle, CORE, SWAP2)
    middle = jnp.moveaxis(in_order(core, middle, other), 0, 1).reshape(TILE, HALF)
    out_inverse = jnp.concatenate(
        [lax.dynamic_slice_in_dim(padded, at, slice_rows, 0) for at in (own_at, near_at)], 0
    )
    result = mdot(out_inverse, middle)

    near_part = result[slice_rows:].astype(bf16)
    up = lax.ppermute(near_part, Z, [(0, 1), (1, 2), (4, 5), (5, 6)])
    down = lax.ppermute(near_part, Z, [(3, 2), (7, 6)])
    whole = mdot(padded[PIECE : PIECE + TILE], middle)
    squares = jnp.where(m == 2, 0.0, jnp.sum(whole * whole))
    squares = all_sum(all_sum(squares, Z), OWNER)
    summed = result[:slice_rows] + up.astype(f32) + down.astype(f32)
    return (summed * lax.rsqrt(squares / (width * out_width) + 1e-06)).astype(bf16)


def solution(mesh):
    split = Mesh(mesh.devices.reshape(8, 2, 2, 2, 4), DP + OWNER)
    return jax.shard_map(
        shards,
        mesh=split,
        in_specs=(P(DP, None), P(), P(DP, None)),
        out_specs=P(DP, OWNER),
        check_vma=False,
    )
```

```python
import functools

import jax
import jax.numpy as jnp
from jax import lax
from jax.experimental import pallas as pl
from jax.experimental.pallas import tpu as pltpu
from jax.sharding import Mesh
from jax.sharding import PartitionSpec as P

TILE = 1024
PIECE = 256
HALF = 512
Z, YH, CORE, YL, X = "dp_0", "dp_1", "dp_2", "owner_0", "owner_1"
DP = (Z, YH, CORE)
OWNER = (YL, X)
DAMPING = 0.1
bf16, f32 = jnp.bfloat16, jnp.float32
MIB = 1024 * 1024

AWAY = (4, 3, 3, 2, 2, 1, 1, 0, 0)
SWAP2 = [(0, 1), (1, 0)]
SWAP_X = [(0, 1), (1, 0), (2, 3), (3, 2)]
SWAP_BOTH = [(4 * a + b, 4 * (1 - a) + (b ^ 1)) for a in range(2) for b in range(4)]


def tdot(a, b):
    return lax.dot_general(a, b, (((0,), (0,)), ((), ())), preferred_element_type=f32)


def mdot(a, b):
    return jnp.dot(a, b, preferred_element_type=f32)


def aligned(start, size):
    return pl.ds(pl.multiple_of(start, size), size)


def pick_kernel(out_blocks, at_ref, cot_ref, pick_ref):
    h, k = at_ref[0], at_ref[1]
    rows = pl.ds(pl.multiple_of(pl.program_id(0) * pick_ref.shape[0], 8), pick_ref.shape[0])
    for j in range(out_blocks):
        here = slice(j * HALF, (j + 1) * HALF)
        there = slice(out_blocks * HALF + j * PIECE, out_blocks * HALF + (j + 1) * PIECE)
        pick_ref[:, here] = cot_ref[rows, aligned(j * TILE + h * HALF, HALF)]
        pick_ref[:, there] = cot_ref[rows, aligned(j * TILE + k * PIECE, PIECE)]


def load_tokens(pick_ref, recv_ref, own_ref, got_ref, out_ref, in_ref, sems):
    count = pick_ref.shape[0]
    copies = [
        pltpu.make_async_copy(src, dst.at[pl.ds(start, count)], sems.at[n])
        for n, (src, dst, start) in enumerate(
            (
                (pick_ref, out_ref, 0),
                (recv_ref, out_ref, count),
                (own_ref, in_ref, 0),
                (got_ref, in_ref, count),
            )
        )
    ]
    for copy in copies:
        copy.start()
    for copy in copies:
        copy.wait()


def factor_kernel(
    out_blocks, at_ref, pick_ref, recv_ref, own_ref, got_ref,
    part_ref, first_ref, out_ref, in_ref, sems,
):
    i = pl.program_id(0)

    @pl.when(i == 0)
    def _():
        load_tokens(pick_ref, recv_ref, own_ref, got_ref, out_ref, in_ref, sems)

    h, plane, block, piece = at_ref[0], at_ref[2 + 3 * i], at_ref[3 + 3 * i], at_ref[4 + 3 * i]
    left = out_ref[:, aligned(block * HALF + piece * PIECE, PIECE)]
    right = out_ref[:, aligned(out_blocks * HALF + block * PIECE, PIECE)]
    rows = in_ref[:, aligned((2 * h + piece) * PIECE, PIECE)]
    tiles = (
        tdot(left, right).astype(bf16),
        tdot(rows, in_ref[:, aligned(plane * 128, 128)]).astype(bf16),
    )
    for here, ref in ((i == 0, first_ref), (i > 0, part_ref)):

        @pl.when(here)
        def _():
            ref[0, :, :PIECE], ref[0, :, PIECE:] = tiles


def cross_kernel(base, gives, at_ref, pick_ref, recv_ref, own_ref, got_ref, keep_ref, *refs):
    give_refs, (out_ref, in_ref, sems) = refs[:-3], refs[-3:]
    i = pl.program_id(0)

    @pl.when(i == 0)
    def _():
        load_tokens(pick_ref, recv_ref, own_ref, got_ref, out_ref, in_ref, sems)

    yh, block, piece = at_ref[1], at_ref[3 + 3 * (base + i)], at_ref[4 + 3 * (base + i)]

    def rows_of(side):
        rows = out_ref[:, aligned(block * HALF + piece * PIECE + side * 128, 128)]
        return tdot(rows, in_ref[...]).astype(bf16)

    keep_ref[0] = rows_of(yh)
    give = rows_of(1 - yh)
    for slots, ref in zip(gives, give_refs):
        for n, slot in enumerate(slots):

            @pl.when(i + base == slot)
            def _():
                ref[n] = give


def split_factor(tokens, sums_ref, first_ref, low_ref):
    row = lax.broadcasted_iota(jnp.int32, (PIECE, PIECE), 0)
    eye = (row == lax.broadcasted_iota(jnp.int32, (PIECE, PIECE), 1)).astype(f32)
    largest = jnp.zeros((1, TILE), f32)
    for r in range(4):
        here = slice(r * PIECE, (r + 1) * PIECE)
        first_ref[here, :] = sums_ref[here, :].astype(f32) / tokens
        first_ref[here, here] += DAMPING * eye
        largest += jnp.sum(jnp.abs(first_ref[here, :]), axis=0, keepdims=True)
    scale = 1.0 / jnp.max(largest)
    for r in range(4):
        here = slice(r * PIECE, (r + 1) * PIECE)
        matrix = first_ref[here, :]
        sums_ref[here, :] = matrix.astype(bf16)
        first_ref[here, :] = -(scale * scale) * matrix
        first_ref[here, here] += (2.0 * scale) * eye
        low_ref[here, :] = first_ref[here, :].astype(bf16)


def inverse_rows(rows, sums_ref, low_ref):
    product = mdot(rows.astype(bf16), sums_ref[...]).astype(bf16)
    return (2.0 * rows - mdot(product, low_ref[...])).astype(bf16)


def in_inverse_kernel(
    tokens, at_ref, shard_ref, own_ref, other_ref,
    out_ref, sums_ref, first_ref, low_ref,
):
    i = pl.program_id(0)

    @pl.when(i == 0)
    def _():
        z, core = at_ref[0], at_ref[1]
        back = 1 - 2 * core

        def put(h, away, value):
            here = aligned((z + away + 8) % 8 * 128, 128)
            for piece in range(2):
                rows = aligned((2 * h + piece) * PIECE, PIECE)
                sums_ref[rows, here] = value[:, piece * 128 : (piece + 1) * 128]

        for h in range(2):
            put(h, 0, shard_ref[h])
            for d in (1, 2, 3):
                put(h, back * d, own_ref[2 * (d - 1) + h])
                put(h, -back * d, other_ref[2 * (d - 1) + h])
        put(core, 4, own_ref[6])
        put(1 - core, 4, other_ref[6])
        split_factor(tokens, sums_ref, first_ref, low_ref)

    out_ref[...] = inverse_rows(first_ref[aligned(i * HALF, HALF), :], sums_ref, low_ref)


def out_inverse_kernel(tokens, at_ref, own_ref, other_ref, out_ref, sums_ref, first_ref, low_ref):
    i = pl.program_id(0)

    @pl.when(i == 0)
    def _():
        core = at_ref[0]
        for owner in range(8):
            here = slice(owner // 2 * PIECE, (owner // 2 + 1) * PIECE)
            for piece, ref in ((core, own_ref), (1 - core, other_ref)):
                sums_ref[aligned((2 * (owner % 2) + piece) * PIECE, PIECE), here] = ref[owner]
        split_factor(tokens, sums_ref, first_ref, low_ref)

    outside = jnp.logical_or(i == 0, i == 3)

    @pl.when(outside)
    def _():
        out_ref[...] = jnp.zeros_like(out_ref)

    @pl.when(jnp.logical_not(outside))
    def _():
        out_ref[...] = inverse_rows(first_ref[aligned((i - 1) * HALF, HALF), :], sums_ref, low_ref)


def call(kernel, steps, block, out_shape, at, *args, limit, scratch=()):
    def whole(a):
        return pl.BlockSpec(a.shape, lambda i, at: (0,) * len(a.shape))

    return pl.pallas_call(
        kernel,
        grid_spec=pltpu.PrefetchScalarGridSpec(
            num_scalar_prefetch=1,
            grid=(steps,),
            in_specs=[whole(a) for a in args],
            out_specs=pl.BlockSpec(block, lambda i, at: (i, 0)),
            scratch_shapes=[pltpu.VMEM(shape, dtype) for shape, dtype in scratch],
        ),
        out_shape=jax.ShapeDtypeStruct(out_shape, bf16),
        compiler_params=pltpu.CompilerParams(vmem_limit_bytes=limit * MIB),
    )(at, *args)


def ring_pairs(away=0, skip=False):
    pairs = []
    for plane in range(8):
        for core, way in ((0, -1), (1, 1)):
            if not skip or (plane + way * away) % 4 != 2:
                pairs.append((2 * plane + core, 2 * ((plane + way) % 8) + core))
    return pairs


def phase(*sends):
    values = lax.optimization_barrier(tuple(send[0] for send in sends))
    got = [lax.ppermute(value, *send[1:]) for value, send in zip(values, sends)]
    return lax.optimization_barrier(tuple(got))


def added(*parts):
    return functools.reduce(jnp.add, [p.astype(f32) for p in parts])


def in_order(flag, own, other):
    first = jnp.where(flag == 0, own, other)
    second = jnp.where(flag == 0, other, own)
    return jnp.stack([first, second])


def all_sum(value, axis):
    n = lax.axis_size(axis)
    shares = lax.all_to_all(jnp.full((n, 128), value, f32), axis, 0, 0, tiled=True)
    return jnp.sum(shares[:, 0])


def shards(hidden, norm_gain, cotangent):
    z, yh, core = lax.axis_index(Z), lax.axis_index(YH), lax.axis_index(CORE)
    yl, x = lax.axis_index(YL), lax.axis_index(X)
    k, h = 2 * yl + x // 2, x % 2
    here, width = hidden.shape
    out_width = cotangent.shape[1]
    out_blocks = out_width // TILE
    tokens = here * lax.axis_size(DP)

    def numbers(*values):
        return jnp.stack([jnp.asarray(v, jnp.int32) for v in values])

    pick = call(
        functools.partial(pick_kernel, out_blocks),
        4,
        (here // 4, out_blocks * (HALF + PIECE)),
        (here, out_blocks * (HALF + PIECE)),
        numbers(h, k),
        cotangent,
        limit=8,
    )
    recv = lax.ppermute(pick, CORE, SWAP2)

    states = hidden.astype(f32)
    rms = lax.rsqrt(jnp.mean(states * states, axis=1, keepdims=True) + 1e-05)
    gain = lax.dynamic_slice_in_dim(norm_gain, k * TILE, TILE)
    mine = lax.dynamic_slice_in_dim(hidden, k * TILE, TILE, 1)
    normed = (mine.astype(f32) * rms * gain).astype(bf16)
    normed_recv = lax.ppermute(normed, CORE, SWAP2)

    way = 2 * core - 1
    table = []
    for i, away in enumerate(AWAY):
        plane = (z + way * away + 8) % 8
        piece = core if i in (0, 7) else 1 - core if i == 8 else (i + 1) % 2
        table += [plane, 3 * (plane // 4) + plane % 4 - plane % 4 // 2, piece]
    table = numbers(h, yh, *table)

    def slots(kernel, count, block, gives, skip=0):
        tokens_in = (pick, recv, normed, normed_recv)
        more = [(len(slots), *block) for slots in gives]
        return pl.pallas_call(
            kernel,
            grid_spec=pltpu.PrefetchScalarGridSpec(
                num_scalar_prefetch=1,
                grid=(count,),
                in_specs=[pl.BlockSpec(memory_space=pl.ANY) for _ in tokens_in],
                out_specs=[pl.BlockSpec((1, *block), lambda i, at: (jnp.maximum(i - skip, 0), 0, 0))]
                + [pl.BlockSpec(m, lambda i, at: (0, 0, 0)) for m in more],
                scratch_shapes=[
                    pltpu.VMEM((2 * here, pick.shape[1]), bf16),
                    pltpu.VMEM((2 * here, TILE), bf16),
                    pltpu.SemaphoreType.DMA((4,)),
                ],
            ),
            out_shape=[jax.ShapeDtypeStruct(m, bf16) for m in [(count - skip, *block)] + more],
            compiler_params=pltpu.CompilerParams(vmem_limit_bytes=12 * MIB),
        )(table, *tokens_in)

    def cross_part(base, count, gives):
        return slots(functools.partial(cross_kernel, base, gives), count, (128, TILE), gives)

    block = (PIECE, PIECE + 128)
    part, part_0 = slots(functools.partial(factor_kernel, out_blocks), 9, block, ((0,),), 1)
    keep_a, give_0, give_1, give_2 = cross_part(0, 3, ((0,), (1,), (2,)))
    keep_b, *give_b = cross_part(3, 5, ((3,), (4,), (5,), (6,), (7,)))

    def to_other_y(value):
        return value, YH, SWAP2

    def ring(value, *args):
        return value, (Z, CORE), ring_pairs(*args)

    def widened(got):
        nothing = jnp.zeros_like(got)
        return in_order(core, got, nothing)

    (far,) = phase(ring(part_0[0]))
    far, y0 = phase(ring(added(part[0:2], widened(far)).astype(bf16)), to_other_y(give_0))
    far, y1 = phase(ring(added(part[2:4], far).astype(bf16)), to_other_y(give_1))
    far, y2 = phase(ring(added(part[4:6], far).astype(bf16)), to_other_y(give_2))
    far, keep_b = lax.optimization_barrier((far, keep_b))
    both_in = jnp.concatenate([far[0, :, PIECE:], far[1, :, PIECE:]], 1)
    out_own = jnp.where(core == 0, far[0, :, :PIECE], far[1, :, :PIECE])
    out_other = jnp.where(core == 0, far[1, :, :PIECE], far[0, :, :PIECE])
    (other,) = phase((jnp.concatenate([out_other, both_in], 1), CORE, SWAP2))
    here_in = in_order(core, part[6, :, PIECE:], part[7, :, PIECE:])
    local = jnp.concatenate([part[6, :, :PIECE], here_in[0], here_in[1]], 1)
    tiles = (added(jnp.concatenate([out_own, both_in], 1), other) + local.astype(f32)).astype(bf16)
    other, far = phase((tiles, YH, SWAP2), ring(added(keep_a[0], y0[0]).astype(bf16), 4, True))
    tiles = added(tiles, other).astype(bf16)
    out_tile, in_tile = tiles[:, :PIECE], tiles[:, PIECE:]
    copies = jnp.broadcast_to(out_tile[None], (8, PIECE, PIECE))
    (near_in,) = phase((in_tile, X, SWAP_X))
    shard = in_order(h, in_tile, near_in)
    both_y = jnp.concatenate([y1, y2])
    one, far, y3 = phase(
        ring(shard),
        ring(added(keep_a[1:3], both_y, widened(far)).astype(bf16), 3, True),
        to_other_y(give_b[0]),
    )
    two, y4 = phase(ring(one), to_other_y(give_b[1]))
    three, y5 = phase(ring(two), to_other_y(give_b[2]))
    last, y6 = phase(ring(jnp.where(core == 0, three[:1], three[1:])), to_other_y(give_b[3]))
    in_own = jnp.concatenate([one, two, three, last], 0)
    in_own, copies = lax.optimization_barrier((in_own, copies))
    out_tiles = lax.all_to_all(copies, OWNER, 0, 0, tiled=True)
    both_y = jnp.concatenate([y3, y4])
    cross, in_other = phase(
        ring(added(keep_b[0:2], both_y, far).astype(bf16), 2, True), (in_own, CORE, SWAP2)
    )
    square = (TILE, TILE)
    in_inverse = call(
        functools.partial(in_inverse_kernel, tokens),
        2,
        (HALF, TILE),
        square,
        numbers(z, core),
        shard,
        in_own,
        in_other,
        limit=32,
        scratch=[(square, bf16), (square, f32), (square, bf16)],
    )
    both_y = jnp.concatenate([y5, y6])
    cross, y7 = phase(
        ring(added(keep_b[2:4], both_y, cross).astype(bf16), 1, True), to_other_y(give_b[4])
    )
    cross, in_inverse = lax.optimization_barrier((cross, in_inverse))
    other, out_other = phase((cross, CORE, SWAP2), (out_tiles, CORE, SWAP2))
    own, other = [jnp.where(core == 0, a[0], a[1]) for a in (cross, other)]
    cross = added(own, other, keep_b[4], y7[0]).astype(bf16)
    m = z % 4
    row = 2 * yh + core
    slice_rows = out_width // lax.axis_size(DP)
    base = TILE * (m - m // 2)
    near = jnp.where(m == 3, 2, m + 1)
    own_at = jnp.where(m == 2, TILE, slice_rows * (4 * m + row) - base)
    near_at = jnp.where(m == 2, TILE, slice_rows * (4 * near + row) - base)
    own_at, near_at = [jnp.clip(a, -slice_rows, TILE) + HALF for a in (own_at, near_at)]
    padded = call(
        functools.partial(out_inverse_kernel, tokens),
        4,
        (HALF, TILE),
        (4 * HALF, TILE),
        numbers(core),
        out_tiles,
        out_other,
        limit=32,
        scratch=[(square, bf16), (square, f32), (square, bf16)],
    )
    middle = mdot(cross, in_inverse).astype(bf16)
    mine = lax.dynamic_slice_in_dim(middle, h * HALF, HALF, 1)
    theirs = lax.dynamic_slice_in_dim(middle, (1 - h) * HALF, HALF, 1)
    near_x, near_y, near_xy = phase(
        (theirs, X, SWAP_X), (mine, YH, SWAP2), (theirs, (YH, X), SWAP_BOTH)
    )
    middle = in_order(h, in_order(yh, mine, near_y), in_order(yh, near_x, near_xy))
    middle, padded = lax.optimization_barrier((middle, padded))
    other = lax.ppermute(middle, CORE, SWAP2)
    middle = jnp.moveaxis(in_order(core, middle, other), 0, 1).reshape(TILE, HALF)
    out_inverse = jnp.concatenate(
        [lax.dynamic_slice_in_dim(padded, at, slice_rows, 0) for at in (own_at, near_at)], 0
    )
    result = mdot(out_inverse, middle)

    near_part = result[slice_rows:].astype(bf16)
    up = lax.ppermute(near_part, Z, [(0, 1), (1, 2), (4, 5), (5, 6)])
    down = lax.ppermute(near_part, Z, [(3, 2), (7, 6)])
    whole = mdot(padded[HALF : HALF + TILE], middle)
    squares = jnp.where(m == 2, 0.0, jnp.sum(whole * whole))
    squares = all_sum(all_sum(squares, Z), OWNER)
    summed = result[:slice_rows] + up.astype(f32) + down.astype(f32)
    return (summed * lax.rsqrt(squares / (width * out_width) + 1e-06)).astype(bf16)


def solution(mesh):
    split = Mesh(mesh.devices.reshape(8, 2, 2, 2, 4), DP + OWNER)
    return jax.shard_map(
        shards,
        mesh=split,
        in_specs=(P(DP, None), P(), P(DP, None)),
        out_specs=P(DP, OWNER),
        check_vma=False,
    )
```

```python
import functools

import jax
import jax.numpy as jnp
from jax import lax
from jax.experimental import pallas as pl
from jax.experimental.pallas import tpu as pltpu
from jax.sharding import Mesh
from jax.sharding import PartitionSpec as P

TILE = 1024
PIECE = 256
HALF = 512
Z, YH, CORE, YL, X = "dp_0", "dp_1", "dp_2", "owner_0", "owner_1"
DP = (Z, YH, CORE)
OWNER = (YL, X)
DAMPING = 0.1
bf16, f32 = jnp.bfloat16, jnp.float32
MIB = 1024 * 1024

AWAY = (4, 3, 3, 2, 2, 1, 1, 0, 0)
SWAP2 = [(0, 1), (1, 0)]
SWAP_X = [(0, 1), (1, 0), (2, 3), (3, 2)]
SWAP_BOTH = [(4 * a + b, 4 * (1 - a) + (b ^ 1)) for a in range(2) for b in range(4)]


def tdot(a, b):
    return lax.dot_general(a, b, (((0,), (0,)), ((), ())), preferred_element_type=f32)


def mdot(a, b):
    return jnp.dot(a, b, preferred_element_type=f32)


def aligned(start, size):
    return pl.ds(pl.multiple_of(start, size), size)


def pick_kernel(out_blocks, at_ref, cot_ref, pick_ref):
    h, k = at_ref[0], at_ref[1]
    rows = pl.ds(pl.multiple_of(pl.program_id(0) * pick_ref.shape[0], 8), pick_ref.shape[0])
    for j in range(out_blocks):
        here = slice(j * HALF, (j + 1) * HALF)
        there = slice(out_blocks * HALF + j * PIECE, out_blocks * HALF + (j + 1) * PIECE)
        pick_ref[:, here] = cot_ref[rows, aligned(j * TILE + h * HALF, HALF)]
        pick_ref[:, there] = cot_ref[rows, aligned(j * TILE + k * PIECE, PIECE)]


def load_tokens(pick_ref, recv_ref, own_ref, got_ref, out_ref, in_ref, sems):
    count = pick_ref.shape[0]
    copies = [
        pltpu.make_async_copy(src, dst.at[pl.ds(start, count)], sems.at[n])
        for n, (src, dst, start) in enumerate(
            (
                (pick_ref, out_ref, 0),
                (recv_ref, out_ref, count),
                (own_ref, in_ref, 0),
                (got_ref, in_ref, count),
            )
        )
    ]
    for copy in copies:
        copy.start()
    for copy in copies:
        copy.wait()


def factor_kernel(
    out_blocks, at_ref, pick_ref, recv_ref, own_ref, got_ref,
    part_ref, first_ref, out_ref, in_ref, sems,
):
    i = pl.program_id(0)

    @pl.when(i == 0)
    def _():
        load_tokens(pick_ref, recv_ref, own_ref, got_ref, out_ref, in_ref, sems)

    h, plane, block, piece = at_ref[0], at_ref[2 + 3 * i], at_ref[3 + 3 * i], at_ref[4 + 3 * i]
    left = out_ref[:, aligned(block * HALF + piece * PIECE, PIECE)]
    right = out_ref[:, aligned(out_blocks * HALF + block * PIECE, PIECE)]
    rows = in_ref[:, aligned((2 * h + piece) * PIECE, PIECE)]
    tiles = (
        tdot(left, right).astype(bf16),
        tdot(rows, in_ref[:, aligned(plane * 128, 128)]).astype(bf16),
    )
    for here, ref in ((i == 0, first_ref), (i > 0, part_ref)):

        @pl.when(here)
        def _():
            ref[0, :, :PIECE], ref[0, :, PIECE:] = tiles


def cross_kernel(base, gives, at_ref, pick_ref, recv_ref, own_ref, got_ref, keep_ref, *refs):
    give_refs, (out_ref, in_ref, sems) = refs[:-3], refs[-3:]
    i = pl.program_id(0)

    @pl.when(i == 0)
    def _():
        load_tokens(pick_ref, recv_ref, own_ref, got_ref, out_ref, in_ref, sems)

    yh, block, piece = at_ref[1], at_ref[3 + 3 * (base + i)], at_ref[4 + 3 * (base + i)]

    def rows_of(side):
        rows = out_ref[:, aligned(block * HALF + piece * PIECE + side * 128, 128)]
        return tdot(rows, in_ref[...]).astype(bf16)

    keep_ref[0] = rows_of(yh)
    give = rows_of(1 - yh)
    for slots, ref in zip(gives, give_refs):
        for n, slot in enumerate(slots):

            @pl.when(i + base == slot)
            def _():
                ref[n] = give


def split_factor(tokens, sums_ref, first_ref, low_ref):
    row = lax.broadcasted_iota(jnp.int32, (PIECE, PIECE), 0)
    eye = (row == lax.broadcasted_iota(jnp.int32, (PIECE, PIECE), 1)).astype(f32)
    largest = jnp.zeros((1, TILE), f32)
    for r in range(4):
        here = slice(r * PIECE, (r + 1) * PIECE)
        first_ref[here, :] = sums_ref[here, :].astype(f32) / tokens
        first_ref[here, here] += DAMPING * eye
        largest += jnp.sum(jnp.abs(first_ref[here, :]), axis=0, keepdims=True)
    scale = 1.0 / jnp.max(largest)
    for r in range(4):
        here = slice(r * PIECE, (r + 1) * PIECE)
        matrix = first_ref[here, :]
        sums_ref[here, :] = matrix.astype(bf16)
        first_ref[here, :] = -(scale * scale) * matrix
        first_ref[here, here] += (2.0 * scale) * eye
        low_ref[here, :] = first_ref[here, :].astype(bf16)


def inverse_rows(rows, sums_ref, low_ref):
    product = mdot(rows.astype(bf16), sums_ref[...]).astype(bf16)
    return (2.0 * rows - mdot(product, low_ref[...])).astype(bf16)


def in_inverse_kernel(
    tokens, at_ref, shard_ref, own_ref, other_ref,
    out_ref, sums_ref, first_ref, low_ref,
):
    i = pl.program_id(0)

    @pl.when(i == 0)
    def _():
        z, core = at_ref[0], at_ref[1]
        back = 1 - 2 * core

        def put(h, away, value):
            here = aligned((z + away + 8) % 8 * 128, 128)
            for piece in range(2):
                rows = aligned((2 * h + piece) * PIECE, PIECE)
                sums_ref[rows, here] = value[:, piece * 128 : (piece + 1) * 128]

        for h in range(2):
            put(h, 0, shard_ref[h])
            for d in (1, 2, 3):
                put(h, back * d, own_ref[2 * (d - 1) + h])
                put(h, -back * d, other_ref[2 * (d - 1) + h])
        put(core, 4, own_ref[6])
        put(1 - core, 4, other_ref[6])
        split_factor(tokens, sums_ref, first_ref, low_ref)

    out_ref[...] = inverse_rows(first_ref[aligned(i * HALF, HALF), :], sums_ref, low_ref)


def out_inverse_kernel(
    tokens, count, at_ref, own_ref, other_ref,
    out_ref, rows_ref, sums_ref, first_ref, low_ref, padded_ref,
):
    i = pl.program_id(0)

    @pl.when(i == 0)
    def _():
        core = at_ref[0]
        for owner in range(8):
            here = slice(owner // 2 * PIECE, (owner // 2 + 1) * PIECE)
            for piece, ref in ((core, own_ref), (1 - core, other_ref)):
                sums_ref[aligned((2 * (owner % 2) + piece) * PIECE, PIECE), here] = ref[owner]
        split_factor(tokens, sums_ref, first_ref, low_ref)
        nothing = jnp.zeros((count, TILE), bf16)
        padded_ref[:count, :] = nothing
        padded_ref[count + TILE :, :] = nothing

    inverse = inverse_rows(first_ref[aligned(i * HALF, HALF), :], sums_ref, low_ref)
    out_ref[...] = inverse
    padded_ref[pl.ds(pl.multiple_of(count + i * HALF, 64), HALF), :] = inverse

    @pl.when(i == 1)
    def _():
        for n in range(2):
            at = pl.ds(pl.multiple_of(at_ref[1 + n], 64), count)
            rows_ref[n * count : (n + 1) * count, :] = padded_ref[at, :]


def call(kernel, steps, block, out_shape, at, *args, limit, scratch=(), more=()):
    def whole(a):
        return pl.BlockSpec(a.shape, lambda i, at: (0,) * len(a.shape))

    outs = pl.pallas_call(
        kernel,
        grid_spec=pltpu.PrefetchScalarGridSpec(
            num_scalar_prefetch=1,
            grid=(steps,),
            in_specs=[whole(a) for a in args],
            out_specs=[pl.BlockSpec(block, lambda i, at: (i, 0))]
            + [pl.BlockSpec(m, lambda i, at: (0, 0)) for m in more],
            scratch_shapes=[pltpu.VMEM(shape, dtype) for shape, dtype in scratch],
        ),
        out_shape=[jax.ShapeDtypeStruct(m, bf16) for m in [out_shape, *more]],
        compiler_params=pltpu.CompilerParams(vmem_limit_bytes=limit * MIB),
    )(at, *args)
    return outs if more else outs[0]


def ring_pairs(away=0, skip=False):
    pairs = []
    for plane in range(8):
        for core, way in ((0, -1), (1, 1)):
            if not skip or (plane + way * away) % 4 != 2:
                pairs.append((2 * plane + core, 2 * ((plane + way) % 8) + core))
    return pairs


def phase(*sends):
    values = lax.optimization_barrier(tuple(send[0] for send in sends))
    got = [lax.ppermute(value, *send[1:]) for value, send in zip(values, sends)]
    return lax.optimization_barrier(tuple(got))


def added(*parts):
    return functools.reduce(jnp.add, [p.astype(f32) for p in parts])


def in_order(flag, own, other):
    first = jnp.where(flag == 0, own, other)
    second = jnp.where(flag == 0, other, own)
    return jnp.stack([first, second])


def all_sum(value, axis):
    n = lax.axis_size(axis)
    shares = lax.all_to_all(jnp.full((n, 128), value, f32), axis, 0, 0, tiled=True)
    return jnp.sum(shares[:, 0])


def shards(hidden, norm_gain, cotangent):
    z, yh, core = lax.axis_index(Z), lax.axis_index(YH), lax.axis_index(CORE)
    yl, x = lax.axis_index(YL), lax.axis_index(X)
    k, h = 2 * yl + x // 2, x % 2
    here, width = hidden.shape
    out_width = cotangent.shape[1]
    out_blocks = out_width // TILE
    tokens = here * lax.axis_size(DP)

    def numbers(*values):
        return jnp.stack([jnp.asarray(v, jnp.int32) for v in values])

    pick = call(
        functools.partial(pick_kernel, out_blocks),
        4,
        (here // 4, out_blocks * (HALF + PIECE)),
        (here, out_blocks * (HALF + PIECE)),
        numbers(h, k),
        cotangent,
        limit=8,
    )
    recv = lax.ppermute(pick, CORE, SWAP2)

    states = hidden.astype(f32)
    rms = lax.rsqrt(jnp.mean(states * states, axis=1, keepdims=True) + 1e-05)
    gain = lax.dynamic_slice_in_dim(norm_gain, k * TILE, TILE)
    mine = lax.dynamic_slice_in_dim(hidden, k * TILE, TILE, 1)
    normed = (mine.astype(f32) * rms * gain).astype(bf16)
    normed_recv = lax.ppermute(normed, CORE, SWAP2)

    way = 2 * core - 1
    table = []
    for i, away in enumerate(AWAY):
        plane = (z + way * away + 8) % 8
        piece = core if i in (0, 7) else 1 - core if i == 8 else (i + 1) % 2
        table += [plane, 3 * (plane // 4) + plane % 4 - plane % 4 // 2, piece]
    table = numbers(h, yh, *table)

    def slots(kernel, count, block, gives, skip=0):
        tokens_in = (pick, recv, normed, normed_recv)
        more = [(len(slots), *block) for slots in gives]
        return pl.pallas_call(
            kernel,
            grid_spec=pltpu.PrefetchScalarGridSpec(
                num_scalar_prefetch=1,
                grid=(count,),
                in_specs=[pl.BlockSpec(memory_space=pl.ANY) for _ in tokens_in],
                out_specs=[pl.BlockSpec((1, *block), lambda i, at: (jnp.maximum(i - skip, 0), 0, 0))]
                + [pl.BlockSpec(m, lambda i, at: (0, 0, 0)) for m in more],
                scratch_shapes=[
                    pltpu.VMEM((2 * here, pick.shape[1]), bf16),
                    pltpu.VMEM((2 * here, TILE), bf16),
                    pltpu.SemaphoreType.DMA((4,)),
                ],
            ),
            out_shape=[jax.ShapeDtypeStruct(m, bf16) for m in [(count - skip, *block)] + more],
            compiler_params=pltpu.CompilerParams(vmem_limit_bytes=12 * MIB),
        )(table, *tokens_in)

    def cross_part(base, count, gives):
        return slots(functools.partial(cross_kernel, base, gives), count, (128, TILE), gives)

    block = (PIECE, PIECE + 128)
    part, part_0 = slots(functools.partial(factor_kernel, out_blocks), 9, block, ((0,),), 1)
    keep_a, give_0, give_1, give_2 = cross_part(0, 3, ((0,), (1,), (2,)))
    keep_b, *give_b = cross_part(3, 5, ((3,), (4,), (5,), (6,), (7,)))

    def to_other_y(value):
        return value, YH, SWAP2

    def ring(value, *args):
        return value, (Z, CORE), ring_pairs(*args)

    def widened(got):
        nothing = jnp.zeros_like(got)
        return in_order(core, got, nothing)

    (far,) = phase(ring(part_0[0]))
    far, y0 = phase(ring(added(part[0:2], widened(far)).astype(bf16)), to_other_y(give_0))
    far, y1 = phase(ring(added(part[2:4], far).astype(bf16)), to_other_y(give_1))
    far, y2 = phase(ring(added(part[4:6], far).astype(bf16)), to_other_y(give_2))
    far, keep_b = lax.optimization_barrier((far, keep_b))
    both_in = jnp.concatenate([far[0, :, PIECE:], far[1, :, PIECE:]], 1)
    out_own = jnp.where(core == 0, far[0, :, :PIECE], far[1, :, :PIECE])
    out_other = jnp.where(core == 0, far[1, :, :PIECE], far[0, :, :PIECE])
    (other,) = phase((jnp.concatenate([out_other, both_in], 1), CORE, SWAP2))
    here_in = in_order(core, part[6, :, PIECE:], part[7, :, PIECE:])
    local = jnp.concatenate([part[6, :, :PIECE], here_in[0], here_in[1]], 1)
    tiles = (added(jnp.concatenate([out_own, both_in], 1), other) + local.astype(f32)).astype(bf16)
    other, far = phase((tiles, YH, SWAP2), ring(added(keep_a[0], y0[0]).astype(bf16), 4, True))
    tiles = added(tiles, other).astype(bf16)
    out_tile, in_tile = tiles[:, :PIECE], tiles[:, PIECE:]
    copies = jnp.broadcast_to(out_tile[None], (8, PIECE, PIECE))
    (near_in,) = phase((in_tile, X, SWAP_X))
    shard = in_order(h, in_tile, near_in)
    both_y = jnp.concatenate([y1, y2])
    one, far, y3 = phase(
        ring(shard),
        ring(added(keep_a[1:3], both_y, widened(far)).astype(bf16), 3, True),
        to_other_y(give_b[0]),
    )
    two, y4 = phase(ring(one), to_other_y(give_b[1]))
    three, y5 = phase(ring(two), to_other_y(give_b[2]))
    last, y6 = phase(ring(jnp.where(core == 0, three[:1], three[1:])), to_other_y(give_b[3]))
    in_own = jnp.concatenate([one, two, three, last], 0)
    in_own, copies = lax.optimization_barrier((in_own, copies))
    out_tiles = lax.all_to_all(copies, OWNER, 0, 0, tiled=True)
    both_y = jnp.concatenate([y3, y4])
    cross, in_other = phase(
        ring(added(keep_b[0:2], both_y, far).astype(bf16), 2, True), (in_own, CORE, SWAP2)
    )
    square = (TILE, TILE)
    in_inverse = call(
        functools.partial(in_inverse_kernel, tokens),
        2,
        (HALF, TILE),
        square,
        numbers(z, core),
        shard,
        in_own,
        in_other,
        limit=32,
        scratch=[(square, bf16), (square, f32), (square, bf16)],
    )
    both_y = jnp.concatenate([y5, y6])
    cross, y7 = phase(
        ring(added(keep_b[2:4], both_y, cross).astype(bf16), 1, True), to_other_y(give_b[4])
    )
    cross, in_inverse = lax.optimization_barrier((cross, in_inverse))
    other, out_other = phase((cross, CORE, SWAP2), (out_tiles, CORE, SWAP2))
    own, other = [jnp.where(core == 0, a[0], a[1]) for a in (cross, other)]
    cross = added(own, other, keep_b[4], y7[0]).astype(bf16)
    m = z % 4
    row = 2 * yh + core
    slice_rows = out_width // lax.axis_size(DP)
    base = TILE * (m - m // 2)
    near = jnp.where(m == 3, 2, m + 1)
    own_at = jnp.where(m == 2, TILE, slice_rows * (4 * m + row) - base)
    near_at = jnp.where(m == 2, TILE, slice_rows * (4 * near + row) - base)
    own_at, near_at = [jnp.clip(a, -slice_rows, TILE) + slice_rows for a in (own_at, near_at)]
    rows_of_two = (2 * slice_rows, TILE)
    inverse, out_inverse = call(
        functools.partial(out_inverse_kernel, tokens, slice_rows),
        2,
        (HALF, TILE),
        square,
        numbers(core, own_at, near_at),
        out_tiles,
        out_other,
        limit=32,
        scratch=[(square, bf16), (square, f32), (square, bf16), ((TILE + 2 * slice_rows, TILE), bf16)],
        more=(rows_of_two,),
    )
    middle = mdot(cross, in_inverse).astype(bf16)
    mine = lax.dynamic_slice_in_dim(middle, h * HALF, HALF, 1)
    theirs = lax.dynamic_slice_in_dim(middle, (1 - h) * HALF, HALF, 1)
    near_x, near_y, near_xy = phase(
        (theirs, X, SWAP_X), (mine, YH, SWAP2), (theirs, (YH, X), SWAP_BOTH)
    )
    middle = in_order(h, in_order(yh, mine, near_y), in_order(yh, near_x, near_xy))
    middle, inverse, out_inverse = lax.optimization_barrier((middle, inverse, out_inverse))
    other = lax.ppermute(middle, CORE, SWAP2)
    middle = jnp.moveaxis(in_order(core, middle, other), 0, 1).reshape(TILE, HALF)
    result = mdot(out_inverse, middle)

    near_part = result[slice_rows:].astype(bf16)
    up = lax.ppermute(near_part, Z, [(0, 1), (1, 2), (4, 5), (5, 6)])
    down = lax.ppermute(near_part, Z, [(3, 2), (7, 6)])
    whole = mdot(inverse, middle)
    squares = jnp.where(m == 2, 0.0, jnp.sum(whole * whole))
    squares = all_sum(all_sum(squares, Z), OWNER)
    summed = result[:slice_rows] + up.astype(f32) + down.astype(f32)
    return (summed * lax.rsqrt(squares / (width * out_width) + 1e-06)).astype(bf16)


def solution(mesh):
    split = Mesh(mesh.devices.reshape(8, 2, 2, 2, 4), DP + OWNER)
    return jax.shard_map(
        shards,
        mesh=split,
        in_specs=(P(DP, None), P(), P(DP, None)),
        out_specs=P(DP, OWNER),
        check_vma=False,
    )
```

```python
import functools

import jax
import jax.numpy as jnp
from jax import lax
from jax.experimental import pallas as pl
from jax.experimental.pallas import tpu as pltpu
from jax.sharding import Mesh
from jax.sharding import PartitionSpec as P

TILE = 1024
PIECE = 256
HALF = 512
Z, YH, CORE, YL, X = "dp_0", "dp_1", "dp_2", "owner_0", "owner_1"
DP = (Z, YH, CORE)
OWNER = (YL, X)
DAMPING = 0.1
bf16, f32 = jnp.bfloat16, jnp.float32
MIB = 1024 * 1024

AWAY = (4, 3, 3, 2, 2, 1, 1, 0, 0)
SWAP2 = [(0, 1), (1, 0)]
SWAP_X = [(0, 1), (1, 0), (2, 3), (3, 2)]
SWAP_BOTH = [(4 * a + b, 4 * (1 - a) + (b ^ 1)) for a in range(2) for b in range(4)]


def tdot(a, b):
    return lax.dot_general(a, b, (((0,), (0,)), ((), ())), preferred_element_type=f32)


def mdot(a, b):
    return jnp.dot(a, b, preferred_element_type=f32)


def aligned(start, size):
    return pl.ds(pl.multiple_of(start, size), size)


def pick_kernel(out_blocks, at_ref, cot_ref, pick_ref):
    h, k = at_ref[0], at_ref[1]
    rows = pl.ds(pl.multiple_of(pl.program_id(0) * pick_ref.shape[0], 8), pick_ref.shape[0])
    for j in range(out_blocks):
        here = slice(j * HALF, (j + 1) * HALF)
        there = slice(out_blocks * HALF + j * PIECE, out_blocks * HALF + (j + 1) * PIECE)
        pick_ref[:, here] = cot_ref[rows, aligned(j * TILE + h * HALF, HALF)]
        pick_ref[:, there] = cot_ref[rows, aligned(j * TILE + k * PIECE, PIECE)]


def load_tokens(pick_ref, recv_ref, own_ref, got_ref, out_ref, in_ref, sems):
    count = pick_ref.shape[0]
    copies = [
        pltpu.make_async_copy(src, dst.at[pl.ds(start, count)], sems.at[n])
        for n, (src, dst, start) in enumerate(
            (
                (pick_ref, out_ref, 0),
                (recv_ref, out_ref, count),
                (own_ref, in_ref, 0),
                (got_ref, in_ref, count),
            )
        )
    ]
    for copy in copies:
        copy.start()
    for copy in copies:
        copy.wait()


def factor_kernel(
    out_blocks, at_ref, pick_ref, recv_ref, own_ref, got_ref,
    part_ref, first_ref, out_ref, in_ref, sems,
):
    i = pl.program_id(0)

    @pl.when(i == 0)
    def _():
        load_tokens(pick_ref, recv_ref, own_ref, got_ref, out_ref, in_ref, sems)

    h, plane, block, piece = at_ref[0], at_ref[2 + 3 * i], at_ref[3 + 3 * i], at_ref[4 + 3 * i]
    left = out_ref[:, aligned(block * HALF + piece * PIECE, PIECE)]
    right = out_ref[:, aligned(out_blocks * HALF + block * PIECE, PIECE)]
    rows = in_ref[:, aligned((2 * h + piece) * PIECE, PIECE)]
    tiles = (
        tdot(left, right).astype(bf16),
        tdot(rows, in_ref[:, aligned(plane * 128, 128)]).astype(bf16),
    )
    for here, ref in ((i == 0, first_ref), (i > 0, part_ref)):

        @pl.when(here)
        def _():
            ref[0, :, :PIECE], ref[0, :, PIECE:] = tiles


def cross_kernel(base, gives, at_ref, pick_ref, recv_ref, own_ref, got_ref, keep_ref, *refs):
    give_refs, (out_ref, in_ref, sems) = refs[:-3], refs[-3:]
    i = pl.program_id(0)

    @pl.when(i == 0)
    def _():
        load_tokens(pick_ref, recv_ref, own_ref, got_ref, out_ref, in_ref, sems)

    yh, block, piece = at_ref[1], at_ref[3 + 3 * (base + i)], at_ref[4 + 3 * (base + i)]

    def rows_of(side):
        rows = out_ref[:, aligned(block * HALF + piece * PIECE + side * 128, 128)]
        return tdot(rows, in_ref[...]).astype(bf16)

    keep_ref[0] = rows_of(yh)
    give = rows_of(1 - yh)
    for slots, ref in zip(gives, give_refs):
        for n, slot in enumerate(slots):

            @pl.when(i + base == slot)
            def _():
                ref[n] = give


def split_factor(tokens, sums_ref, first_ref, low_ref):
    row = lax.broadcasted_iota(jnp.int32, (PIECE, PIECE), 0)
    eye = (row == lax.broadcasted_iota(jnp.int32, (PIECE, PIECE), 1)).astype(f32)
    largest = jnp.zeros((1, TILE), f32)
    for r in range(4):
        here = slice(r * PIECE, (r + 1) * PIECE)
        first_ref[here, :] = sums_ref[here, :].astype(f32) / tokens
        first_ref[here, here] += DAMPING * eye
        largest += jnp.sum(jnp.abs(first_ref[here, :]), axis=0, keepdims=True)
    scale = 1.0 / jnp.max(largest)
    for r in range(4):
        here = slice(r * PIECE, (r + 1) * PIECE)
        matrix = first_ref[here, :]
        sums_ref[here, :] = matrix.astype(bf16)
        first_ref[here, :] = -(scale * scale) * matrix
        first_ref[here, here] += (2.0 * scale) * eye
        low_ref[here, :] = first_ref[here, :].astype(bf16)


def inverse_rows(rows, sums_ref, low_ref):
    product = mdot(rows.astype(bf16), sums_ref[...]).astype(bf16)
    return (2.0 * rows - mdot(product, low_ref[...])).astype(bf16)


def in_inverse_kernel(
    tokens, at_ref, shard_ref, own_ref, other_ref,
    out_ref, sums_ref, first_ref, low_ref,
):
    i = pl.program_id(0)

    @pl.when(i == 0)
    def _():
        z, core = at_ref[0], at_ref[1]
        back = 1 - 2 * core

        def put(h, away, value):
            here = aligned((z + away + 8) % 8 * 128, 128)
            for piece in range(2):
                rows = aligned((2 * h + piece) * PIECE, PIECE)
                sums_ref[rows, here] = value[:, piece * 128 : (piece + 1) * 128]

        for h in range(2):
            put(h, 0, shard_ref[h])
            for d in (1, 2, 3):
                put(h, back * d, own_ref[2 * (d - 1) + h])
                put(h, -back * d, other_ref[2 * (d - 1) + h])
        put(core, 4, own_ref[6])
        put(1 - core, 4, other_ref[6])
        split_factor(tokens, sums_ref, first_ref, low_ref)

    out_ref[...] = inverse_rows(first_ref[aligned(i * HALF, HALF), :], sums_ref, low_ref)


def out_inverse_kernel(
    tokens, count, at_ref, own_ref, other_ref,
    out_ref, rows_ref, sums_ref, first_ref, low_ref, padded_ref,
):
    i = pl.program_id(0)

    @pl.when(i == 0)
    def _():
        core = at_ref[0]
        for owner in range(8):
            here = slice(owner // 2 * PIECE, (owner // 2 + 1) * PIECE)
            for piece, ref in ((core, own_ref), (1 - core, other_ref)):
                sums_ref[aligned((2 * (owner % 2) + piece) * PIECE, PIECE), here] = ref[owner]
        split_factor(tokens, sums_ref, first_ref, low_ref)
        nothing = jnp.zeros((count, TILE), bf16)
        padded_ref[:count, :] = nothing
        padded_ref[count + TILE :, :] = nothing

    inverse = inverse_rows(first_ref[aligned(i * HALF, HALF), :], sums_ref, low_ref)
    out_ref[...] = inverse
    padded_ref[pl.ds(pl.multiple_of(count + i * HALF, 64), HALF), :] = inverse

    @pl.when(i == 1)
    def _():
        for n in range(2):
            at = pl.ds(pl.multiple_of(at_ref[1 + n], 64), count)
            rows_ref[n * count : (n + 1) * count, :] = padded_ref[at, :]


def call(kernel, steps, block, out_shape, at, *args, limit, scratch=(), more=()):
    def whole(a):
        return pl.BlockSpec(a.shape, lambda i, at: (0,) * len(a.shape))

    outs = pl.pallas_call(
        kernel,
        grid_spec=pltpu.PrefetchScalarGridSpec(
            num_scalar_prefetch=1,
            grid=(steps,),
            in_specs=[whole(a) for a in args],
            out_specs=[pl.BlockSpec(block, lambda i, at: (i, 0))]
            + [pl.BlockSpec(m, lambda i, at: (0, 0)) for m in more],
            scratch_shapes=[pltpu.VMEM(shape, dtype) for shape, dtype in scratch],
        ),
        out_shape=[jax.ShapeDtypeStruct(m, bf16) for m in [out_shape, *more]],
        compiler_params=pltpu.CompilerParams(vmem_limit_bytes=limit * MIB),
    )(at, *args)
    return outs if more else outs[0]


def ring_pairs(away=0, skip=False):
    pairs = []
    for plane in range(8):
        for core, way in ((0, -1), (1, 1)):
            if not skip or (plane + way * away) % 4 != 2:
                pairs.append((2 * plane + core, 2 * ((plane + way) % 8) + core))
    return pairs


def phase(*sends):
    values = lax.optimization_barrier(tuple(send[0] for send in sends))
    got = [lax.ppermute(value, *send[1:]) for value, send in zip(values, sends)]
    return lax.optimization_barrier(tuple(got))


def added(*parts):
    return functools.reduce(jnp.add, [p.astype(f32) for p in parts])


def in_order(flag, own, other):
    first = jnp.where(flag == 0, own, other)
    second = jnp.where(flag == 0, other, own)
    return jnp.stack([first, second])


def all_sum(value, axis):
    n = lax.axis_size(axis)
    shares = lax.all_to_all(jnp.full((n, 128), value, f32), axis, 0, 0, tiled=True)
    return jnp.sum(shares[:, 0])


def shards(hidden, norm_gain, cotangent):
    z, yh, core = lax.axis_index(Z), lax.axis_index(YH), lax.axis_index(CORE)
    yl, x = lax.axis_index(YL), lax.axis_index(X)
    k, h = 2 * yl + x // 2, x % 2
    here, width = hidden.shape
    out_width = cotangent.shape[1]
    out_blocks = out_width // TILE
    tokens = here * lax.axis_size(DP)

    def numbers(*values):
        return jnp.stack([jnp.asarray(v, jnp.int32) for v in values])

    pick = call(
        functools.partial(pick_kernel, out_blocks),
        4,
        (here // 4, out_blocks * (HALF + PIECE)),
        (here, out_blocks * (HALF + PIECE)),
        numbers(h, k),
        cotangent,
        limit=8,
    )
    recv = lax.ppermute(pick, CORE, SWAP2)

    states = hidden.astype(f32)
    rms = lax.rsqrt(jnp.mean(states * states, axis=1, keepdims=True) + 1e-05)
    gain = lax.dynamic_slice_in_dim(norm_gain, k * TILE, TILE)
    mine = lax.dynamic_slice_in_dim(hidden, k * TILE, TILE, 1)
    normed = (mine.astype(f32) * rms * gain).astype(bf16)
    normed_recv = lax.ppermute(normed, CORE, SWAP2)

    way = 2 * core - 1
    table = []
    for i, away in enumerate(AWAY):
        plane = (z + way * away + 8) % 8
        piece = core if i in (0, 7) else 1 - core if i == 8 else (i + 1) % 2
        table += [plane, 3 * (plane // 4) + plane % 4 - plane % 4 // 2, piece]
    table = numbers(h, yh, *table)

    def slots(kernel, count, block, gives, skip=0):
        tokens_in = (pick, recv, normed, normed_recv)
        more = [(len(slots), *block) for slots in gives]
        return pl.pallas_call(
            kernel,
            grid_spec=pltpu.PrefetchScalarGridSpec(
                num_scalar_prefetch=1,
                grid=(count,),
                in_specs=[pl.BlockSpec(memory_space=pl.ANY) for _ in tokens_in],
                out_specs=[pl.BlockSpec((1, *block), lambda i, at: (jnp.maximum(i - skip, 0), 0, 0))]
                + [pl.BlockSpec(m, lambda i, at: (0, 0, 0)) for m in more],
                scratch_shapes=[
                    pltpu.VMEM((2 * here, pick.shape[1]), bf16),
                    pltpu.VMEM((2 * here, TILE), bf16),
                    pltpu.SemaphoreType.DMA((4,)),
                ],
            ),
            out_shape=[jax.ShapeDtypeStruct(m, bf16) for m in [(count - skip, *block)] + more],
            compiler_params=pltpu.CompilerParams(vmem_limit_bytes=12 * MIB),
        )(table, *tokens_in)

    def cross_part(base, count, gives):
        return slots(functools.partial(cross_kernel, base, gives), count, (128, TILE), gives)

    block = (PIECE, PIECE + 128)
    part, part_0 = slots(functools.partial(factor_kernel, out_blocks), 9, block, ((0,),), 1)
    keep_a, give_0, give_1, give_2 = cross_part(0, 3, ((0,), (1,), (2,)))
    keep_b, *give_b = cross_part(3, 5, ((3,), (4,), (5,), (6,), (7,)))

    def to_other_y(value):
        return value, YH, SWAP2

    def ring(value, *args):
        return value, (Z, CORE), ring_pairs(*args)

    def widened(got):
        nothing = jnp.zeros_like(got)
        return in_order(core, got, nothing)

    (far,) = phase(ring(part_0[0]))
    far, y0 = phase(ring(added(part[0:2], widened(far)).astype(bf16)), to_other_y(give_0))
    far, y1 = phase(ring(added(part[2:4], far).astype(bf16)), to_other_y(give_1))
    far, y2 = phase(ring(added(part[4:6], far).astype(bf16)), to_other_y(give_2))
    far, keep_b = lax.optimization_barrier((far, keep_b))
    both_in = jnp.concatenate([far[0, :, PIECE:], far[1, :, PIECE:]], 1)
    out_own = jnp.where(core == 0, far[0, :, :PIECE], far[1, :, :PIECE])
    out_other = jnp.where(core == 0, far[1, :, :PIECE], far[0, :, :PIECE])
    (other,) = phase((jnp.concatenate([out_other, both_in], 1), CORE, SWAP2))
    here_in = in_order(core, part[6, :, PIECE:], part[7, :, PIECE:])
    local = jnp.concatenate([part[6, :, :PIECE], here_in[0], here_in[1]], 1)
    tiles = (added(jnp.concatenate([out_own, both_in], 1), other) + local.astype(f32)).astype(bf16)
    other, far = phase((tiles, YH, SWAP2), ring(added(keep_a[0], y0[0]).astype(bf16), 4, True))
    tiles = added(tiles, other).astype(bf16)
    out_tile, in_tile = tiles[:, :PIECE], tiles[:, PIECE:]
    copies = jnp.broadcast_to(out_tile[None], (8, PIECE, PIECE))
    (near_in,) = phase((in_tile, X, SWAP_X))
    shard = in_order(h, in_tile, near_in)
    both_y = jnp.concatenate([y1, y2])
    one, far, y3 = phase(
        ring(shard),
        ring(added(keep_a[1:3], both_y, widened(far)).astype(bf16), 3, True),
        to_other_y(give_b[0]),
    )
    two, y4 = phase(ring(one), to_other_y(give_b[1]))
    three, y5 = phase(ring(two), to_other_y(give_b[2]))
    last, y6 = phase(ring(jnp.where(core == 0, three[:1], three[1:])), to_other_y(give_b[3]))
    in_own = jnp.concatenate([one, two, three, last], 0)
    in_own, copies = lax.optimization_barrier((in_own, copies))
    out_tiles = lax.all_to_all(copies, OWNER, 0, 0, tiled=True)
    both_y = jnp.concatenate([y3, y4])
    cross, in_other = phase(
        ring(added(keep_b[0:2], both_y, far).astype(bf16), 2, True), (in_own, CORE, SWAP2)
    )
    square = (TILE, TILE)
    in_inverse = call(
        functools.partial(in_inverse_kernel, tokens),
        2,
        (HALF, TILE),
        square,
        numbers(z, core),
        shard,
        in_own,
        in_other,
        limit=32,
        scratch=[(square, bf16), (square, f32), (square, bf16)],
    )
    both_y = jnp.concatenate([y5, y6])
    cross, y7 = phase(
        ring(added(keep_b[2:4], both_y, cross).astype(bf16), 1, True), to_other_y(give_b[4])
    )
    cross, in_inverse = lax.optimization_barrier((cross, in_inverse))
    other, out_other = phase((cross, CORE, SWAP2), (out_tiles, CORE, SWAP2))
    own, other = [jnp.where(core == 0, a[0], a[1]) for a in (cross, other)]
    cross = added(own, other, keep_b[4], y7[0]).astype(bf16)
    m = z % 4
    row = 2 * yh + core
    slice_rows = out_width // lax.axis_size(DP)
    base = TILE * (m - m // 2)
    near = jnp.where(m == 3, 2, m + 1)
    own_at = jnp.where(m == 2, TILE, slice_rows * (4 * m + row) - base)
    near_at = jnp.where(m == 2, TILE, slice_rows * (4 * near + row) - base)
    own_at, near_at = [jnp.clip(a, -slice_rows, TILE) + slice_rows for a in (own_at, near_at)]
    rows_of_two = (2 * slice_rows, TILE)
    inverse, out_inverse = call(
        functools.partial(out_inverse_kernel, tokens, slice_rows),
        2,
        (HALF, TILE),
        square,
        numbers(core, own_at, near_at),
        out_tiles,
        out_other,
        limit=32,
        scratch=[(square, bf16), (square, f32), (square, bf16), ((TILE + 2 * slice_rows, TILE), bf16)],
        more=(rows_of_two,),
    )
    middle = mdot(cross, in_inverse).astype(bf16)
    mine = lax.dynamic_slice_in_dim(middle, h * HALF, HALF, 1)
    theirs = lax.dynamic_slice_in_dim(middle, (1 - h) * HALF, HALF, 1)
    near_x, near_y, near_xy = phase(
        (theirs, X, SWAP_X), (mine, YH, SWAP2), (theirs, (YH, X), SWAP_BOTH)
    )
    middle = in_order(h, in_order(yh, mine, near_y), in_order(yh, near_x, near_xy))
    middle, inverse, out_inverse = lax.optimization_barrier((middle, inverse, out_inverse))
    other = lax.ppermute(middle, CORE, SWAP2)
    middle = jnp.moveaxis(in_order(core, middle, other), 0, 1).reshape(TILE, HALF)
    result = mdot(out_inverse, middle)

    whole = mdot(inverse, middle)
    squares = all_sum(jnp.where(m == 2, 0.0, jnp.sum(whole * whole)), Z)
    near_part, squares = lax.optimization_barrier((result[slice_rows:].astype(bf16), squares))
    up = lax.ppermute(near_part, Z, [(0, 1), (1, 2), (4, 5), (5, 6)])
    down = lax.ppermute(near_part, Z, [(3, 2), (7, 6)])
    squares = all_sum(squares, OWNER)
    summed = result[:slice_rows] + up.astype(f32) + down.astype(f32)
    return (summed * lax.rsqrt(squares / (width * out_width) + 1e-06)).astype(bf16)


def solution(mesh):
    split = Mesh(mesh.devices.reshape(8, 2, 2, 2, 4), DP + OWNER)
    return jax.shard_map(
        shards,
        mesh=split,
        in_specs=(P(DP, None), P(), P(DP, None)),
        out_specs=P(DP, OWNER),
        check_vma=False,
    )
```
